32 devices in a mesh: dp: 4 (over x, core), expert: 8 (over z, y).
Axes of the slice: x: 2, y: 2, z: 4, core: 2. Of those that a mesh axis runs over, the one named last changes fastest.
Arguments:
- tokens: bfloat16 [6304, 768], P(('dp', 'expert')), may hold values from -6 to 6
- packed_weight: bfloat16 [768, 2304], P(('dp', 'expert')), may hold values from -0.21875 to 0.21875
- output_weight: bfloat16 [768, 768], P(('dp', 'expert')), may hold values from -0.625 to 0.625
- router_weight: bfloat16 [768, 8], P(('dp', 'expert')), may hold values from -0.21875 to 0.21875
- first_gain: bfloat16 [768], P(('dp', 'expert')), may hold values from 0.5 to 1.5
- first_bias: bfloat16 [768], P(('dp', 'expert')), may hold values from -3 to 3
- second_gain: bfloat16 [768], P(('dp', 'expert')), may hold values from 0.5 to 1.5
- second_bias: bfloat16 [768], P(('dp', 'expert')), may hold values from -3 to 3
- expert_up: bfloat16 [8, 768, 3072], P('expert', None, 'dp'), may hold values from -0.21875 to 0.21875
- expert_down: bfloat16 [8, 768, 3072], P('expert', None, 'dp'), may hold values from -0.875 to 0.875
- expert_choice: int32 [6304, 2], P(('dp', 'expert')), may hold values from 0 to 7, as said below
- slot_index: int32 [6304, 2], P(('dp', 'expert')), may hold values from 0 to 46, as said below
- cotangent: bfloat16 [6304, 768], P(('dp', 'expert')), may hold values from -6 to 6
Outputs:
- block_output: bfloat16 [6304, 768], P(('dp', 'expert'))
- input_grad: bfloat16 [6304, 768], P(('dp', 'expert'))
- packed_grad: float32 [768, 2304], P(('dp', 'expert'))
- output_grad: float32 [768, 768], P(('dp', 'expert'))
- router_grad: float32 [768, 8], P(('dp', 'expert'))
- first_gain_grad: float32 [768], P(('dp', 'expert'))
- first_bias_grad: float32 [768], P(('dp', 'expert'))
- second_gain_grad: float32 [768], P(('dp', 'expert'))
- second_bias_grad: float32 [768], P(('dp', 'expert'))
- expert_up_grad: float32 [8, 768, 3072], P('expert', None, 'dp')
- expert_down_grad: float32 [8, 768, 3072], P('expert', None, 'dp')
The draws below stay inside these ranges and needn't reach their ends.
Inputs may be any that keep to these rules, and one draw needn't show every extreme that they name: `expert_choice`: each row names 2 different experts. `slot_index`: among the tokens of one device, taken choice by choice and then token by token, the number of earlier choices of the same expert, or 46 where that number is 46 or more.
All inputs are finite; a program needn't handle non-finite values.
Results may differ from the reference program's by a relative error of at most 0.019.
Values may be sent and summed in bfloat16 or wider, within the bound.
A program may use at most 128 MiB of HBM per device.

```python
import jax
import jax.numpy as jnp
from jax import lax

D = 768
HEADS = 12
HEAD = 64
FF = 3072
TOP = 2
SEQ = 197
EXPERT_TOTAL = 8
TOK_DEV = 197
TOKENS = 6304
CAP = 46
N_DP = 4
N_EXPERT = 8


def route_table(key):
    base = jax.random.fold_in(key, 11)
    initial_key, second_key = jax.random.split(base)
    extra_amount = jax.random.randint(initial_key, (EXPERT_TOTAL,), 0, 3) * 128
    random_jitter = jax.random.randint(second_key, (TOKENS, EXPERT_TOTAL), 0, 4096)
    router_scores = (random_jitter + extra_amount[None, :]) * EXPERT_TOTAL + jnp.arange(EXPERT_TOTAL, dtype=jnp.int32)[None, :]
    unused, chosen = lax.top_k(router_scores, TOP)
    chosen = chosen.astype(jnp.int32)
    blocks = TOKENS // TOK_DEV
    ordered = jnp.transpose(chosen.reshape(blocks, TOK_DEV, TOP), (0, 2, 1)).reshape(blocks, TOP * TOK_DEV)
    onehot = (ordered[:, :, None] == jnp.arange(EXPERT_TOTAL, dtype=jnp.int32)[None, None, :]).astype(jnp.int32)
    counts = jnp.cumsum(onehot, axis=1)
    ranks = jnp.sum(counts * onehot, axis=2) - 1
    slots = jnp.minimum(ranks, CAP)
    slots = jnp.transpose(slots.reshape(blocks, TOP, TOK_DEV), (0, 2, 1)).reshape(TOKENS, TOP)
    return (chosen, slots.astype(jnp.int32))


def draw_expert_choice(key, part):
    return route_table(key)[0]


def draw_slot_index(key, part):
    return route_table(key)[1]


def raised(drawn, key, source, target, shards_of, factor):
    def block_of(axis_at):
        return (jnp.arange(drawn.shape[axis_at]) // (drawn.shape[axis_at] // shards_of)).reshape((-1,) + (1,) * (drawn.ndim - 1 - axis_at))

    near = jax.random.permutation(key, shards_of)[block_of(target)]
    far = (block_of(target) + shards_of // 2) % shards_of
    return jnp.where((block_of(source) == near) | (block_of(source) == far), factor * drawn, drawn)


def steps_of(stream_key, dims, cuts, least, largest):
    gain = 1.0
    for axis_at, shards_of in cuts:
        steps = jax.random.uniform(jax.random.fold_in(jax.random.fold_in(stream_key, 6), axis_at), (shards_of,), jnp.float32, least / len(cuts), largest / len(cuts))
        gain = gain * jnp.repeat(jnp.exp(steps), dims[axis_at] // shards_of).reshape((-1,) + (1,) * (len(dims) - 1 - axis_at))
    return gain


def noise(stream_key, extent, width, limit, cuts=(), kind=jnp.bfloat16):
    gain = steps_of(stream_key, extent, cuts, -0.22, 0.18) if cuts else 1.0
    values = jax.random.normal(stream_key, extent, jnp.float32) * width * gain
    return jnp.minimum(jnp.maximum(values, -limit), limit).astype(kind)


def heavy_noise(stream_key, shape, deviation, bound, pieces, heavy, kind=jnp.bfloat16):
    values = deviation * jax.random.normal(stream_key, shape, jnp.float32)
    if pieces:
        values = values * steps_of(stream_key, shape, pieces, -0.22, 0.18)
    return jnp.clip(raised(values, jax.random.fold_in(stream_key, 3), *heavy), -bound, bound).astype(kind)


def setup_inputs(seed: int = 0) -> dict:
    arg_keys = jax.random.split(jax.random.key(seed), 14)
    return {
        "tokens": heavy_noise(arg_keys[0], (TOKENS, D), 1.0, 6.0, ((0, 32),), (0, 1, 32, 2.75)),
        "packed_weight": noise(arg_keys[1], (D, 3 * D), D ** -0.5, 0.21875, ((0, 32),)),
        "output_weight": noise(arg_keys[2], (D, D), (D // 8) ** -0.5, 0.625, ((0, 32),)),
        "router_weight": noise(arg_keys[3], (D, EXPERT_TOTAL), D ** -0.5, 0.21875, ((0, 32),)),
        "first_gain": jnp.clip(1.0 + 0.1 * jax.random.normal(arg_keys[4], (D,), jnp.float32), 0.5, 1.5).astype(jnp.bfloat16),
        "first_bias": noise(arg_keys[5], (D,), 0.5, 3.0, ((0, 32),)),
        "second_gain": jnp.clip(1.0 + 0.1 * jax.random.normal(arg_keys[6], (D,), jnp.float32), 0.5, 1.5).astype(jnp.bfloat16),
        "second_bias": noise(arg_keys[7], (D,), 0.5, 3.0, ((0, 32),)),
        "expert_up": noise(arg_keys[8], (EXPERT_TOTAL, D, FF), D ** -0.5, 0.21875, ((0, 8), (2, 4))),
        "expert_down": noise(arg_keys[9], (EXPERT_TOTAL, D, FF), (max(FF // (EXPERT_TOTAL * EXPERT_TOTAL), 1)) ** -0.5, 0.875, ((0, 8), (2, 4))),
        "expert_choice": draw_expert_choice(jax.random.fold_in(arg_keys[13], 71), 0),
        "slot_index": draw_slot_index(jax.random.fold_in(arg_keys[13], 71), 0),
        "cotangent": noise(arg_keys[12], (TOKENS, D), 1.0, 6.0, ((0, 32),)),
    }


epsilon = 1e-06
inv_root_two = 0.7071067811865476
inv_root_two_pi = 0.3989422804014327

def round_half(arg_values):
    return lax.optimization_barrier(arg_values.astype(jnp.bfloat16)).astype(jnp.float32)

def normalize(rows_in, gain_vec, offset):
    centred = rows_in - lax.optimization_barrier(jnp.mean(rows_in, axis=-1, keepdims=True))
    inverse = lax.rsqrt(lax.optimization_barrier(jnp.mean(centred * centred, axis=-1, keepdims=True)) + epsilon)
    unit_rows = centred * inverse
    return (unit_rows * gain_vec.astype(jnp.float32) + offset.astype(jnp.float32), unit_rows, inverse)

def normalize_back(grad_rows, unit_rows, inverse, gain_vec):
    grad_unit = grad_rows * gain_vec.astype(jnp.float32)
    mean_grad = lax.optimization_barrier(jnp.mean(grad_unit, axis=-1, keepdims=True))
    mean_dot = lax.optimization_barrier(jnp.mean(grad_unit * unit_rows, axis=-1, keepdims=True))
    grad_in = inverse * (grad_unit - mean_grad - unit_rows * mean_dot)
    return (grad_in, lax.optimization_barrier(jnp.sum(grad_rows * unit_rows, axis=0)), lax.optimization_barrier(jnp.sum(grad_rows, axis=0)))

def gelu_exact(arg_values):
    return 0.5 * arg_values * (1.0 + jax.scipy.special.erf(arg_values * inv_root_two))

def gelu_slope(arg_values):
    return 0.5 * (1.0 + jax.scipy.special.erf(arg_values * inv_root_two)) + arg_values * jnp.exp(-0.5 * arg_values * arg_values) * inv_root_two_pi

def attend_block(packed_heads):
    queries = packed_heads[:, :, 0].astype(jnp.float32)
    key_rows = packed_heads[:, :, 1].astype(jnp.float32)
    values = packed_heads[:, :, 2].astype(jnp.float32)
    router_scores = jnp.einsum('ishd,ithd->ihst', queries, key_rows) * HEAD ** (-0.5)
    log_total = jnp.log(lax.optimization_barrier(jnp.sum(jnp.exp(router_scores), axis=-1, keepdims=True)))
    weights = round_half(jnp.exp(router_scores - log_total))
    mixed_heads = jnp.einsum('ihst,ithd->ishd', weights, values)
    return (mixed_heads.astype(jnp.bfloat16), log_total)

def attend_back(operands):
    packed_heads, log_total, grad_mixed = operands
    queries = packed_heads[:, :, 0].astype(jnp.float32)
    key_rows = packed_heads[:, :, 1].astype(jnp.float32)
    values = packed_heads[:, :, 2].astype(jnp.float32)
    grad_heads = grad_mixed.astype(jnp.float32)
    router_scores = jnp.einsum('ishd,ithd->ihst', queries, key_rows) * HEAD ** (-0.5)
    weights = jnp.exp(router_scores - log_total)
    rounded = round_half(weights)
    grad_values = jnp.einsum('ihst,ishd->ithd', rounded, grad_heads)
    grad_weights = jnp.einsum('ishd,ithd->ihst', grad_heads, values)
    row_delta = lax.optimization_barrier(jnp.sum(weights * grad_weights, axis=-1, keepdims=True))
    grad_scores = round_half(weights * (grad_weights - row_delta) * HEAD ** (-0.5))
    grad_queries = jnp.einsum('ihst,ithd->ishd', grad_scores, key_rows)
    grad_keys = jnp.einsum('ihst,ishd->ithd', grad_scores, queries)
    return jnp.stack([grad_queries, grad_keys, grad_values], axis=2)

def expert_forward(operands):
    slot_rows, weight_up, weight_down = operands
    before_act = jnp.dot(slot_rows, weight_up, preferred_element_type=jnp.float32)
    hidden = gelu_exact(before_act).astype(jnp.bfloat16)
    return jnp.dot(hidden, weight_down.T, preferred_element_type=jnp.float32).astype(jnp.bfloat16)

def expert_backward(operands):
    slot_rows, grad_rows, weight_up, weight_down = operands
    before_act = jnp.dot(slot_rows, weight_up, preferred_element_type=jnp.float32)
    hidden = gelu_exact(before_act).astype(jnp.bfloat16)
    grad_hidden = jnp.dot(grad_rows, weight_down, preferred_element_type=jnp.float32)
    grad_pre = (grad_hidden * gelu_slope(before_act)).astype(jnp.bfloat16)
    grad_down = jnp.dot(grad_rows.T, hidden, preferred_element_type=jnp.float32)
    grad_up = jnp.dot(slot_rows.T, grad_pre, preferred_element_type=jnp.float32)
    grad_sent = jnp.dot(grad_pre, weight_up.T, preferred_element_type=jnp.float32).astype(jnp.bfloat16)
    return (grad_sent, grad_up, grad_down)

def reference(tokens, packed_weight, output_weight, router_weight, first_gain, first_bias, second_gain, second_bias, expert_up, expert_down, expert_choice, slot_index, cotangent):
    devices = N_DP * N_EXPERT
    images = TOKENS // SEQ
    blocks = N_DP
    slot_count = EXPERT_TOTAL * CAP + 1
    inputs = tokens.astype(jnp.float32)
    normed_first, unit_first, inverse_first = normalize(inputs, first_gain, first_bias)
    normed_first = normed_first.astype(jnp.bfloat16)
    packed = jnp.dot(normed_first, packed_weight, preferred_element_type=jnp.float32).astype(jnp.bfloat16)
    packed_blocks = packed.reshape(blocks, images // blocks, SEQ, 3, HEADS, HEAD)
    mixed_heads, log_total = lax.map(attend_block, packed_blocks)
    mixed_flat = mixed_heads.reshape(TOKENS, D)
    hidden_first = inputs + jnp.dot(mixed_flat, output_weight, preferred_element_type=jnp.float32)
    normed_second, unit_second, inverse_second = normalize(hidden_first, second_gain, second_bias)
    normed_second = normed_second.astype(jnp.bfloat16)
    logits = jnp.dot(normed_second, router_weight, preferred_element_type=jnp.float32)
    exp_terms = jnp.exp(logits)
    router_probs = exp_terms / lax.optimization_barrier(jnp.sum(exp_terms, axis=-1, keepdims=True))
    gate_values = jnp.take_along_axis(router_probs, expert_choice, axis=1)
    device_of = (jnp.arange(TOKENS, dtype=jnp.int32) // TOK_DEV)[:, None]
    local_slot = jnp.where(slot_index < CAP, expert_choice * CAP + slot_index, EXPERT_TOTAL * CAP)
    global_slot = (device_of * slot_count + local_slot).reshape(-1).astype(jnp.int32)

    def to_experts(slot_rows):
        slot_table = jnp.zeros((devices * slot_count, D), jnp.bfloat16).at[global_slot].set(slot_rows)
        slot_table = slot_table.reshape(devices, slot_count, D)[:, :-1].reshape(devices, EXPERT_TOTAL, CAP, D)
        return jnp.transpose(slot_table, (1, 0, 2, 3)).reshape(EXPERT_TOTAL, devices * CAP, D)

    def from_experts(slot_table):
        slot_table = jnp.transpose(slot_table.reshape(EXPERT_TOTAL, devices, CAP, D), (1, 0, 2, 3)).reshape(devices, EXPERT_TOTAL * CAP, D)
        slot_table = jnp.concatenate([slot_table, jnp.zeros((devices, 1, D), slot_table.dtype)], axis=1).reshape(devices * slot_count, D)
        return slot_table[global_slot].reshape(TOKENS, TOP, D).astype(jnp.float32)
    expert_rows = to_experts(jnp.repeat(normed_second, TOP, axis=0))
    expert_out = lax.map(expert_forward, (expert_rows, expert_up, expert_down))
    returned = from_experts(expert_out)
    combined = lax.optimization_barrier(jnp.sum(gate_values[:, :, None] * returned, axis=1))
    block_output = (hidden_first + combined).astype(jnp.bfloat16)
    grad_top = cotangent.astype(jnp.float32)
    grad_gates = lax.optimization_barrier(jnp.sum(grad_top[:, None, :] * returned, axis=2))
    grad_slots = (gate_values[:, :, None] * grad_top[:, None, :]).astype(jnp.bfloat16).reshape(TOKENS * TOP, D)
    grad_table = to_experts(grad_slots)
    grad_sent, expert_up_grad, expert_down_grad = lax.map(expert_backward, (expert_rows, grad_table, expert_up, expert_down))
    gradient_second_normed = lax.optimization_barrier(jnp.sum(from_experts(grad_sent), axis=1))
    choice_mask = (expert_choice[:, :, None] == jnp.arange(EXPERT_TOTAL, dtype=jnp.int32)[None, None, :]).astype(jnp.float32)
    grad_probs = lax.optimization_barrier(jnp.sum(choice_mask * grad_gates[:, :, None], axis=1))
    grad_logits = (router_probs * (grad_probs - lax.optimization_barrier(jnp.sum(router_probs * grad_probs, axis=1, keepdims=True)))).astype(jnp.bfloat16)
    router_grad = jnp.dot(normed_second.T, grad_logits, preferred_element_type=jnp.float32)
    gradient_second_normed = gradient_second_normed + jnp.dot(grad_logits, router_weight.T, preferred_element_type=jnp.float32)
    grad_hidden, second_gain_grad, second_bias_grad = normalize_back(gradient_second_normed, unit_second, inverse_second, second_gain)
    grad_hidden = grad_hidden + grad_top
    grad_hidden_half = grad_hidden.astype(jnp.bfloat16)
    output_grad = jnp.dot(mixed_flat.T, grad_hidden_half, preferred_element_type=jnp.float32)
    grad_mixed = jnp.dot(grad_hidden_half, output_weight.T, preferred_element_type=jnp.float32).astype(jnp.bfloat16)
    grad_mixed = grad_mixed.reshape(blocks, images // blocks, SEQ, HEADS, HEAD)
    gradient_packed_rows = lax.map(attend_back, (packed_blocks, log_total, grad_mixed))
    gradient_packed_rows = gradient_packed_rows.reshape(TOKENS, 3 * D).astype(jnp.bfloat16)
    packed_grad = jnp.dot(normed_first.T, gradient_packed_rows, preferred_element_type=jnp.float32)
    grad_normed_first = jnp.dot(gradient_packed_rows, packed_weight.T, preferred_element_type=jnp.float32)
    grad_inputs, first_gain_grad, first_bias_grad = normalize_back(grad_normed_first, unit_first, inverse_first, first_gain)
    input_grad = (grad_inputs + grad_hidden).astype(jnp.bfloat16)
    return (block_output, input_grad, packed_grad, output_grad, router_grad, first_gain_grad, first_bias_grad, second_gain_grad, second_bias_grad, expert_up_grad, expert_down_grad)
```

```python
import functools

import jax
import jax.numpy as jnp
from jax import lax
from jax.experimental import pallas as pl
from jax.experimental.pallas import tpu as pltpu
from jax.sharding import PartitionSpec as P

HEADS = 12
HEAD = 64
SEQ = 197


epsilon = 1e-06
inv_root_two = 0.7071067811865476
inv_root_two_pi = 0.3989422804014327


def normalize(rows_in, gain_vec, offset):
    centred = rows_in - jnp.mean(rows_in, axis=-1, keepdims=True)
    inverse = lax.rsqrt(jnp.mean(centred * centred, axis=-1, keepdims=True) + epsilon)
    unit_rows = centred * inverse
    return (
        unit_rows * gain_vec.astype(jnp.float32) + offset.astype(jnp.float32),
        unit_rows,
        inverse,
    )


def normalize_back(grad_rows, unit_rows, inverse, gain_vec):
    grad_unit = grad_rows * gain_vec.astype(jnp.float32)
    mean_grad = jnp.mean(grad_unit, axis=-1, keepdims=True)
    mean_dot = jnp.mean(grad_unit * unit_rows, axis=-1, keepdims=True)
    grad_in = inverse * (grad_unit - mean_grad - unit_rows * mean_dot)
    return (grad_in, jnp.sum(grad_rows * unit_rows, axis=0), jnp.sum(grad_rows, axis=0))


def gelu_exact(arg_values):
    return 0.5 * arg_values * (1.0 + jax.scipy.special.erf(arg_values * inv_root_two))


def gelu_slope(arg_values):
    return (
        0.5 * (1.0 + jax.scipy.special.erf(arg_values * inv_root_two))
        + arg_values * jnp.exp(-0.5 * arg_values * arg_values) * inv_root_two_pi
    )


def attend_forward(packed_heads):
    queries = packed_heads[:, :, 0]
    key_rows = packed_heads[:, :, 1]
    values = packed_heads[:, :, 2]
    router_scores = jnp.einsum(
        "ishd,ithd->ihst", queries, key_rows, preferred_element_type=jnp.float32
    ) * HEAD ** (-0.5)
    log_total = jnp.log(jnp.sum(jnp.exp(router_scores), axis=-1, keepdims=True))
    weights = jnp.exp(router_scores - log_total).astype(jnp.bfloat16)
    mixed_heads = jnp.einsum("ihst,ithd->ishd", weights, values, preferred_element_type=jnp.float32)
    return (mixed_heads.astype(jnp.bfloat16), log_total)


def attend_back(packed_heads, log_total, grad_mixed):
    queries = packed_heads[:, :, 0]
    key_rows = packed_heads[:, :, 1]
    values = packed_heads[:, :, 2]
    router_scores = jnp.einsum(
        "ishd,ithd->ihst", queries, key_rows, preferred_element_type=jnp.float32
    ) * HEAD ** (-0.5)
    weights = jnp.exp(router_scores - log_total)
    rounded = weights.astype(jnp.bfloat16)
    grad_values = jnp.einsum(
        "ihst,ishd->ithd", rounded, grad_mixed, preferred_element_type=jnp.float32
    )
    grad_weights = jnp.einsum(
        "ishd,ithd->ihst", grad_mixed, values, preferred_element_type=jnp.float32
    )
    row_delta = jnp.sum(weights * grad_weights, axis=-1, keepdims=True)
    grad_scores = (weights * (grad_weights - row_delta) * HEAD ** (-0.5)).astype(jnp.bfloat16)
    grad_queries = jnp.einsum(
        "ihst,ithd->ishd", grad_scores, key_rows, preferred_element_type=jnp.float32
    )
    grad_keys = jnp.einsum(
        "ihst,ishd->ithd", grad_scores, queries, preferred_element_type=jnp.float32
    )
    return jnp.stack([grad_queries, grad_keys, grad_values], axis=2)


EXTRA = 128
MESH = pl.DeviceIdType.MESH
VMEM_LIMIT = 60 * 1024 * 1024


class Place:
    def __init__(self):
        self.nx = lax.axis_size("dp") // 2
        self.ny = self.nx
        self.nz = lax.axis_size("expert") // self.ny
        dp, expert = lax.axis_index("dp"), lax.axis_index("expert")
        self.x, self.c = dp // 2, dp % 2
        self.z, self.y = expert // self.ny, expert % self.ny

    def device(self, x, c, z, y):
        return (x * 2 + c, z * self.ny + y)

    def owner(self, x, c, z, y):
        return (x * 2 + c) * (self.nz * self.ny) + z * self.ny + y

    def sibling(self):
        return self.device(self.x, 1 - self.c, self.z, self.y)


def flip(value, k):
    bit = 1
    out = value
    while bit <= k:
        if k & bit:
            out = out + bit * (1 - 2 * ((value // bit) % 2))
        bit *= 2
    return out


def spot(place, core, kz, kf, ks):
    x, y = place.x, place.y
    dx = (1 - core) * (flip(x, kf) - x) + core * (flip(x, ks) - x)
    dy = (1 - core) * (flip(y, ks) - y) + core * (flip(y, kf) - y)
    return (x + dx, core, flip(place.z, kz), y + dy)


def greet(devices):
    barrier = pltpu.get_barrier_semaphore()
    for device in devices:
        pl.semaphore_signal(barrier, inc=1, device_id=device, device_id_type=MESH)
    pl.semaphore_wait(barrier, len(devices))


def grid_partners(place):
    partners = [place.device(*spot(place, place.c, k, 0, 0)) for k in range(1, place.nz)]
    partners += [place.device(*spot(place, place.c, 0, k, 0)) for k in range(1, place.nx)]
    partners += [place.device(*spot(place, place.c, 0, 0, k)) for k in range(1, place.nx)]
    return partners + [place.sibling()]


def labels_of(nx, nz):
    return [(kz, kf, ks) for ks in range(nx) for kf in range(nx) for kz in range(nz)]


def gather_kernel(nx, nz, shard, out, own_sem, send_sem, recv_sem):
    place = Place()
    labels = labels_of(nx, nz)
    number = {}
    for label in labels:
        if label != (0, 0, 0):
            number["plane", label] = len(number)
    for label in labels:
        number["pair", label] = len(number)
    greet(grid_partners(place))
    sent = []

    def here(label):
        return place.owner(*spot(place, place.c, *label))

    def send(kind, label, origin, target):
        at = number[kind, label]
        source = shard if origin == (0, 0, 0) else out.at[here(origin)]
        copy = pltpu.make_async_remote_copy(
            src_ref=source,
            dst_ref=out.at[here(origin)],
            send_sem=send_sem.at[at],
            recv_sem=recv_sem.at[at],
            device_id=target,
            device_id_type=MESH,
        )
        copy.start()
        sent.append(copy)

    def arrived(kind, label, index):
        at = number[kind, label]
        pltpu.make_async_remote_copy(
            src_ref=out.at[index],
            dst_ref=out.at[index],
            send_sem=send_sem.at[at],
            recv_sem=recv_sem.at[at],
            device_id=place.sibling(),
            device_id_type=MESH,
        ).wait_recv()

    def spread_first(kz):
        for kf in range(1, nx):
            send("plane", (kz, kf, 0), (kz, 0, 0), place.device(*spot(place, place.c, 0, kf, 0)))

    def spread_second(kz, kf):
        for ks in range(1, nx):
            send("plane", (kz, kf, ks), (kz, kf, 0), place.device(*spot(place, place.c, 0, 0, ks)))

    def share(label):
        send("pair", label, label, place.sibling())

    spread_first(0)
    spread_second(0, 0)
    for kz in range(1, nz):
        send("plane", (kz, 0, 0), (0, 0, 0), place.device(*spot(place, place.c, kz, 0, 0)))
    share((0, 0, 0))
    own = pltpu.make_async_copy(shard, out.at[here((0, 0, 0))], own_sem)
    own.start()
    for kz in range(1, nz + 1):
        if kz < nz:
            arrived("plane", (kz, 0, 0), here((kz, 0, 0)))
            spread_first(kz)
            spread_second(kz, 0)
            share((kz, 0, 0))
        for kf in range(1, nx):
            label = (kz - 1, kf, 0)
            arrived("plane", label, here(label))
            spread_second(kz - 1, kf)
            share(label)
    for kz in range(nz):
        for kf in range(nx):
            for ks in range(1, nx):
                arrived("plane", (kz, kf, ks), here((kz, kf, ks)))
                share((kz, kf, ks))
    for label in labels:
        arrived("pair", label, place.owner(*spot(place, 1 - place.c, *label)))
    own.wait()
    for copy in sent:
        copy.wait_send()


def gather_dense(shard):
    nx = lax.axis_size("dp") // 2
    nz = lax.axis_size("expert") // nx
    devices = 2 * nx * nx * nz
    edges = devices - 1
    return pl.pallas_call(
        functools.partial(gather_kernel, nx, nz),
        out_shape=jax.ShapeDtypeStruct((devices,) + shard.shape, shard.dtype),
        in_specs=[pl.BlockSpec(memory_space=pl.ANY)],
        out_specs=pl.BlockSpec(memory_space=pl.ANY),
        scratch_shapes=[
            pltpu.SemaphoreType.DMA,
            pltpu.SemaphoreType.DMA((edges,)),
            pltpu.SemaphoreType.DMA((edges,)),
        ],
        compiler_params=pltpu.CompilerParams(collective_id=0, has_side_effects=True),
        name="gather_dense",
    )(shard)


def scatter_kernel(
    nx, nz, main, side, extra, out, mine, pair, second, first, last, send_sem, recv_sem
):
    place = Place()
    labels = labels_of(nx, nz)
    slot = {label: i for i, label in enumerate(labels)}
    number = {("pair", label): i for i, label in enumerate(labels)}
    for label in labels:
        if label != (0, 0, 0):
            number["plane", label] = len(number)
    widths = [main.shape[2], side.shape[2], extra.shape[2]]
    starts = [0, widths[0], widths[0] + widths[1]]
    for part, start, width in zip((main, side, extra), starts, widths):
        mine[:, :, start : start + width] = part[...]
    greet(grid_partners(place))
    sent = []

    def send(kind, label, source, target_ref, target):
        at = number[kind, label]
        copy = pltpu.make_async_remote_copy(
            src_ref=source,
            dst_ref=target_ref,
            send_sem=send_sem.at[at],
            recv_sem=recv_sem.at[at],
            device_id=target,
            device_id_type=MESH,
        )
        copy.start()
        sent.append(copy)

    def arrived(kind, label, ref):
        at = number[kind, label]
        pltpu.make_async_remote_copy(
            src_ref=ref,
            dst_ref=ref,
            send_sem=send_sem.at[at],
            recv_sem=recv_sem.at[at],
            device_id=place.sibling(),
            device_id_type=MESH,
        ).wait_recv()

    order = sorted(labels, key=lambda k: (k[2] == 0, k[1] == 0, k[0] == 0, k))
    for label in order:
        index = place.owner(*spot(place, 1 - place.c, *label))
        send("pair", label, mine.at[index], pair.at[slot[label]], place.sibling())
    for label in order:
        kz, kf, ks = label
        at = slot[label]
        arrived("pair", label, pair.at[at])
        total = mine[place.owner(*spot(place, place.c, *label))].astype(jnp.float32)
        total = total + pair[at].astype(jnp.float32)
        if ks == 0:
            for k in range(1, nx):
                got = second.at[slot[kz, kf, k] - nx * nz]
                arrived("plane", (kz, kf, k), got)
                total = total + got[...].astype(jnp.float32)
            if kf == 0:
                for k in range(1, nx):
                    got = first.at[(k - 1) * nz + kz]
                    arrived("plane", (kz, k, 0), got)
                    total = total + got[...].astype(jnp.float32)
                if kz == 0:
                    for k in range(1, nz):
                        got = last.at[k - 1]
                        arrived("plane", (k, 0, 0), got)
                        total = total + got[...].astype(jnp.float32)
                    out[...] = total
                    continue
        pair[at] = total.astype(pair.dtype)
        if ks:
            target_ref = second.at[at - nx * nz]
            target = spot(place, place.c, 0, 0, ks)
        elif kf:
            target_ref = first.at[(kf - 1) * nz + kz]
            target = spot(place, place.c, 0, kf, 0)
        else:
            target_ref = last.at[kz - 1]
            target = spot(place, place.c, kz, 0, 0)
        send("plane", label, pair.at[at], target_ref, place.device(*target))
    for copy in sent:
        copy.wait_send()


def scatter_dense(main, side, extra):
    nx = lax.axis_size("dp") // 2
    nz = lax.axis_size("expert") // nx
    plane = nx * nx * nz
    edges = 2 * plane - 1
    rows = main.shape[1]
    width = main.shape[2] + side.shape[2] + extra.shape[2]
    kind = main.dtype
    return pl.pallas_call(
        functools.partial(scatter_kernel, nx, nz),
        out_shape=jax.ShapeDtypeStruct((rows, width), jnp.float32),
        in_specs=[pl.BlockSpec(memory_space=pltpu.VMEM)] * 3,
        out_specs=pl.BlockSpec(memory_space=pltpu.VMEM),
        scratch_shapes=[
            pltpu.VMEM((2 * plane, rows, width), kind),
            pltpu.VMEM((plane, rows, width), kind),
            pltpu.VMEM((plane - nx * nz, rows, width), kind),
            pltpu.VMEM(((nx - 1) * nz, rows, width), kind),
            pltpu.VMEM((nz - 1, rows, width), kind),
            pltpu.SemaphoreType.DMA((edges,)),
            pltpu.SemaphoreType.DMA((edges,)),
        ],
        compiler_params=pltpu.CompilerParams(
            collective_id=1, has_side_effects=True, vmem_limit_bytes=VMEM_LIMIT
        ),
        name="scatter_dense",
    )(main, side, extra)


def toggle(value, k, size):
    out, bit = 0, 1
    while bit < size:
        out = out + bit * ((value // bit + k // bit) % 2)
        bit *= 2
    return out


def expert_kernel(
    nx,
    nz,
    rows_in,
    cots_in,
    up,
    down,
    back_out,
    back_grad,
    up_grad,
    down_grad,
    landed,
    slope,
    hidden,
    grad_pre,
    product,
    kept,
    pair_out,
    pair_in,
    line_out,
    line_in,
    total,
    plane_sem,
    line_sem,
    pair_sem,
    sum_sem,
    part_sem,
    home_sem,
):
    place = Place()
    ny = nx
    x, c, z, y = place.x, place.c, place.z, place.y
    me = z * ny + y
    capacity, width = rows_in.shape[1:]
    chunk = ny * nx * 2 * capacity
    f32 = jnp.float32
    sources = (rows_in, cots_in)
    backs = (back_out, back_grad)
    steps = 2 * nz
    partners = [
        place.device(x, c, flip(z, j), flip(y, k))
        for j in range(nz)
        for k in range(ny)
        if (j, k) != (0, 0)
    ]
    partners += [place.device(flip(x, k), c, z, y) for k in range(1, nx)]
    greet(partners + [place.sibling()])

    def copy_of(sem, at, source, target_ref, target):
        return pltpu.make_async_remote_copy(
            src_ref=source,
            dst_ref=target_ref,
            send_sem=sem.at[(0,) + at],
            recv_sem=sem.at[(1,) + at],
            device_id=target,
            device_id_type=MESH,
        )

    def send(sem, at, source, target_ref, target):
        copy_of(sem, at, source, target_ref, target).start()

    def arrived(sem, at, ref):
        copy_of(sem, at, ref, ref, place.sibling()).wait_recv()

    def left(sem, at, ref):
        copy_of(sem, at, ref, ref, place.sibling()).wait_send()

    def seat(a, j, k, kx, core):
        return landed.at[a, toggle(z, j, nz), flip(y, k), flip(x, kx), core]

    def spread(a, j, k, source):
        for kx in range(1, nx):
            target = place.device(flip(x, kx), c, z, y)
            send(line_sem, (a, j, k, kx), source, seat(a, j, k, 0, c), target)
        send(pair_sem, (a, j, k, 0), source, seat(a, j, k, 0, c), place.sibling())

    for a in range(2):
        for j in range(nz):
            for k in range(ny):
                if (j, k) != (0, 0):
                    there = (flip(z, j), flip(y, k))
                    send(
                        plane_sem,
                        (a, j, k),
                        sources[a].at[there[0] * ny + there[1]],
                        seat(a, 0, 0, 0, c),
                        place.device(x, c, *there),
                    )
                elif a == 0:
                    for b in range(2):
                        spread(b, 0, 0, sources[b].at[me])
    for a in range(2):
        landed[a, z, y, x, c] = sources[a][me]

    def take_plane(a, j):
        for k in range(ny):

            def take(k=k):
                arrived(plane_sem, (a, j, k), seat(a, j, k, 0, c))
                spread(a, j, k, seat(a, j, k, 0, c))

            if k == 0:
                pl.when(j > 0)(take)
            else:
                take()

    def take_line(a, j):
        for k in range(ny):
            for kx in range(1, nx):
                block = seat(a, j, k, kx, c)
                arrived(line_sem, (a, j, k, kx), block)
                send(pair_sem, (a, j, k, kx), block, block, place.sibling())

    def take_pair(a, j):
        for k in range(ny):
            for kx in range(nx):
                arrived(pair_sem, (a, j, k, kx), seat(a, j, k, kx, 1 - c))

    def give_pair(i, value):
        a, j = i // nz, i % nz
        product[...] = value.reshape(product.shape)
        kept[i % 3] = product[:, :, c]
        pair_out[a, j] = product[:, :, 1 - c].astype(pair_out.dtype)
        send(sum_sem, (a, j), pair_out.at[a, j], pair_in.at[a, j], place.sibling())

    def give_line(i):
        a, j = i // nz, i % nz
        arrived(sum_sem, (a, j), pair_in.at[a, j])
        kept[i % 3] = kept[i % 3] + pair_in[a, j].astype(f32)
        for kx in range(1, nx):
            line_out[a, j, kx - 1] = kept[i % 3, :, flip(x, kx)].astype(line_out.dtype)
            send(
                part_sem,
                (a, j, kx),
                line_out.at[a, j, kx - 1],
                line_in.at[a, j, kx - 1],
                place.device(flip(x, kx), c, z, y),
            )

    def give_plane(i):
        a, j = i // nz, i % nz
        value = kept[i % 3, :, x]
        for kx in range(1, nx):
            arrived(part_sem, (a, j, kx), line_in.at[a, j, kx - 1])
            value = value + line_in[a, j, kx - 1].astype(f32)
        total[a, j] = value.astype(total.dtype)
        for b in range(2):
            for k in range(ny):

                def go(b=b, k=k):
                    there = (toggle(z, j, nz), flip(y, k))
                    send(
                        home_sem,
                        (b, j, k),
                        total.at[b, j, there[1]],
                        backs[b].at[me],
                        place.device(x, c, *there),
                    )

                def stay(b=b):
                    backs[b][me] = total[b, 0, y]

                if k == 0:
                    pl.when((a == b) & (j > 0))(go)
                    pl.when((a == b) & (j == 0))(stay)
                else:
                    pl.when(a == b)(go)

    def forward(i, j):
        block = landed[0, toggle(z, j, nz)].reshape(chunk, width)
        before = jnp.dot(block, up[...], preferred_element_type=f32)
        bell = jnp.exp(-0.5 * before * before) * inv_root_two_pi
        share = 0.5 * (1.0 + lax.erf(before * inv_root_two))
        act = (before * share).astype(jnp.bfloat16)
        slope[j] = share + before * bell
        hidden[j] = act
        give_pair(
            i,
            lax.dot_general(act, down[...], (((1,), (1,)), ((), ())), preferred_element_type=f32),
        )

    def backward(i, j):
        block = landed[1, toggle(z, j, nz)].reshape(chunk, width)
        grad = jnp.dot(block, down[...], preferred_element_type=f32)
        pre = (grad * slope[j]).astype(jnp.bfloat16)
        grad_pre[j] = pre
        give_pair(
            i,
            lax.dot_general(pre, up[...], (((1,), (1,)), ((), ())), preferred_element_type=f32),
        )

    def weights(j):
        for a, (out, right) in enumerate(((up_grad, grad_pre), (down_grad, hidden))):
            out[...] += lax.dot_general(
                landed[a, toggle(z, j, nz)].reshape(chunk, width),
                right[j],
                (((0,), (0,)), ((), ())),
                preferred_element_type=f32,
            )

    take_plane(0, 0)

    @pl.loop(0, steps)
    def _(i):
        a, j = i // nz, i % nz
        pl.when(i + 1 < steps)(lambda: take_plane((i + 1) // nz, (i + 1) % nz))
        take_line(a, j)
        take_pair(a, j)
        pl.when(a == 0)(lambda: forward(i, j))
        pl.when(a == 1)(lambda: backward(i, j))
        pl.when(i >= 1)(lambda: give_line(i - 1))
        pl.when(i >= 2)(lambda: give_plane(i - 2))

    up_grad[...] = jnp.zeros_like(up_grad)
    down_grad[...] = jnp.zeros_like(down_grad)

    @pl.loop(0, nz)
    def _(j):
        weights(j)

        @pl.when(j == 0)
        def _():
            give_line(steps - 1)
            give_plane(steps - 2)

        pl.when(j == 1)(lambda: give_plane(steps - 1))

    for a in range(2):

        @pl.loop(0, nz)
        def _(j, a=a):
            left(sum_sem, (a, j), pair_out.at[a, j])
            for kx in range(1, nx):
                left(part_sem, (a, j, kx), line_out.at[a, j, kx - 1])
            for k in range(ny):
                for kx in range(nx):
                    left(pair_sem, (a, j, k, kx), seat(a, j, k, kx, c))
                    if kx:
                        left(line_sem, (a, j, k, kx), seat(a, j, k, 0, c))

                def rest(k=k):
                    there = toggle(z, j, nz) * ny + flip(y, k)
                    arrived(home_sem, (a, j, k), backs[a].at[there])
                    left(home_sem, (a, j, k), total.at[a, j, flip(y, k)])
                    left(plane_sem, (a, j, k), sources[a].at[there])

                if k == 0:
                    pl.when(j > 0)(rest)
                else:
                    rest()


def run_experts(rows_in, cots_in, up, down):
    nx = lax.axis_size("dp") // 2
    ny = nx
    nz = lax.axis_size("expert") // ny
    experts, capacity, width = rows_in.shape
    inner = up.shape[1]
    chunk = ny * nx * 2 * capacity
    half, f32 = jnp.bfloat16, jnp.float32
    vmem = pl.BlockSpec(memory_space=pltpu.VMEM)
    sems = [(ny,), (ny, nx), (ny, nx), (), (nx,), (ny,)]
    return pl.pallas_call(
        functools.partial(expert_kernel, nx, nz),
        out_shape=(
            jax.ShapeDtypeStruct(rows_in.shape, half),
            jax.ShapeDtypeStruct(rows_in.shape, half),
            jax.ShapeDtypeStruct(up.shape, f32),
            jax.ShapeDtypeStruct(down.shape, f32),
        ),
        in_specs=[vmem] * 4,
        out_specs=(vmem,) * 4,
        scratch_shapes=[
            pltpu.VMEM((2, nz, ny, nx, 2, capacity, width), half),
            pltpu.VMEM((nz, chunk, inner), f32),
            pltpu.VMEM((nz, chunk, inner), half),
            pltpu.VMEM((nz, chunk, inner), half),
            pltpu.VMEM((ny, nx, 2, capacity, width), f32),
            pltpu.VMEM((3, ny, nx, capacity, width), f32),
            pltpu.VMEM((2, nz, ny, nx, capacity, width), half),
            pltpu.VMEM((2, nz, ny, nx, capacity, width), half),
            pltpu.VMEM((2, nz, nx - 1, ny, capacity, width), half),
            pltpu.VMEM((2, nz, nx - 1, ny, capacity, width), half),
            pltpu.VMEM((2, nz, ny, capacity, width), half),
        ]
        + [pltpu.SemaphoreType.DMA((2, 2, nz) + shape) for shape in sems],
        compiler_params=pltpu.CompilerParams(
            collective_id=2, has_side_effects=True, vmem_limit_bytes=VMEM_LIMIT
        ),
        name="experts",
    )(rows_in, cots_in, up, down)


def per_device(
    tokens,
    packed_weight,
    output_weight,
    router_weight,
    first_gain,
    first_bias,
    second_gain,
    second_bias,
    expert_up,
    expert_down,
    expert_choice,
    slot_index,
    cotangent,
):
    local_tokens = tokens.shape[0]
    model_width = tokens.shape[1]
    top_count = expert_choice.shape[1]
    experts = lax.axis_size("expert")
    capacity = max(15 * local_tokens * top_count // (16 * experts), 2)
    rows_owned = packed_weight.shape[0]
    vectors = jnp.stack([first_gain, first_bias, second_gain, second_bias], axis=1)
    extra_columns = jnp.concatenate([router_weight, vectors], axis=1)
    extra_columns = jnp.pad(extra_columns, ((0, 0), (0, EXTRA - extra_columns.shape[1])))
    dense = gather_dense(jnp.concatenate([packed_weight, output_weight, extra_columns], axis=1))
    dense = dense.reshape(model_width, dense.shape[2])
    packed_full = dense[:, : 3 * model_width]
    output_full = dense[:, 3 * model_width : 4 * model_width]
    router_full = dense[:, 4 * model_width : 4 * model_width + experts]
    vectors = dense[:, 4 * model_width + experts : 4 * model_width + experts + 4].T
    gain_first, bias_first, second_norm_gain, bias_second = (vectors[i] for i in range(4))
    inputs = tokens.astype(jnp.float32)
    normed_first, unit_first, inverse_first = normalize(inputs, gain_first, bias_first)
    normed_first = normed_first.astype(jnp.bfloat16)
    packed = jnp.dot(normed_first, packed_full, preferred_element_type=jnp.float32).astype(
        jnp.bfloat16
    )
    packed_heads = packed.reshape(local_tokens // SEQ, SEQ, 3, HEADS, HEAD)
    mixed_heads, log_total = attend_forward(packed_heads)
    mixed_flat = mixed_heads.reshape(local_tokens, model_width)
    hidden_first = inputs + jnp.dot(mixed_flat, output_full, preferred_element_type=jnp.float32)
    normed_second, unit_second, inverse_second = normalize(
        hidden_first, second_norm_gain, bias_second
    )
    normed_second = normed_second.astype(jnp.bfloat16)
    logits = jnp.dot(normed_second, router_full, preferred_element_type=jnp.float32)
    exp_terms = jnp.exp(logits)
    router_probs = exp_terms / jnp.sum(exp_terms, axis=-1, keepdims=True)
    labels = jnp.arange(experts, dtype=jnp.int32)
    choice_mask = (expert_choice[:, :, None] == labels[None, None, :]).astype(jnp.float32)
    gate_values = jnp.sum(choice_mask * router_probs[:, None, :], axis=2)
    padded = -(-capacity // 16) * 16
    local_slot = jnp.where(
        slot_index < capacity, expert_choice * padded + slot_index, experts * padded
    )

    grad_top = cotangent.astype(jnp.float32)
    slots = jnp.arange(experts * padded, dtype=jnp.int32)
    place = [
        (local_slot[:, k, None] == slots[None, :]).astype(jnp.bfloat16) for k in range(top_count)
    ]
    place_any = sum(place[1:], place[0])
    slot_gate = sum(
        jnp.sum(place[k].astype(jnp.float32) * gate_values[:, k, None], axis=0)
        for k in range(top_count)
    )
    sent_rows = lax.dot_general(
        place_any, normed_second, (((0,), (0,)), ((), ())), preferred_element_type=jnp.float32
    ).astype(jnp.bfloat16)
    sent_cots = lax.dot_general(
        place_any, cotangent, (((0,), (0,)), ((), ())), preferred_element_type=jnp.float32
    )
    sent_cots = (sent_cots * slot_gate[:, None]).astype(jnp.bfloat16)
    block_shape = (experts, padded, model_width)
    returned_rows, grad_back, grad_up_part, grad_down_part = run_experts(
        sent_rows.reshape(block_shape),
        sent_cots.reshape(block_shape),
        expert_up[0],
        expert_down[0],
    )
    returned_rows = returned_rows.reshape(experts * padded, model_width)
    grad_back = grad_back.reshape(experts * padded, model_width)
    returned = [
        jnp.dot(place[k], returned_rows, preferred_element_type=jnp.float32)
        for k in range(top_count)
    ]
    combined = sum(gate_values[:, k, None] * returned[k] for k in range(top_count))
    block_output = (hidden_first + combined).astype(jnp.bfloat16)
    grad_gates = jnp.stack(
        [jnp.sum(grad_top * returned[k], axis=1) for k in range(top_count)], axis=1
    )
    gradient_second_normed = jnp.dot(place_any, grad_back, preferred_element_type=jnp.float32)
    grad_probs = jnp.sum(choice_mask * grad_gates[:, :, None], axis=1)
    grad_logits = (
        router_probs * (grad_probs - jnp.sum(router_probs * grad_probs, axis=1, keepdims=True))
    ).astype(jnp.bfloat16)
    grad_router = jnp.dot(normed_second.T, grad_logits, preferred_element_type=jnp.float32)
    gradient_second_normed = gradient_second_normed + jnp.einsum(
        "te,de->td", grad_logits, router_full, preferred_element_type=jnp.float32
    )
    grad_hidden, grad_gain_second, grad_bias_second = normalize_back(
        gradient_second_normed, unit_second, inverse_second, second_norm_gain
    )
    grad_hidden = grad_hidden + grad_top
    grad_hidden_half = grad_hidden.astype(jnp.bfloat16)
    grad_output = jnp.dot(mixed_flat.T, grad_hidden_half, preferred_element_type=jnp.float32)
    grad_mixed = jnp.einsum(
        "td,ed->te", grad_hidden_half, output_full, preferred_element_type=jnp.float32
    ).astype(jnp.bfloat16)
    grad_mixed = grad_mixed.reshape(local_tokens // SEQ, SEQ, HEADS, HEAD)
    gradient_packed_rows = (
        attend_back(packed_heads, log_total, grad_mixed)
        .reshape(local_tokens, 3 * model_width)
        .astype(jnp.bfloat16)
    )
    grad_packed_weight = jnp.dot(
        normed_first.T, gradient_packed_rows, preferred_element_type=jnp.float32
    )
    grad_normed_first = jnp.einsum(
        "tc,dc->td", gradient_packed_rows, packed_full, preferred_element_type=jnp.float32
    )
    grad_inputs, grad_gain_first, grad_bias_first = normalize_back(
        grad_normed_first, unit_first, inverse_first, gain_first
    )
    input_grad = (grad_inputs + grad_hidden).astype(jnp.bfloat16)
    extra_grad = jnp.concatenate(
        [
            grad_router,
            jnp.stack([grad_gain_first, grad_bias_first, grad_gain_second, grad_bias_second]).T,
        ],
        axis=1,
    )
    extra_grad = jnp.pad(extra_grad, ((0, 0), (0, EXTRA - extra_grad.shape[1])))
    owned = scatter_dense(
        *(
            part.astype(jnp.bfloat16).reshape(-1, rows_owned, part.shape[1])
            for part in (grad_packed_weight, grad_output, extra_grad)
        )
    )
    extra = 4 * model_width + experts
    return (
        block_output,
        input_grad,
        owned[:, : 3 * model_width],
        owned[:, 3 * model_width : 4 * model_width],
        owned[:, 4 * model_width : extra],
        owned[:, extra],
        owned[:, extra + 1],
        owned[:, extra + 2],
        owned[:, extra + 3],
        grad_up_part[None],
        grad_down_part[None],
    )


def solution(mesh):
    return jax.shard_map(
        per_device,
        mesh=mesh,
        in_specs=(
            P(("dp", "expert"), None),
            P(("dp", "expert"), None),
            P(("dp", "expert"), None),
            P(("dp", "expert"), None),
            P(("dp", "expert")),
            P(("dp", "expert")),
            P(("dp", "expert")),
            P(("dp", "expert")),
            P("expert", None, "dp"),
            P("expert", None, "dp"),
            P(("dp", "expert"), None),
            P(("dp", "expert"), None),
            P(("dp", "expert"), None),
        ),
        out_specs=(
            P(("dp", "expert"), None),
            P(("dp", "expert"), None),
            P(("dp", "expert"), None),
            P(("dp", "expert"), None),
            P(("dp", "expert"), None),
            P(("dp", "expert")),
            P(("dp", "expert")),
            P(("dp", "expert")),
            P(("dp", "expert")),
            P("expert", None, "dp"),
            P("expert", None, "dp"),
        ),
        check_vma=False,
    )
```

```python
import functools

import jax
import jax.numpy as jnp
from jax import lax
from jax.experimental import pallas as pl
from jax.experimental.pallas import tpu as pltpu
from jax.sharding import PartitionSpec as P

HEADS = 12
HEAD = 64
SEQ = 197


epsilon = 1e-06
inv_root_two = 0.7071067811865476
inv_root_two_pi = 0.3989422804014327


def normalize(rows_in, gain_vec, offset):
    centred = rows_in - jnp.mean(rows_in, axis=-1, keepdims=True)
    inverse = lax.rsqrt(jnp.mean(centred * centred, axis=-1, keepdims=True) + epsilon)
    unit_rows = centred * inverse
    return (
        unit_rows * gain_vec.astype(jnp.float32) + offset.astype(jnp.float32),
        unit_rows,
        inverse,
    )


def normalize_back(grad_rows, unit_rows, inverse, gain_vec):
    grad_unit = grad_rows * gain_vec.astype(jnp.float32)
    mean_grad = jnp.mean(grad_unit, axis=-1, keepdims=True)
    mean_dot = jnp.mean(grad_unit * unit_rows, axis=-1, keepdims=True)
    grad_in = inverse * (grad_unit - mean_grad - unit_rows * mean_dot)
    return (grad_in, jnp.sum(grad_rows * unit_rows, axis=0), jnp.sum(grad_rows, axis=0))


def gelu_exact(arg_values):
    return 0.5 * arg_values * (1.0 + jax.scipy.special.erf(arg_values * inv_root_two))


def gelu_slope(arg_values):
    return (
        0.5 * (1.0 + jax.scipy.special.erf(arg_values * inv_root_two))
        + arg_values * jnp.exp(-0.5 * arg_values * arg_values) * inv_root_two_pi
    )


def attend_forward(packed_heads):
    queries = packed_heads[:, :, 0]
    key_rows = packed_heads[:, :, 1]
    values = packed_heads[:, :, 2]
    router_scores = jnp.einsum(
        "ishd,ithd->ihst", queries, key_rows, preferred_element_type=jnp.float32
    ) * HEAD ** (-0.5)
    log_total = jnp.log(jnp.sum(jnp.exp(router_scores), axis=-1, keepdims=True))
    weights = jnp.exp(router_scores - log_total).astype(jnp.bfloat16)
    mixed_heads = jnp.einsum("ihst,ithd->ishd", weights, values, preferred_element_type=jnp.float32)
    return (mixed_heads.astype(jnp.bfloat16), log_total)


def attend_back(packed_heads, log_total, grad_mixed):
    queries = packed_heads[:, :, 0]
    key_rows = packed_heads[:, :, 1]
    values = packed_heads[:, :, 2]
    router_scores = jnp.einsum(
        "ishd,ithd->ihst", queries, key_rows, preferred_element_type=jnp.float32
    ) * HEAD ** (-0.5)
    weights = jnp.exp(router_scores - log_total)
    rounded = weights.astype(jnp.bfloat16)
    grad_values = jnp.einsum(
        "ihst,ishd->ithd", rounded, grad_mixed, preferred_element_type=jnp.float32
    )
    grad_weights = jnp.einsum(
        "ishd,ithd->ihst", grad_mixed, values, preferred_element_type=jnp.float32
    )
    row_delta = jnp.sum(weights * grad_weights, axis=-1, keepdims=True)
    grad_scores = (weights * (grad_weights - row_delta) * HEAD ** (-0.5)).astype(jnp.bfloat16)
    grad_queries = jnp.einsum(
        "ihst,ithd->ishd", grad_scores, key_rows, preferred_element_type=jnp.float32
    )
    grad_keys = jnp.einsum(
        "ihst,ishd->ithd", grad_scores, queries, preferred_element_type=jnp.float32
    )
    return jnp.stack([grad_queries, grad_keys, grad_values], axis=2)


EXTRA = 128
MESH = pl.DeviceIdType.MESH
VMEM_LIMIT = 60 * 1024 * 1024


class Place:
    def __init__(self):
        self.nx = lax.axis_size("dp") // 2
        self.ny = self.nx
        self.nz = lax.axis_size("expert") // self.ny
        dp, expert = lax.axis_index("dp"), lax.axis_index("expert")
        self.x, self.c = dp // 2, dp % 2
        self.z, self.y = expert // self.ny, expert % self.ny

    def device(self, x, c, z, y):
        return (x * 2 + c, z * self.ny + y)

    def owner(self, x, c, z, y):
        return (x * 2 + c) * (self.nz * self.ny) + z * self.ny + y

    def sibling(self):
        return self.device(self.x, 1 - self.c, self.z, self.y)


def flip(value, k):
    bit = 1
    out = value
    while bit <= k:
        if k & bit:
            out = out + bit * (1 - 2 * ((value // bit) % 2))
        bit *= 2
    return out


def toggle(value, k, size):
    out, bit = 0, 1
    while bit < size:
        out = out + bit * ((value // bit + k // bit) % 2)
        bit *= 2
    return out


def spot(place, core, kz, kf, ks):
    x, y = place.x, place.y
    dx = (1 - core) * (flip(x, kf) - x) + core * (flip(x, ks) - x)
    dy = (1 - core) * (flip(y, ks) - y) + core * (flip(y, kf) - y)
    z = flip(place.z, kz) if isinstance(kz, int) else toggle(place.z, kz, place.nz)
    return (x + dx, core, z, y + dy)


def greet(devices):
    barrier = pltpu.get_barrier_semaphore()
    for device in devices:
        pl.semaphore_signal(barrier, inc=1, device_id=device, device_id_type=MESH)
    pl.semaphore_wait(barrier, len(devices))


def grid_partners(place):
    partners = [place.device(*spot(place, place.c, k, 0, 0)) for k in range(1, place.nz)]
    partners += [place.device(*spot(place, place.c, 0, k, 0)) for k in range(1, place.nx)]
    partners += [place.device(*spot(place, place.c, 0, 0, k)) for k in range(1, place.nx)]
    return partners + [place.sibling()]


def labels_of(nx, nz):
    return [(kz, kf, ks) for ks in range(nx) for kf in range(nx) for kz in range(nz)]


def gather_kernel(nx, nz, shard, out, own_sem, send_sem, recv_sem):
    place = Place()
    labels = labels_of(nx, nz)
    number = {}
    for label in labels:
        if label != (0, 0, 0):
            number["plane", label] = len(number)
    for label in labels:
        number["pair", label] = len(number)
    greet(grid_partners(place))
    sent = []

    def here(label):
        return place.owner(*spot(place, place.c, *label))

    def send(kind, label, origin, target):
        at = number[kind, label]
        source = shard if origin == (0, 0, 0) else out.at[here(origin)]
        copy = pltpu.make_async_remote_copy(
            src_ref=source,
            dst_ref=out.at[here(origin)],
            send_sem=send_sem.at[at],
            recv_sem=recv_sem.at[at],
            device_id=target,
            device_id_type=MESH,
        )
        copy.start()
        sent.append(copy)

    def arrived(kind, label, index):
        at = number[kind, label]
        pltpu.make_async_remote_copy(
            src_ref=out.at[index],
            dst_ref=out.at[index],
            send_sem=send_sem.at[at],
            recv_sem=recv_sem.at[at],
            device_id=place.sibling(),
            device_id_type=MESH,
        ).wait_recv()

    def spread_first(kz):
        for kf in range(1, nx):
            send("plane", (kz, kf, 0), (kz, 0, 0), place.device(*spot(place, place.c, 0, kf, 0)))

    def spread_second(kz, kf):
        for ks in range(1, nx):
            send("plane", (kz, kf, ks), (kz, kf, 0), place.device(*spot(place, place.c, 0, 0, ks)))

    def share(label):
        send("pair", label, label, place.sibling())

    spread_first(0)
    spread_second(0, 0)
    for kz in range(1, nz):
        send("plane", (kz, 0, 0), (0, 0, 0), place.device(*spot(place, place.c, kz, 0, 0)))
    share((0, 0, 0))
    own = pltpu.make_async_copy(shard, out.at[here((0, 0, 0))], own_sem)
    own.start()
    for kz in range(1, nz + 1):
        if kz < nz:
            arrived("plane", (kz, 0, 0), here((kz, 0, 0)))
            spread_first(kz)
            spread_second(kz, 0)
            share((kz, 0, 0))
        for kf in range(1, nx):
            label = (kz - 1, kf, 0)
            arrived("plane", label, here(label))
            spread_second(kz - 1, kf)
            share(label)
    for kz in range(nz):
        for kf in range(nx):
            for ks in range(1, nx):
                arrived("plane", (kz, kf, ks), here((kz, kf, ks)))
                share((kz, kf, ks))
    for label in labels:
        arrived("pair", label, place.owner(*spot(place, 1 - place.c, *label)))
    own.wait()
    for copy in sent:
        copy.wait_send()


def gather_dense(shard):
    nx = lax.axis_size("dp") // 2
    nz = lax.axis_size("expert") // nx
    devices = 2 * nx * nx * nz
    edges = devices - 1
    return pl.pallas_call(
        functools.partial(gather_kernel, nx, nz),
        out_shape=jax.ShapeDtypeStruct((devices,) + shard.shape, shard.dtype),
        in_specs=[pl.BlockSpec(memory_space=pl.ANY)],
        out_specs=pl.BlockSpec(memory_space=pl.ANY),
        scratch_shapes=[
            pltpu.SemaphoreType.DMA,
            pltpu.SemaphoreType.DMA((edges,)),
            pltpu.SemaphoreType.DMA((edges,)),
        ],
        compiler_params=pltpu.CompilerParams(collective_id=0, has_side_effects=True),
        name="gather_dense",
    )(shard)


def expert_kernel(
    nx,
    nz,
    rows_in,
    cots_in,
    up,
    down,
    back_out,
    back_grad,
    up_grad,
    down_grad,
    landed,
    slope,
    hidden,
    grad_pre,
    product,
    kept,
    pair_out,
    pair_in,
    line_out,
    line_in,
    total,
    plane_sem,
    line_sem,
    pair_sem,
    sum_sem,
    part_sem,
    home_sem,
):
    place = Place()
    ny = nx
    x, c, z, y = place.x, place.c, place.z, place.y
    me = z * ny + y
    capacity, width = rows_in.shape[1:]
    chunk = ny * nx * 2 * capacity
    f32 = jnp.float32
    sources = (rows_in, cots_in)
    backs = (back_out, back_grad)
    steps = 2 * nz
    partners = [
        place.device(x, c, flip(z, j), flip(y, k))
        for j in range(nz)
        for k in range(ny)
        if (j, k) != (0, 0)
    ]
    partners += [place.device(flip(x, k), c, z, y) for k in range(1, nx)]
    greet(partners + [place.sibling()])

    def copy_of(sem, at, source, target_ref, target):
        return pltpu.make_async_remote_copy(
            src_ref=source,
            dst_ref=target_ref,
            send_sem=sem.at[(0,) + at],
            recv_sem=sem.at[(1,) + at],
            device_id=target,
            device_id_type=MESH,
        )

    def send(sem, at, source, target_ref, target):
        copy_of(sem, at, source, target_ref, target).start()

    def arrived(sem, at, ref):
        copy_of(sem, at, ref, ref, place.sibling()).wait_recv()

    def left(sem, at, ref):
        copy_of(sem, at, ref, ref, place.sibling()).wait_send()

    def seat(a, j, k, kx, core):
        return landed.at[a, toggle(z, j, nz), flip(y, k), flip(x, kx), core]

    def spread(a, j, k, source):
        for kx in range(1, nx):
            target = place.device(flip(x, kx), c, z, y)
            send(line_sem, (a, j, k, kx), source, seat(a, j, k, 0, c), target)
        send(pair_sem, (a, j, k, 0), source, seat(a, j, k, 0, c), place.sibling())

    for a in range(2):
        for j in range(nz):
            for k in range(ny):
                if (j, k) != (0, 0):
                    there = (flip(z, j), flip(y, k))
                    send(
                        plane_sem,
                        (a, j, k),
                        sources[a].at[there[0] * ny + there[1]],
                        seat(a, 0, 0, 0, c),
                        place.device(x, c, *there),
                    )
                elif a == 0:
                    for b in range(2):
                        spread(b, 0, 0, sources[b].at[me])
    for a in range(2):
        landed[a, z, y, x, c] = sources[a][me]

    def take_plane(a, j):
        for k in range(ny):

            def take(k=k):
                arrived(plane_sem, (a, j, k), seat(a, j, k, 0, c))
                spread(a, j, k, seat(a, j, k, 0, c))

            if k == 0:
                pl.when(j > 0)(take)
            else:
                take()

    def take_line(a, j):
        for k in range(ny):
            for kx in range(1, nx):
                block = seat(a, j, k, kx, c)
                arrived(line_sem, (a, j, k, kx), block)
                send(pair_sem, (a, j, k, kx), block, block, place.sibling())

    def take_pair(a, j):
        for k in range(ny):
            for kx in range(nx):
                arrived(pair_sem, (a, j, k, kx), seat(a, j, k, kx, 1 - c))

    def give_pair(i, value):
        a, j = i // nz, i % nz
        product[...] = value.reshape(product.shape)
        kept[i % 3] = product[:, :, c]
        pair_out[a, j] = product[:, :, 1 - c].astype(pair_out.dtype)
        send(sum_sem, (a, j), pair_out.at[a, j], pair_in.at[a, j], place.sibling())

    def give_line(i):
        a, j = i // nz, i % nz
        arrived(sum_sem, (a, j), pair_in.at[a, j])
        kept[i % 3] = kept[i % 3] + pair_in[a, j].astype(f32)
        for kx in range(1, nx):
            line_out[a, j, kx - 1] = kept[i % 3, :, flip(x, kx)].astype(line_out.dtype)
            send(
                part_sem,
                (a, j, kx),
                line_out.at[a, j, kx - 1],
                line_in.at[a, j, kx - 1],
                place.device(flip(x, kx), c, z, y),
            )

    def give_plane(i):
        a, j = i // nz, i % nz
        value = kept[i % 3, :, x]
        for kx in range(1, nx):
            arrived(part_sem, (a, j, kx), line_in.at[a, j, kx - 1])
            value = value + line_in[a, j, kx - 1].astype(f32)
        total[a, j] = value.astype(total.dtype)
        for b in range(2):
            for k in range(ny):

                def go(b=b, k=k):
                    there = (toggle(z, j, nz), flip(y, k))
                    send(
                        home_sem,
                        (b, j, k),
                        total.at[b, j, there[1]],
                        backs[b].at[me],
                        place.device(x, c, *there),
                    )

                def stay(b=b):
                    backs[b][me] = total[b, 0, y]

                if k == 0:
                    pl.when((a == b) & (j > 0))(go)
                    pl.when((a == b) & (j == 0))(stay)
                else:
                    pl.when(a == b)(go)

    def forward(i, j):
        block = landed[0, toggle(z, j, nz)].reshape(chunk, width)
        before = jnp.dot(block, up[...], preferred_element_type=f32)
        bell = jnp.exp(-0.5 * before * before) * inv_root_two_pi
        share = 0.5 * (1.0 + lax.erf(before * inv_root_two))
        act = (before * share).astype(jnp.bfloat16)
        slope[j] = share + before * bell
        hidden[j] = act
        give_pair(
            i,
            lax.dot_general(act, down[...], (((1,), (1,)), ((), ())), preferred_element_type=f32),
        )

    def backward(i, j):
        block = landed[1, toggle(z, j, nz)].reshape(chunk, width)
        grad = jnp.dot(block, down[...], preferred_element_type=f32)
        pre = (grad * slope[j]).astype(jnp.bfloat16)
        grad_pre[j] = pre
        give_pair(
            i,
            lax.dot_general(pre, up[...], (((1,), (1,)), ((), ())), preferred_element_type=f32),
        )

    def weights(j):
        for a, (out, right) in enumerate(((up_grad, grad_pre), (down_grad, hidden))):
            out[...] += lax.dot_general(
                landed[a, toggle(z, j, nz)].reshape(chunk, width),
                right[j],
                (((0,), (0,)), ((), ())),
                preferred_element_type=f32,
            )

    take_plane(0, 0)

    @pl.loop(0, steps)
    def _(i):
        a, j = i // nz, i % nz
        pl.when(i + 1 < steps)(lambda: take_plane((i + 1) // nz, (i + 1) % nz))
        take_line(a, j)
        take_pair(a, j)
        pl.when(a == 0)(lambda: forward(i, j))
        pl.when(a == 1)(lambda: backward(i, j))
        pl.when(i >= 1)(lambda: give_line(i - 1))
        pl.when(i >= 2)(lambda: give_plane(i - 2))

    up_grad[...] = jnp.zeros_like(up_grad)
    down_grad[...] = jnp.zeros_like(down_grad)

    @pl.loop(0, nz)
    def _(j):
        weights(j)

        @pl.when(j == 0)
        def _():
            give_line(steps - 1)
            give_plane(steps - 2)

        pl.when(j == 1)(lambda: give_plane(steps - 1))

    for a in range(2):

        @pl.loop(0, nz)
        def _(j, a=a):
            left(sum_sem, (a, j), pair_out.at[a, j])
            for kx in range(1, nx):
                left(part_sem, (a, j, kx), line_out.at[a, j, kx - 1])
            for k in range(ny):
                for kx in range(nx):
                    left(pair_sem, (a, j, k, kx), seat(a, j, k, kx, c))
                    if kx:
                        left(line_sem, (a, j, k, kx), seat(a, j, k, 0, c))

                def rest(k=k):
                    there = toggle(z, j, nz) * ny + flip(y, k)
                    arrived(home_sem, (a, j, k), backs[a].at[there])
                    left(home_sem, (a, j, k), total.at[a, j, flip(y, k)])
                    left(plane_sem, (a, j, k), sources[a].at[there])

                if k == 0:
                    pl.when(j > 0)(rest)
                else:
                    rest()


def run_experts(rows_in, cots_in, up, down):
    nx = lax.axis_size("dp") // 2
    ny = nx
    nz = lax.axis_size("expert") // ny
    experts, capacity, width = rows_in.shape
    inner = up.shape[1]
    chunk = ny * nx * 2 * capacity
    half, f32 = jnp.bfloat16, jnp.float32
    vmem = pl.BlockSpec(memory_space=pltpu.VMEM)
    sems = [(ny,), (ny, nx), (ny, nx), (), (nx,), (ny,)]
    return pl.pallas_call(
        functools.partial(expert_kernel, nx, nz),
        out_shape=(
            jax.ShapeDtypeStruct(rows_in.shape, half),
            jax.ShapeDtypeStruct(rows_in.shape, half),
            jax.ShapeDtypeStruct(up.shape, f32),
            jax.ShapeDtypeStruct(down.shape, f32),
        ),
        in_specs=[vmem] * 4,
        out_specs=(vmem,) * 4,
        scratch_shapes=[
            pltpu.VMEM((2, nz, ny, nx, 2, capacity, width), half),
            pltpu.VMEM((nz, chunk, inner), f32),
            pltpu.VMEM((nz, chunk, inner), half),
            pltpu.VMEM((nz, chunk, inner), half),
            pltpu.VMEM((ny, nx, 2, capacity, width), f32),
            pltpu.VMEM((3, ny, nx, capacity, width), f32),
            pltpu.VMEM((2, nz, ny, nx, capacity, width), half),
            pltpu.VMEM((2, nz, ny, nx, capacity, width), half),
            pltpu.VMEM((2, nz, nx - 1, ny, capacity, width), half),
            pltpu.VMEM((2, nz, nx - 1, ny, capacity, width), half),
            pltpu.VMEM((2, nz, ny, capacity, width), half),
        ]
        + [pltpu.SemaphoreType.DMA((2, 2, nz) + shape) for shape in sems],
        compiler_params=pltpu.CompilerParams(
            collective_id=2, has_side_effects=True, vmem_limit_bytes=VMEM_LIMIT
        ),
        name="experts",
    )(rows_in, cots_in, up, down)


def row_stats(rows):
    centred = rows - jnp.mean(rows, axis=-1, keepdims=True)
    inverse = lax.rsqrt(jnp.mean(centred * centred, axis=-1, keepdims=True) + epsilon)
    return centred * inverse, inverse


def row_stats_back(grad, unit_rows, inverse, gain_row):
    grad_unit = grad * gain_row
    mean_grad = jnp.mean(grad_unit, axis=-1, keepdims=True)
    mean_dot = jnp.mean(grad_unit * unit_rows, axis=-1, keepdims=True)
    return inverse * (grad_unit - mean_grad - unit_rows * mean_dot)


def dot_nt(left, right):
    return lax.dot_general(left, right, (((1,), (1,)), ((), ())), preferred_element_type=jnp.float32)


def dot_tn(left, right):
    return lax.dot_general(left, right, (((0,), (0,)), ((), ())), preferred_element_type=jnp.float32)


def dot_nn(left, right):
    return jnp.dot(left, right, preferred_element_type=jnp.float32)


def lanes_of(shape):
    return lax.broadcasted_iota(jnp.int32, shape, len(shape) - 1)


def router_terms(normed, extra, choice, experts):
    logits = dot_nn(normed, extra)
    lane = lanes_of(logits.shape)
    terms = jnp.where(lane < experts, jnp.exp(logits), 0.0)
    probs = terms / jnp.sum(terms, axis=-1, keepdims=True)
    masks = [(lane == choice[:, k : k + 1]).astype(jnp.float32) for k in range(choice.shape[1])]
    gates = [jnp.sum(mask * probs, axis=-1, keepdims=True) for mask in masks]
    return probs, masks, gates


def place_terms(choice, slot, capacity, padded, experts):
    where = jnp.where(slot < capacity, choice * padded + slot, experts * padded)
    lane = lanes_of((choice.shape[0], experts * padded))
    return [
        (lane == where[:, k : k + 1]).astype(jnp.float32).astype(jnp.bfloat16)
        for k in range(choice.shape[1])
    ]


def backward_kernel(
    nx,
    nz,
    experts,
    capacity,
    padded,
    tokens,
    cotangent,
    choice_in,
    slot_in,
    packed,
    mixed,
    hidden_in,
    returned_in,
    grad_back,
    dense,
    block_out,
    input_out,
    main_out,
    side_out,
    extra_out,
    tokens_pad,
    cots_pad,
    choice_pad,
    slot_pad,
    grads,
    tails,
    *boxes,
):
    place = Place()
    plane = nx * nx * nz
    count, width = tokens.shape
    rows_up = tokens_pad.shape[0]
    parts = width // 256
    half, f32 = jnp.bfloat16, jnp.float32
    pair, second, first, last, pair_t, second_t, first_t, last_t, sems = boxes
    owners = 2 * plane

    def refs(g):
        if g == parts + 1:
            return tails, pair_t, second_t, first_t, last_t
        return grads.at[g], pair.at[g], second.at[g], first.at[g], last.at[g]

    def copy_of(g, seat, source, target_ref, target):
        return pltpu.make_async_remote_copy(
            src_ref=source,
            dst_ref=target_ref,
            send_sem=sems.at[0, g, seat],
            recv_sem=sems.at[1, g, seat],
            device_id=target,
            device_id_type=MESH,
        )

    def arrived(g, seat, ref):
        copy_of(g, seat, ref, ref, place.sibling()).wait_recv()

    pairs = sorted(
        ((kf, ks) for kf in range(nx) for ks in range(nx)), key=lambda k: (k[1] == 0, k[0] == 0, k)
    )

    def at_of(kz, kf, ks):
        return ks * nx * nz + kf * nz + kz

    def scatter_pair(g):
        own, theirs = refs(g)[:2]
        for kf, ks in pairs:

            @pl.loop(0, nz)
            def _(i, kf=kf, ks=ks):
                kz = (i + 1) % nz
                index = place.owner(*spot(place, 1 - place.c, kz, kf, ks))
                at = at_of(kz, kf, ks)
                copy_of(g, at, own.at[index], theirs.at[at], place.sibling()).start()

    def gathered(g, kz, kf, ks):
        own, theirs, from_second, from_first, from_last = refs(g)
        at = at_of(kz, kf, ks)
        arrived(g, at, theirs.at[at])
        total = own[place.owner(*spot(place, place.c, kz, kf, ks))].astype(f32)
        total = total + theirs[at].astype(f32)
        if ks == 0:
            for k in range(1, nx):
                seat = at_of(kz, kf, k)
                arrived(g, plane + seat, from_second.at[seat - nx * nz])
                total = total + from_second[seat - nx * nz].astype(f32)
        if ks == 0 and kf == 0:
            for k in range(1, nx):
                seat = at_of(kz, k, 0)
                arrived(g, plane + seat, from_first.at[seat - nz])
                total = total + from_first[seat - nz].astype(f32)
        return total

    def pass_on(g, kz, kf, ks):
        own, theirs, from_second, from_first, from_last = refs(g)
        at = at_of(kz, kf, ks)
        theirs[at] = gathered(g, kz, kf, ks).astype(half)
        if ks:
            target_ref = from_second.at[at - nx * nz]
            target = spot(place, place.c, 0, 0, ks)
        elif kf:
            target_ref = from_first.at[at - nz]
            target = spot(place, place.c, 0, kf, 0)
        else:
            target_ref = from_last.at[kz - 1]
            target = spot(place, place.c, kz, 0, 0)
        copy_of(g, plane + at, theirs.at[at], target_ref, place.device(*target)).start()

    def scatter_stage(g, stage):
        if stage < 2:
            for kf, ks in pairs:
                if (ks > 0, ks == 0 and kf > 0)[stage]:

                    @pl.loop(0, nz)
                    def _(i, kf=kf, ks=ks):
                        pass_on(g, (i + 1) % nz, kf, ks)

        elif stage == 2:

            @pl.loop(1, nz)
            def _(kz):
                pass_on(g, kz, 0, 0)

        else:
            total = gathered(g, 0, 0, 0)
            from_last = refs(g)[4]
            for k in range(1, nz):
                arrived(g, plane + k, from_last.at[k - 1])
                total = total + from_last[k - 1].astype(f32)
            total = total[: side_out.shape[0]]
            if g == 0:
                side_out[...] = total
            elif g == parts + 1:
                extra_out[...] = total
            else:
                for i in range(3):
                    start = i * width + (g - 1) * 256
                    main_out[:, start : start + 256] = total[:, i * 256 : (i + 1) * 256]

    def scatter_end(g):
        own, theirs = refs(g)[:2]

        @pl.loop(0, plane)
        def _(at):
            copy_of(g, at, theirs.at[at], theirs.at[at], place.sibling()).wait_send()

            @pl.when(at > 0)
            def _():
                copy_of(g, plane + at, theirs.at[at], theirs.at[at], place.sibling()).wait_send()

    def fill(g, value, start):
        owned = owned_rows(value)
        if g == parts + 1:
            tails[...] = owned.astype(half)
        else:
            grads[g, :, :, start : start + value.shape[1]] = owned.astype(half)

    def owned_rows(value):
        rows = grads.shape[2]
        if rows * owners != width:
            shape = (rows * owners, width)
            at = lax.broadcasted_iota(jnp.int32, shape, 0)
            real = width // owners
            meant = jnp.where(at % rows < real, at // rows * real + at % rows, width)
            pick = (meant == lanes_of(shape)).astype(f32).astype(half)
            value = dot_nn(pick, value.astype(half))
        return value.reshape(owners, rows, value.shape[1])

    greet(grid_partners(place))

    for ref, source in (
        (tokens_pad, tokens),
        (cots_pad, cotangent),
        (choice_pad, choice_in),
        (slot_pad, slot_in),
    ):
        ref[...] = jnp.zeros_like(ref)
        ref[:count] = source[...]
    choice, slot = choice_pad[...], slot_pad[...]
    live = lax.broadcasted_iota(jnp.int32, choice.shape, 0) < count
    slot = jnp.where(live, slot, capacity)
    extra = dense[:, 4 * width :]
    turned = extra.astype(f32).T
    gain_first, bias_first, gain_second, bias_second = (
        turned[experts + i : experts + i + 1] for i in range(4)
    )
    grad_top = cots_pad[...].astype(f32)
    hidden_first = hidden_in[...]
    unit_second, inverse_second = row_stats(hidden_first)
    normed_second = (unit_second * gain_second + bias_second).astype(half)
    probs, masks, gates = router_terms(normed_second, extra, choice, experts)
    places = place_terms(choice, slot, capacity, padded, experts)
    returned = [dot_nn(one, returned_in[...]) for one in places]
    combined = sum(gate * rows for gate, rows in zip(gates, returned))
    block_out[...] = (hidden_first + combined)[:count].astype(half)
    gate_grads = [jnp.sum(grad_top * rows, axis=-1, keepdims=True) for rows in returned]
    grad_normed = dot_nn(sum(places[1:], places[0]), grad_back[...])
    grad_probs = sum(mask * grad for mask, grad in zip(masks, gate_grads))
    grad_logits = probs * (grad_probs - jnp.sum(probs * grad_probs, axis=-1, keepdims=True))
    grad_logits = grad_logits.astype(half)
    router_grad = dot_tn(normed_second, grad_logits)
    grad_normed = grad_normed + dot_nt(grad_logits, extra)
    second_sums = [
        jnp.sum(grad_normed * unit_second, axis=0, keepdims=True),
        jnp.sum(grad_normed, axis=0, keepdims=True),
    ]
    grad_hidden = grad_top + row_stats_back(grad_normed, unit_second, inverse_second, gain_second)
    grad_half = grad_hidden.astype(half)
    fill(0, dot_tn(mixed[...], grad_half), 0)
    scatter_pair(0)
    grad_mixed = dot_nt(grad_half, dense[:, 3 * width : 4 * width]).astype(half)
    unit_first, inverse_first = row_stats(tokens_pad[...].astype(f32))
    normed_first = (unit_first * gain_first + bias_first).astype(half)
    key_live = lax.broadcasted_iota(jnp.int32, (rows_up, rows_up), 0) < count
    lane = lanes_of((1, 128))
    sides = [((lane // 64) == i).astype(f32).astype(half) for i in range(2)]
    scale = HEAD ** (-0.5)
    grad_rows = jnp.zeros((rows_up, width), f32)
    for g in range(1, parts + 1):
        pieces = [[], [], []]
        for at in range((g - 1) * 256, g * 256, 128):
            query = packed[:, at : at + 128]
            key = packed[:, width + at : width + at + 128]
            value = packed[:, 2 * width + at : 2 * width + at + 128]
            grad = grad_mixed[:, at : at + 128]
            sums = [0.0, 0.0, 0.0]
            for side in sides:
                query_one, key_one, grad_one = query * side, key * side, grad * side
                terms = jnp.where(key_live, jnp.exp(dot_nt(key, query_one) * scale), 0.0)
                weights = terms * (1.0 / jnp.sum(terms, axis=0, keepdims=True))
                grad_weights = dot_nt(value, grad_one)
                delta = jnp.sum(weights * grad_weights, axis=0, keepdims=True)
                grad_scores = (weights * (grad_weights - delta) * scale).astype(half)
                sums[0] = sums[0] + dot_tn(grad_scores, key_one)
                sums[1] = sums[1] + dot_nn(grad_scores, query_one)
                sums[2] = sums[2] + dot_nn(weights.astype(half), grad_one)
            for piece, total in zip(pieces, sums):
                piece.append(total.astype(half))
        for i in range(3):
            joined = jnp.concatenate(pieces[i], axis=1)
            start = i * width + (g - 1) * 256
            grad_rows = grad_rows + dot_nt(joined, dense[:, start : start + 256])
            fill(g, dot_tn(normed_first, joined), i * 256)
        scatter_pair(g)
        for back in range(3):
            if g - 1 - back >= 0:
                scatter_stage(g - 1 - back, back)
    first_sums = [
        jnp.sum(grad_rows * unit_first, axis=0, keepdims=True),
        jnp.sum(grad_rows, axis=0, keepdims=True),
    ]
    lines = first_sums + second_sums
    line_at = lax.broadcasted_iota(jnp.int32, turned.shape, 0)
    columns = sum(jnp.where(line_at == experts + i, lines[i], 0.0) for i in range(4))
    fill(parts + 1, router_grad + columns.T, 0)
    scatter_pair(parts + 1)
    scatter_stage(parts, 0)
    grad_inputs = row_stats_back(grad_rows, unit_first, inverse_first, gain_first)
    input_out[...] = (grad_inputs + grad_hidden)[:count].astype(half)
    for g in range(parts + 1, parts + 6):
        for back in range(4):
            if g - 1 - back <= parts + 1 and (g, back) != (parts + 1, 0):
                scatter_stage(g - 1 - back, back)
    for g in range(parts + 2):
        scatter_end(g)


def run_backward(sizes, arrays, rows_owned):
    nx = lax.axis_size("dp") // 2
    nz = lax.axis_size("expert") // nx
    plane = nx * nx * nz
    tile_rows = -(-rows_owned // 8) * 8
    tokens, packed, dense = arrays[0], arrays[4], arrays[-1]
    count, width = tokens.shape
    rows_up = packed.shape[0]
    top = arrays[2].shape[1]
    parts = width // 256
    rest = dense.shape[1] - 4 * width
    half, f32 = jnp.bfloat16, jnp.float32
    vmem = pl.BlockSpec(memory_space=pltpu.VMEM)

    def boxes(lead, columns):
        return [
            pltpu.VMEM(lead + (size, tile_rows, columns), half)
            for size in (plane, plane - nx * nz, (nx - 1) * nz, nz - 1)
        ]

    return pl.pallas_call(
        functools.partial(backward_kernel, nx, nz, *sizes),
        out_shape=(
            jax.ShapeDtypeStruct((count, width), half),
            jax.ShapeDtypeStruct((count, width), half),
            jax.ShapeDtypeStruct((rows_owned, 3 * width), f32),
            jax.ShapeDtypeStruct((rows_owned, width), f32),
            jax.ShapeDtypeStruct((rows_owned, rest), f32),
        ),
        in_specs=[vmem] * len(arrays),
        out_specs=(vmem,) * 5,
        scratch_shapes=[
            pltpu.VMEM((rows_up, width), half),
            pltpu.VMEM((rows_up, width), half),
            pltpu.VMEM((rows_up, top), jnp.int32),
            pltpu.VMEM((rows_up, top), jnp.int32),
            pltpu.VMEM((parts + 1, 2 * plane, tile_rows, width), half),
            pltpu.VMEM((2 * plane, tile_rows, rest), half),
        ]
        + boxes((parts + 1,), width)
        + boxes((), rest)
        + [pltpu.SemaphoreType.DMA((2, parts + 2, 2 * plane))],
        compiler_params=pltpu.CompilerParams(
            collective_id=1, has_side_effects=True, vmem_limit_bytes=VMEM_LIMIT
        ),
        name="backward",
    )(*arrays)


def per_device(
    tokens,
    packed_weight,
    output_weight,
    router_weight,
    first_gain,
    first_bias,
    second_gain,
    second_bias,
    expert_up,
    expert_down,
    expert_choice,
    slot_index,
    cotangent,
):
    local_tokens = tokens.shape[0]
    model_width = tokens.shape[1]
    top_count = expert_choice.shape[1]
    experts = lax.axis_size("expert")
    capacity = max(15 * local_tokens * top_count // (16 * experts), 2)
    rows_owned = packed_weight.shape[0]
    vectors = jnp.stack([first_gain, first_bias, second_gain, second_bias], axis=1)
    extra_columns = jnp.concatenate([router_weight, vectors], axis=1)
    extra_columns = jnp.pad(extra_columns, ((0, 0), (0, EXTRA - extra_columns.shape[1])))
    dense = gather_dense(jnp.concatenate([packed_weight, output_weight, extra_columns], axis=1))
    dense = dense.reshape(model_width, dense.shape[2])
    packed_full = dense[:, : 3 * model_width]
    output_full = dense[:, 3 * model_width : 4 * model_width]
    router_full = dense[:, 4 * model_width : 4 * model_width + experts]
    vectors = dense[:, 4 * model_width + experts : 4 * model_width + experts + 4].T
    gain_first, bias_first, second_norm_gain, bias_second = (vectors[i] for i in range(4))
    inputs = tokens.astype(jnp.float32)
    normed_first, unit_first, inverse_first = normalize(inputs, gain_first, bias_first)
    normed_first = normed_first.astype(jnp.bfloat16)
    packed = jnp.dot(normed_first, packed_full, preferred_element_type=jnp.float32).astype(
        jnp.bfloat16
    )
    packed_heads = packed.reshape(local_tokens // SEQ, SEQ, 3, HEADS, HEAD)
    mixed_heads, log_total = attend_forward(packed_heads)
    mixed_flat = mixed_heads.reshape(local_tokens, model_width)
    hidden_first = inputs + jnp.dot(mixed_flat, output_full, preferred_element_type=jnp.float32)
    normed_second, unit_second, inverse_second = normalize(
        hidden_first, second_norm_gain, bias_second
    )
    normed_second = normed_second.astype(jnp.bfloat16)
    logits = jnp.dot(normed_second, router_full, preferred_element_type=jnp.float32)
    exp_terms = jnp.exp(logits)
    router_probs = exp_terms / jnp.sum(exp_terms, axis=-1, keepdims=True)
    labels = jnp.arange(experts, dtype=jnp.int32)
    choice_mask = (expert_choice[:, :, None] == labels[None, None, :]).astype(jnp.float32)
    gate_values = jnp.sum(choice_mask * router_probs[:, None, :], axis=2)
    padded = -(-capacity // 16) * 16
    local_slot = jnp.where(
        slot_index < capacity, expert_choice * padded + slot_index, experts * padded
    )

    slots = jnp.arange(experts * padded, dtype=jnp.int32)
    place = [
        (local_slot[:, k, None] == slots[None, :]).astype(jnp.bfloat16) for k in range(top_count)
    ]
    place_any = sum(place[1:], place[0])
    slot_gate = sum(
        jnp.sum(place[k].astype(jnp.float32) * gate_values[:, k, None], axis=0)
        for k in range(top_count)
    )
    sent_rows = lax.dot_general(
        place_any, normed_second, (((0,), (0,)), ((), ())), preferred_element_type=jnp.float32
    ).astype(jnp.bfloat16)
    sent_cots = lax.dot_general(
        place_any, cotangent, (((0,), (0,)), ((), ())), preferred_element_type=jnp.float32
    )
    sent_cots = (sent_cots * slot_gate[:, None]).astype(jnp.bfloat16)
    block_shape = (experts, padded, model_width)
    returned_rows, grad_back, grad_up_part, grad_down_part = run_experts(
        sent_rows.reshape(block_shape),
        sent_cots.reshape(block_shape),
        expert_up[0],
        expert_down[0],
    )
    returned_rows = returned_rows.reshape(experts * padded, model_width)
    grad_back = grad_back.reshape(experts * padded, model_width)
    rows_up = -(-local_tokens // 16) * 16
    spare = ((0, rows_up - local_tokens), (0, 0))
    block_output, input_grad, main_grad, side_grad, extra_grad = run_backward(
        (experts, capacity, padded),
        (
            tokens,
            cotangent,
            expert_choice,
            slot_index,
            jnp.pad(packed, spare),
            jnp.pad(mixed_flat, spare),
            jnp.pad(hidden_first, spare),
            returned_rows,
            grad_back,
            dense,
        ),
        rows_owned,
    )
    return (
        block_output,
        input_grad,
        main_grad,
        side_grad,
        extra_grad[:, :experts],
        extra_grad[:, experts],
        extra_grad[:, experts + 1],
        extra_grad[:, experts + 2],
        extra_grad[:, experts + 3],
        grad_up_part[None],
        grad_down_part[None],
    )


def solution(mesh):
    return jax.shard_map(
        per_device,
        mesh=mesh,
        in_specs=(
            P(("dp", "expert"), None),
            P(("dp", "expert"), None),
            P(("dp", "expert"), None),
            P(("dp", "expert"), None),
            P(("dp", "expert")),
            P(("dp", "expert")),
            P(("dp", "expert")),
            P(("dp", "expert")),
            P("expert", None, "dp"),
            P("expert", None, "dp"),
            P(("dp", "expert"), None),
            P(("dp", "expert"), None),
            P(("dp", "expert"), None),
        ),
        out_specs=(
            P(("dp", "expert"), None),
            P(("dp", "expert"), None),
            P(("dp", "expert"), None),
            P(("dp", "expert"), None),
            P(("dp", "expert"), None),
            P(("dp", "expert")),
            P(("dp", "expert")),
            P(("dp", "expert")),
            P(("dp", "expert")),
            P("expert", None, "dp"),
            P("expert", None, "dp"),
        ),
        check_vma=False,
    )
```

```python
import functools

import jax
import jax.numpy as jnp
from jax import lax
from jax.experimental import pallas as pl
from jax.experimental.pallas import tpu as pltpu
from jax.sharding import PartitionSpec as P

HEADS = 12
HEAD = 64
SEQ = 197


epsilon = 1e-06
inv_root_two = 0.7071067811865476
inv_root_two_pi = 0.3989422804014327


EXTRA = 128
MESH = pl.DeviceIdType.MESH
VMEM_LIMIT = 60 * 1024 * 1024


class Place:
    def __init__(self):
        self.nx = lax.axis_size("dp") // 2
        self.ny = self.nx
        self.nz = lax.axis_size("expert") // self.ny
        dp, expert = lax.axis_index("dp"), lax.axis_index("expert")
        self.x, self.c = dp // 2, dp % 2
        self.z, self.y = expert // self.ny, expert % self.ny

    def device(self, x, c, z, y):
        return (x * 2 + c, z * self.ny + y)

    def owner(self, x, c, z, y):
        return (x * 2 + c) * (self.nz * self.ny) + z * self.ny + y

    def sibling(self):
        return self.device(self.x, 1 - self.c, self.z, self.y)


def flip(value, k):
    bit = 1
    out = value
    while bit <= k:
        if k & bit:
            out = out + bit * (1 - 2 * ((value // bit) % 2))
        bit *= 2
    return out


def toggle(value, k, size):
    out, bit = 0, 1
    while bit < size:
        out = out + bit * ((value // bit + k // bit) % 2)
        bit *= 2
    return out


def spot(place, core, kz, kf, ks):
    x, y = place.x, place.y
    dx = (1 - core) * (flip(x, kf) - x) + core * (flip(x, ks) - x)
    dy = (1 - core) * (flip(y, ks) - y) + core * (flip(y, kf) - y)
    z = flip(place.z, kz) if isinstance(kz, int) else toggle(place.z, kz, place.nz)
    return (x + dx, core, z, y + dy)


def greet(devices):
    barrier = pltpu.get_barrier_semaphore()
    for device in devices:
        pl.semaphore_signal(barrier, inc=1, device_id=device, device_id_type=MESH)
    pl.semaphore_wait(barrier, len(devices))


def grid_partners(place):
    partners = [place.device(*spot(place, place.c, k, 0, 0)) for k in range(1, place.nz)]
    partners += [place.device(*spot(place, place.c, 0, k, 0)) for k in range(1, place.nx)]
    partners += [place.device(*spot(place, place.c, 0, 0, k)) for k in range(1, place.nx)]
    return partners + [place.sibling()]


def labels_of(nx, nz):
    return [(kz, kf, ks) for ks in range(nx) for kf in range(nx) for kz in range(nz)]


def gather_kernel(
    nx, nz, main, side, router, first, second, third, fourth, out, shard, own_sem, send_sem, recv_sem
):
    place = Place()
    rows, width = side.shape
    experts = router.shape[1]
    shard[:, : 3 * width] = main[...]
    shard[:, 3 * width : 4 * width] = side[...]
    lane = lanes_of((rows, EXTRA))
    diagonal = lanes_of((rows, rows)) == lax.broadcasted_iota(jnp.int32, (rows, rows), 0)
    extra = jnp.zeros((rows, EXTRA), jnp.float32)
    for i, vector in enumerate((first, second, third, fourth)):
        spread = jnp.where(diagonal, vector[...].astype(jnp.float32), 0.0)
        column = jnp.sum(spread, axis=1, keepdims=True)
        extra = jnp.where(lane == experts + i, column, extra)
    shard[:, 4 * width :] = extra.astype(shard.dtype)
    shard[:, 4 * width : 4 * width + experts] = router[...]
    labels = labels_of(nx, nz)
    number = {}
    for label in labels:
        if label != (0, 0, 0):
            number["plane", label] = len(number)
    for label in labels:
        number["pair", label] = len(number)
    greet(grid_partners(place))
    sent = []

    def here(label):
        return place.owner(*spot(place, place.c, *label))

    def send(kind, label, origin, target):
        at = number[kind, label]
        source = shard if origin == (0, 0, 0) else out.at[here(origin)]
        copy = pltpu.make_async_remote_copy(
            src_ref=source,
            dst_ref=out.at[here(origin)],
            send_sem=send_sem.at[at],
            recv_sem=recv_sem.at[at],
            device_id=target,
            device_id_type=MESH,
        )
        copy.start()
        sent.append(copy)

    def arrived(kind, label, index):
        at = number[kind, label]
        pltpu.make_async_remote_copy(
            src_ref=out.at[index],
            dst_ref=out.at[index],
            send_sem=send_sem.at[at],
            recv_sem=recv_sem.at[at],
            device_id=place.sibling(),
            device_id_type=MESH,
        ).wait_recv()

    def spread_first(kz):
        for kf in range(1, nx):
            send("plane", (kz, kf, 0), (kz, 0, 0), place.device(*spot(place, place.c, 0, kf, 0)))

    def spread_second(kz, kf):
        for ks in range(1, nx):
            send("plane", (kz, kf, ks), (kz, kf, 0), place.device(*spot(place, place.c, 0, 0, ks)))

    def share(label):
        send("pair", label, label, place.sibling())

    spread_first(0)
    spread_second(0, 0)
    for kz in range(1, nz):
        send("plane", (kz, 0, 0), (0, 0, 0), place.device(*spot(place, place.c, kz, 0, 0)))
    share((0, 0, 0))
    own = pltpu.make_async_copy(shard, out.at[here((0, 0, 0))], own_sem)
    own.start()
    for kz in range(1, nz + 1):
        if kz < nz:
            arrived("plane", (kz, 0, 0), here((kz, 0, 0)))
            spread_first(kz)
            spread_second(kz, 0)
            share((kz, 0, 0))
        for kf in range(1, nx):
            label = (kz - 1, kf, 0)
            arrived("plane", label, here(label))
            spread_second(kz - 1, kf)
            share(label)
    for kz in range(nz):
        for kf in range(nx):
            for ks in range(1, nx):
                arrived("plane", (kz, kf, ks), here((kz, kf, ks)))
                share((kz, kf, ks))
    for label in labels:
        arrived("pair", label, place.owner(*spot(place, 1 - place.c, *label)))
    own.wait()
    for copy in sent:
        copy.wait_send()


def gather_dense(main, side, router, vectors):
    nx = lax.axis_size("dp") // 2
    nz = lax.axis_size("expert") // nx
    devices = 2 * nx * nx * nz
    edges = devices - 1
    rows, width = side.shape
    shape = (rows, 4 * width + EXTRA)
    vmem = pl.BlockSpec(memory_space=pltpu.VMEM)
    return pl.pallas_call(
        functools.partial(gather_kernel, nx, nz),
        out_shape=jax.ShapeDtypeStruct((devices,) + shape, side.dtype),
        in_specs=[vmem] * 7,
        out_specs=pl.BlockSpec(memory_space=pl.ANY),
        scratch_shapes=[
            pltpu.VMEM(shape, side.dtype),
            pltpu.SemaphoreType.DMA,
            pltpu.SemaphoreType.DMA((edges,)),
            pltpu.SemaphoreType.DMA((edges,)),
        ],
        compiler_params=pltpu.CompilerParams(collective_id=0, has_side_effects=True),
        name="gather_dense",
    )(main, side, router, *(vector.reshape(1, rows) for vector in vectors))


def row_stats(rows):
    centred = rows - jnp.mean(rows, axis=-1, keepdims=True)
    inverse = lax.rsqrt(jnp.mean(centred * centred, axis=-1, keepdims=True) + epsilon)
    return centred * inverse, inverse


def row_stats_back(grad, unit_rows, inverse, gain_row):
    grad_unit = grad * gain_row
    mean_grad = jnp.mean(grad_unit, axis=-1, keepdims=True)
    mean_dot = jnp.mean(grad_unit * unit_rows, axis=-1, keepdims=True)
    return inverse * (grad_unit - mean_grad - unit_rows * mean_dot)


def dot_nt(left, right):
    return lax.dot_general(left, right, (((1,), (1,)), ((), ())), preferred_element_type=jnp.float32)


def dot_tn(left, right):
    return lax.dot_general(left, right, (((0,), (0,)), ((), ())), preferred_element_type=jnp.float32)


def dot_nn(left, right):
    return jnp.dot(left, right, preferred_element_type=jnp.float32)


def lanes_of(shape):
    return lax.broadcasted_iota(jnp.int32, shape, len(shape) - 1)


def router_terms(normed, extra, choice, experts):
    logits = dot_nn(normed, extra)
    lane = lanes_of(logits.shape)
    terms = jnp.where(lane < experts, jnp.exp(logits), 0.0)
    probs = terms / jnp.sum(terms, axis=-1, keepdims=True)
    lane = lane.astype(jnp.float32)
    masks = [(lane == one).astype(jnp.float32) for one in choice]
    gates = [jnp.sum(mask * probs, axis=-1, keepdims=True) for mask in masks]
    return probs, masks, gates


def read_choices(choice_in, slot_in, turn, rows_up, capacity):
    top, count = choice_in.shape
    turn[...] = jnp.zeros_like(turn)
    turn[:top, :count] = choice_in[...].astype(jnp.float32)
    turn[top : 2 * top, :count] = slot_in[...].astype(jnp.float32)
    turned = turn[...].T[:rows_up]
    live = lax.broadcasted_iota(jnp.int32, (rows_up, 1), 0) < count
    choice = [turned[:, k : k + 1] for k in range(top)]
    slot = [
        jnp.where(live, turned[:, top + k : top + k + 1], float(capacity)) for k in range(top)
    ]
    return choice, slot


def place_terms(choice, slot, capacity, padded, experts):
    lane = lanes_of((choice[0].shape[0], experts * padded)).astype(jnp.float32)
    places = []
    for one, at in zip(choice, slot):
        where = jnp.where(at < capacity, one * padded + at, float(experts * padded))
        places.append((lane == where).astype(jnp.float32).astype(jnp.bfloat16))
    return places


def expert_kernel(
    nx,
    nz,
    experts,
    taken,
    tokens,
    cotangent,
    choice_in,
    slot_in,
    dense,
    up,
    down,
    back_out,
    back_grad,
    up_grad,
    down_grad,
    packed,
    mixed,
    hidden_out,
    rows_pad,
    turn,
    rows_in,
    cots_in,
    gate_of,
    landed,
    gated,
    slope,
    hidden,
    grad_pre,
    product,
    kept,
    pair_out,
    pair_in,
    line_out,
    line_in,
    total,
    plane_sem,
    line_sem,
    pair_sem,
    sum_sem,
    part_sem,
    home_sem,
):
    place = Place()
    ny = nx
    x, c, z, y = place.x, place.c, place.z, place.y
    me = z * ny + y
    capacity, width = rows_in.shape[1:]
    count = tokens.shape[0]
    rows_up = rows_pad.shape[0]
    parts = width // 256
    half = jnp.bfloat16
    chunk = ny * nx * 2 * capacity
    f32 = jnp.float32
    sources = (rows_in, cots_in)
    backs = (back_out, back_grad)
    steps = 2 * nz
    partners = [
        place.device(x, c, flip(z, j), flip(y, k))
        for j in range(nz)
        for k in range(ny)
        if (j, k) != (0, 0)
    ]
    partners += [place.device(flip(x, k), c, z, y) for k in range(1, nx)]
    greet(partners + [place.sibling()])

    def copy_of(sem, at, source, target_ref, target):
        return pltpu.make_async_remote_copy(
            src_ref=source,
            dst_ref=target_ref,
            send_sem=sem.at[(0,) + at],
            recv_sem=sem.at[(1,) + at],
            device_id=target,
            device_id_type=MESH,
        )

    def send(sem, at, source, target_ref, target):
        copy_of(sem, at, source, target_ref, target).start()

    def arrived(sem, at, ref):
        copy_of(sem, at, ref, ref, place.sibling()).wait_recv()

    def left(sem, at, ref):
        copy_of(sem, at, ref, ref, place.sibling()).wait_send()

    def seat(a, j, k, kx, core):
        return landed.at[a, toggle(z, j, nz), flip(y, k), flip(x, kx), core]

    def spread(a, j, k, source):
        for kx in range(1, nx):
            target = place.device(flip(x, kx), c, z, y)
            send(line_sem, (a, j, k, kx), source, seat(a, j, k, 0, c), target)
        send(pair_sem, (a, j, k, 0), source, seat(a, j, k, 0, c), place.sibling())

    def dispatch(a, value):
        sources[a][...] = value.astype(half).reshape(sources[a].shape)
        for j in range(nz):
            for k in range(ny):
                if (j, k) != (0, 0):
                    there = (flip(z, j), flip(y, k))
                    send(
                        plane_sem,
                        (a, j, k),
                        sources[a].at[there[0] * ny + there[1]],
                        seat(a, 0, 0, 0, c),
                        place.device(x, c, *there),
                    )
                else:
                    spread(a, 0, 0, sources[a].at[me])
        landed[a, z, y, x, c] = sources[a][me]

    def take_plane(a, j):
        for k in range(ny):

            def take(k=k):
                arrived(plane_sem, (a, j, k), seat(a, j, k, 0, c))
                spread(a, j, k, seat(a, j, k, 0, c))

            if k == 0:
                pl.when(j > 0)(take)
            else:
                take()

    def take_line(a, j):
        for k in range(ny):
            for kx in range(1, nx):
                block = seat(a, j, k, kx, c)
                arrived(line_sem, (a, j, k, kx), block)
                send(pair_sem, (a, j, k, kx), block, block, place.sibling())

    def take_pair(a, j):
        for k in range(ny):
            for kx in range(nx):
                arrived(pair_sem, (a, j, k, kx), seat(a, j, k, kx, 1 - c))

    def pair_left(i):
        left(sum_sem, (i % 2, i // 2), pair_out.at[i % 3])

    def line_left(i):
        for kx in range(1, nx):
            left(part_sem, (i % 2, i // 2, kx), line_out.at[i % 3, kx - 1])

    def give_pair(i, value):
        a, j = i % 2, i // 2
        product[...] = value.reshape(product.shape)
        kept[i % 3] = product[:, :, c]
        pl.when(i >= 3)(lambda: pair_left(i - 3))
        pair_out[i % 3] = product[:, :, 1 - c].astype(half)
        send(sum_sem, (a, j), pair_out.at[i % 3], pair_in.at[a, j], place.sibling())

    def give_line(i):
        a, j = i % 2, i // 2
        arrived(sum_sem, (a, j), pair_in.at[a, j])
        kept[i % 3] = kept[i % 3] + pair_in[a, j].astype(f32)
        pl.when(i >= 3)(lambda: line_left(i - 3))
        for kx in range(1, nx):
            line_out[i % 3, kx - 1] = kept[i % 3, :, flip(x, kx)].astype(half)
            send(
                part_sem,
                (a, j, kx),
                line_out.at[i % 3, kx - 1],
                line_in.at[a, j, kx - 1],
                place.device(flip(x, kx), c, z, y),
            )

    def give_plane(i):
        a, j = i % 2, i // 2
        value = kept[i % 3, :, x]
        for kx in range(1, nx):
            arrived(part_sem, (a, j, kx), line_in.at[a, j, kx - 1])
            value = value + line_in[a, j, kx - 1].astype(f32)
        total[a, j] = value.astype(total.dtype)
        for b in range(2):
            for k in range(ny):

                def go(b=b, k=k):
                    there = (toggle(z, j, nz), flip(y, k))
                    send(
                        home_sem,
                        (b, j, k),
                        total.at[b, j, there[1]],
                        backs[b].at[me],
                        place.device(x, c, *there),
                    )

                def stay(b=b):
                    backs[b][me] = total[b, 0, y]

                if k == 0:
                    pl.when((a == b) & (j > 0))(go)
                    pl.when((a == b) & (j == 0))(stay)
                else:
                    pl.when(a == b)(go)

    def forward(i, j):
        block = landed[0, toggle(z, j, nz)].reshape(chunk, width)
        logits = dot_nn(block, dense[:, 4 * width :])
        lane = lanes_of(logits.shape)
        terms = jnp.where(lane < experts, jnp.exp(logits), 0.0)
        mine = jnp.sum(jnp.where(lane == me, terms, 0.0), axis=-1, keepdims=True)
        gate_of[...] = mine / jnp.sum(terms, axis=-1, keepdims=True)
        before = dot_nn(block, up[...])
        bell = jnp.exp(-0.5 * before * before) * inv_root_two_pi
        share = 0.5 * (1.0 + lax.erf(before * inv_root_two))
        act = (before * share).astype(half)
        slope[...] = share + before * bell
        hidden[j] = act
        give_pair(i, dot_nt(act, down[...]))

    def backward(i, j):
        block = landed[1, toggle(z, j, nz)].reshape(chunk, width).astype(f32)
        block = (block * gate_of[...]).astype(half)
        gated[j] = block
        pre = (dot_nn(block, down[...]) * slope[...]).astype(half)
        grad_pre[j] = pre
        give_pair(i, dot_nt(pre, up[...]))

    def weights(j):
        up_grad[...] += dot_tn(landed[0, toggle(z, j, nz)].reshape(chunk, width), grad_pre[j])
        down_grad[...] += dot_tn(gated[j], hidden[j])

    rows_pad[...] = jnp.zeros_like(rows_pad)
    rows_pad[:count] = cotangent[...]
    choice, slot = read_choices(choice_in, slot_in, turn, rows_up, taken)
    places = place_terms(choice, slot, taken, capacity, experts)
    place_any = sum(places[1:], places[0])
    dispatch(1, dot_tn(place_any, rows_pad[...]))
    rows_pad[:count] = tokens[...]
    inputs = rows_pad[...].astype(f32)
    turned = dense[:, 4 * width :].astype(f32).T
    gain_first, bias_first, gain_second, bias_second = (
        turned[experts + i : experts + i + 1] for i in range(4)
    )
    normed_first = (row_stats(inputs)[0] * gain_first + bias_first).astype(half)
    packed[...] = dot_nn(normed_first, dense[:, : 3 * width]).astype(half)

    def take_cots(start, end):
        @pl.loop(start, end)
        def _(j):
            take_plane(1, j)
            pl.when(j >= 1)(lambda: take_line(1, j - 1))

    key_live = lanes_of((1, rows_up)) < count
    lane = lanes_of((1, 128))
    sides = [((lane // 64) == i).astype(f32).astype(half) for i in range(2)]
    scale = HEAD ** (-0.5)
    for g in range(parts):
        for at in range(g * 256, g * 256 + 256, 128):
            query = packed[:, at : at + 128]
            key = packed[:, width + at : width + at + 128]
            value = packed[:, 2 * width + at : 2 * width + at + 128]
            total_mixed = 0.0
            for side in sides:
                terms = jnp.where(key_live, jnp.exp(dot_nt(query * side, key) * scale), 0.0)
                weigh = (terms * (1.0 / jnp.sum(terms, axis=-1, keepdims=True))).astype(half)
                total_mixed = total_mixed + dot_nn(weigh, value * side)
            mixed[:, at : at + 128] = total_mixed.astype(half)
        take_cots(nz * g // (parts + 1), nz * (g + 1) // (parts + 1))
    hidden_first = inputs + dot_nn(mixed[...], dense[:, 3 * width : 4 * width])
    hidden_out[...] = hidden_first
    normed_second = (row_stats(hidden_first)[0] * gain_second + bias_second).astype(half)
    dispatch(0, dot_tn(place_any, normed_second))
    take_cots(nz * parts // (parts + 1), nz)
    take_plane(0, 0)
    take_line(1, nz - 1)

    @pl.loop(0, steps)
    def _(i):
        a, j = i % 2, i // 2
        pl.when((a == 0) & (j + 1 < nz))(lambda: take_plane(0, j + 1))
        pl.when(a == 0)(lambda: take_line(0, j))
        take_pair(a, j)
        pl.when(a == 0)(lambda: forward(i, j))
        pl.when(a == 1)(lambda: backward(i, j))
        pl.when(i >= 1)(lambda: give_line(i - 1))
        pl.when(i >= 2)(lambda: give_plane(i - 2))

    up_grad[...] = jnp.zeros_like(up_grad)
    down_grad[...] = jnp.zeros_like(down_grad)

    @pl.loop(0, nz)
    def _(j):
        weights(j)

        @pl.when(j == 0)
        def _():
            give_line(steps - 1)
            give_plane(steps - 2)

        pl.when(j == 1)(lambda: give_plane(steps - 1))

    for i in range(max(steps - 3, 0), steps):
        pair_left(i)
        line_left(i)
    for a in range(2):

        @pl.loop(0, nz)
        def _(j, a=a):
            for k in range(ny):
                for kx in range(nx):
                    left(pair_sem, (a, j, k, kx), seat(a, j, k, kx, c))
                    if kx:
                        left(line_sem, (a, j, k, kx), seat(a, j, k, 0, c))

                def rest(k=k):
                    there = toggle(z, j, nz) * ny + flip(y, k)
                    arrived(home_sem, (a, j, k), backs[a].at[there])
                    left(home_sem, (a, j, k), total.at[a, j, flip(y, k)])
                    left(plane_sem, (a, j, k), sources[a].at[there])

                if k == 0:
                    pl.when(j > 0)(rest)
                else:
                    rest()


def run_forward(tokens, cotangent, choice_in, slot_in, dense, up, down, taken):
    nx = lax.axis_size("dp") // 2
    ny = nx
    nz = lax.axis_size("expert") // ny
    experts = ny * nz
    capacity = -(-taken // 16) * 16
    count, width = tokens.shape
    rows_up = -(-count // 16) * 16
    top = choice_in.shape[0]
    inner = up.shape[1]
    chunk = ny * nx * 2 * capacity
    half, f32 = jnp.bfloat16, jnp.float32
    vmem = pl.BlockSpec(memory_space=pltpu.VMEM)
    sems = [(ny,), (ny, nx), (ny, nx), (), (nx,), (ny,)]
    block = (experts, capacity, width)
    return pl.pallas_call(
        functools.partial(expert_kernel, nx, nz, experts, taken),
        out_shape=(
            jax.ShapeDtypeStruct(block, half),
            jax.ShapeDtypeStruct(block, half),
            jax.ShapeDtypeStruct(up.shape, f32),
            jax.ShapeDtypeStruct(down.shape, f32),
            jax.ShapeDtypeStruct((rows_up, 3 * width), half),
            jax.ShapeDtypeStruct((rows_up, width), half),
            jax.ShapeDtypeStruct((rows_up, width), f32),
        ),
        in_specs=[vmem] * 7,
        out_specs=(vmem,) * 7,
        scratch_shapes=[
            pltpu.VMEM((rows_up, width), half),
            pltpu.VMEM((max(8, 2 * top), -(-rows_up // 128) * 128), f32),
            pltpu.VMEM(block, half),
            pltpu.VMEM(block, half),
            pltpu.VMEM((chunk, 1), f32),
            pltpu.VMEM((2, nz, ny, nx, 2, capacity, width), half),
            pltpu.VMEM((nz, chunk, width), half),
            pltpu.VMEM((chunk, inner), f32),
            pltpu.VMEM((nz, chunk, inner), half),
            pltpu.VMEM((nz, chunk, inner), half),
            pltpu.VMEM((ny, nx, 2, capacity, width), f32),
            pltpu.VMEM((3, ny, nx, capacity, width), f32),
            pltpu.VMEM((3, ny, nx, capacity, width), half),
            pltpu.VMEM((2, nz, ny, nx, capacity, width), half),
            pltpu.VMEM((3, nx - 1, ny, capacity, width), half),
            pltpu.VMEM((2, nz, nx - 1, ny, capacity, width), half),
            pltpu.VMEM((2, nz, ny, capacity, width), half),
        ]
        + [pltpu.SemaphoreType.DMA((2, 2, nz) + shape) for shape in sems],
        compiler_params=pltpu.CompilerParams(
            collective_id=2, has_side_effects=True, vmem_limit_bytes=VMEM_LIMIT
        ),
        name="forward",
    )(tokens, cotangent, choice_in, slot_in, dense, up, down)


def backward_kernel(
    nx,
    nz,
    experts,
    capacity,
    padded,
    tokens,
    cotangent,
    choice_in,
    slot_in,
    packed,
    mixed,
    hidden_in,
    returned_in,
    grad_back,
    dense,
    block_out,
    input_out,
    main_out,
    side_out,
    extra_out,
    tokens_pad,
    cots_pad,
    turn,
    grads,
    tails,
    *boxes,
):
    place = Place()
    plane = nx * nx * nz
    count, width = tokens.shape
    rows_up = tokens_pad.shape[0]
    parts = width // 256
    half, f32 = jnp.bfloat16, jnp.float32
    pair, second, first, last, pair_t, second_t, first_t, last_t, sems = boxes
    owners = 2 * plane

    def refs(g):
        if g == parts + 1:
            return tails, pair_t, second_t, first_t, last_t
        return grads.at[g], pair.at[g], second.at[g], first.at[g], last.at[g]

    def copy_of(g, seat, source, target_ref, target):
        return pltpu.make_async_remote_copy(
            src_ref=source,
            dst_ref=target_ref,
            send_sem=sems.at[0, g, seat],
            recv_sem=sems.at[1, g, seat],
            device_id=target,
            device_id_type=MESH,
        )

    def arrived(g, seat, ref):
        copy_of(g, seat, ref, ref, place.sibling()).wait_recv()

    pairs = sorted(
        ((kf, ks) for kf in range(nx) for ks in range(nx)), key=lambda k: (k[1] == 0, k[0] == 0, k)
    )

    def at_of(kz, kf, ks):
        return ks * nx * nz + kf * nz + kz

    def scatter_pair(g):
        own, theirs = refs(g)[:2]
        for kf, ks in pairs:

            @pl.loop(0, nz)
            def _(i, kf=kf, ks=ks):
                kz = (i + 1) % nz
                index = place.owner(*spot(place, 1 - place.c, kz, kf, ks))
                at = at_of(kz, kf, ks)
                copy_of(g, at, own.at[index], theirs.at[at], place.sibling()).start()

    def gathered(g, kz, kf, ks):
        own, theirs, from_second, from_first, from_last = refs(g)
        at = at_of(kz, kf, ks)
        arrived(g, at, theirs.at[at])
        total = own[place.owner(*spot(place, place.c, kz, kf, ks))].astype(f32)
        total = total + theirs[at].astype(f32)
        if ks == 0:
            for k in range(1, nx):
                seat = at_of(kz, kf, k)
                arrived(g, plane + seat, from_second.at[seat - nx * nz])
                total = total + from_second[seat - nx * nz].astype(f32)
        if ks == 0 and kf == 0:
            for k in range(1, nx):
                seat = at_of(kz, k, 0)
                arrived(g, plane + seat, from_first.at[seat - nz])
                total = total + from_first[seat - nz].astype(f32)
        return total

    def pass_on(g, kz, kf, ks):
        own, theirs, from_second, from_first, from_last = refs(g)
        at = at_of(kz, kf, ks)
        theirs[at] = gathered(g, kz, kf, ks).astype(half)
        if ks:
            target_ref = from_second.at[at - nx * nz]
            target = spot(place, place.c, 0, 0, ks)
        elif kf:
            target_ref = from_first.at[at - nz]
            target = spot(place, place.c, 0, kf, 0)
        else:
            target_ref = from_last.at[kz - 1]
            target = spot(place, place.c, kz, 0, 0)
        copy_of(g, plane + at, theirs.at[at], target_ref, place.device(*target)).start()

    def scatter_stage(g, stage):
        if stage < 2:
            for kf, ks in pairs:
                if (ks > 0, ks == 0 and kf > 0)[stage]:

                    @pl.loop(0, nz)
                    def _(i, kf=kf, ks=ks):
                        pass_on(g, (i + 1) % nz, kf, ks)

        elif stage == 2:

            @pl.loop(1, nz)
            def _(kz):
                pass_on(g, kz, 0, 0)

        else:
            total = gathered(g, 0, 0, 0)
            from_last = refs(g)[4]
            for k in range(1, nz):
                arrived(g, plane + k, from_last.at[k - 1])
                total = total + from_last[k - 1].astype(f32)
            total = total[: side_out.shape[0]]
            if g == 0:
                side_out[...] = total
            elif g == parts + 1:
                extra_out[...] = total
            else:
                for i in range(3):
                    start = i * width + (g - 1) * 256
                    main_out[:, start : start + 256] = total[:, i * 256 : (i + 1) * 256]

    def scatter_end(g):
        own, theirs = refs(g)[:2]

        @pl.loop(0, plane)
        def _(at):
            copy_of(g, at, theirs.at[at], theirs.at[at], place.sibling()).wait_send()

            @pl.when(at > 0)
            def _():
                copy_of(g, plane + at, theirs.at[at], theirs.at[at], place.sibling()).wait_send()

    def fill(g, value, start):
        owned = owned_rows(value)
        if g == parts + 1:
            tails[...] = owned.astype(half)
        else:
            grads[g, :, :, start : start + value.shape[1]] = owned.astype(half)

    def owned_rows(value):
        rows = grads.shape[2]
        if rows * owners != width:
            shape = (rows * owners, width)
            at = lax.broadcasted_iota(jnp.int32, shape, 0)
            real = width // owners
            meant = jnp.where(at % rows < real, at // rows * real + at % rows, width)
            pick = (meant == lanes_of(shape)).astype(f32).astype(half)
            value = dot_nn(pick, value.astype(half))
        return value.reshape(owners, rows, value.shape[1])

    greet(grid_partners(place))

    for ref, source in ((tokens_pad, tokens), (cots_pad, cotangent)):
        ref[...] = jnp.zeros_like(ref)
        ref[:count] = source[...]
    choice, slot = read_choices(choice_in, slot_in, turn, rows_up, capacity)
    extra = dense[:, 4 * width :]
    turned = extra.astype(f32).T
    gain_first, bias_first, gain_second, bias_second = (
        turned[experts + i : experts + i + 1] for i in range(4)
    )
    grad_top = cots_pad[...].astype(f32)
    hidden_first = hidden_in[...]
    unit_second, inverse_second = row_stats(hidden_first)
    normed_second = (unit_second * gain_second + bias_second).astype(half)
    probs, masks, gates = router_terms(normed_second, extra, choice, experts)
    places = place_terms(choice, slot, capacity, padded, experts)
    returned = [dot_nn(one, returned_in[...]) for one in places]
    combined = sum(gate * rows for gate, rows in zip(gates, returned))
    block_out[...] = (hidden_first + combined)[:count].astype(half)
    gate_grads = [jnp.sum(grad_top * rows, axis=-1, keepdims=True) for rows in returned]
    grad_normed = dot_nn(sum(places[1:], places[0]), grad_back[...])
    grad_probs = sum(mask * grad for mask, grad in zip(masks, gate_grads))
    grad_logits = probs * (grad_probs - jnp.sum(probs * grad_probs, axis=-1, keepdims=True))
    grad_logits = grad_logits.astype(half)
    router_grad = dot_tn(normed_second, grad_logits)
    grad_normed = grad_normed + dot_nt(grad_logits, extra)
    second_sums = [
        jnp.sum(grad_normed * unit_second, axis=0, keepdims=True),
        jnp.sum(grad_normed, axis=0, keepdims=True),
    ]
    grad_hidden = grad_top + row_stats_back(grad_normed, unit_second, inverse_second, gain_second)
    grad_half = grad_hidden.astype(half)
    fill(0, dot_tn(mixed[...], grad_half), 0)
    scatter_pair(0)
    grad_mixed = dot_nt(grad_half, dense[:, 3 * width : 4 * width]).astype(half)
    unit_first, inverse_first = row_stats(tokens_pad[...].astype(f32))
    normed_first = (unit_first * gain_first + bias_first).astype(half)
    key_live = lax.broadcasted_iota(jnp.int32, (rows_up, rows_up), 0) < count
    lane = lanes_of((1, 128))
    sides = [((lane // 64) == i).astype(f32).astype(half) for i in range(2)]
    scale = HEAD ** (-0.5)
    grad_rows = jnp.zeros((rows_up, width), f32)
    for g in range(1, parts + 1):
        pieces = [[], [], []]
        for at in range((g - 1) * 256, g * 256, 128):
            query = packed[:, at : at + 128]
            key = packed[:, width + at : width + at + 128]
            value = packed[:, 2 * width + at : 2 * width + at + 128]
            grad = grad_mixed[:, at : at + 128]
            sums = [0.0, 0.0, 0.0]
            for side in sides:
                query_one, key_one, grad_one = query * side, key * side, grad * side
                terms = jnp.where(key_live, jnp.exp(dot_nt(key, query_one) * scale), 0.0)
                weights = terms * (1.0 / jnp.sum(terms, axis=0, keepdims=True))
                grad_weights = dot_nt(value, grad_one)
                delta = jnp.sum(weights * grad_weights, axis=0, keepdims=True)
                grad_scores = (weights * (grad_weights - delta) * scale).astype(half)
                sums[0] = sums[0] + dot_tn(grad_scores, key_one)
                sums[1] = sums[1] + dot_nn(grad_scores, query_one)
                sums[2] = sums[2] + dot_nn(weights.astype(half), grad_one)
            for piece, total in zip(pieces, sums):
                piece.append(total.astype(half))
        for i in range(3):
            joined = jnp.concatenate(pieces[i], axis=1)
            start = i * width + (g - 1) * 256
            grad_rows = grad_rows + dot_nt(joined, dense[:, start : start + 256])
            fill(g, dot_tn(normed_first, joined), i * 256)
        scatter_pair(g)
        for back in range(3):
            if g - 1 - back >= 0:
                scatter_stage(g - 1 - back, back)
    first_sums = [
        jnp.sum(grad_rows * unit_first, axis=0, keepdims=True),
        jnp.sum(grad_rows, axis=0, keepdims=True),
    ]
    lines = first_sums + second_sums
    line_at = lax.broadcasted_iota(jnp.int32, turned.shape, 0)
    columns = sum(jnp.where(line_at == experts + i, lines[i], 0.0) for i in range(4))
    fill(parts + 1, router_grad + columns.T, 0)
    scatter_pair(parts + 1)
    scatter_stage(parts, 0)
    grad_inputs = row_stats_back(grad_rows, unit_first, inverse_first, gain_first)
    input_out[...] = (grad_inputs + grad_hidden)[:count].astype(half)
    for g in range(parts + 1, parts + 6):
        for back in range(4):
            if g - 1 - back <= parts + 1 and (g, back) != (parts + 1, 0):
                scatter_stage(g - 1 - back, back)
    for g in range(parts + 2):
        scatter_end(g)


def run_backward(sizes, arrays, rows_owned):
    nx = lax.axis_size("dp") // 2
    nz = lax.axis_size("expert") // nx
    plane = nx * nx * nz
    tile_rows = -(-rows_owned // 8) * 8
    tokens, packed, dense = arrays[0], arrays[4], arrays[-1]
    count, width = tokens.shape
    rows_up = packed.shape[0]
    top = arrays[2].shape[0]
    parts = width // 256
    rest = dense.shape[1] - 4 * width
    half, f32 = jnp.bfloat16, jnp.float32
    vmem = pl.BlockSpec(memory_space=pltpu.VMEM)

    def boxes(lead, columns):
        return [
            pltpu.VMEM(lead + (size, tile_rows, columns), half)
            for size in (plane, plane - nx * nz, (nx - 1) * nz, nz - 1)
        ]

    return pl.pallas_call(
        functools.partial(backward_kernel, nx, nz, *sizes),
        out_shape=(
            jax.ShapeDtypeStruct((count, width), half),
            jax.ShapeDtypeStruct((count, width), half),
            jax.ShapeDtypeStruct((rows_owned, 3 * width), f32),
            jax.ShapeDtypeStruct((rows_owned, width), f32),
            jax.ShapeDtypeStruct((rows_owned, rest), f32),
        ),
        in_specs=[vmem] * len(arrays),
        out_specs=(vmem,) * 5,
        scratch_shapes=[
            pltpu.VMEM((rows_up, width), half),
            pltpu.VMEM((rows_up, width), half),
            pltpu.VMEM((max(8, 2 * top), -(-rows_up // 128) * 128), f32),
            pltpu.VMEM((parts + 1, 2 * plane, tile_rows, width), half),
            pltpu.VMEM((2 * plane, tile_rows, rest), half),
        ]
        + boxes((parts + 1,), width)
        + boxes((), rest)
        + [pltpu.SemaphoreType.DMA((2, parts + 2, 2 * plane))],
        compiler_params=pltpu.CompilerParams(
            collective_id=1, has_side_effects=True, vmem_limit_bytes=VMEM_LIMIT
        ),
        name="backward",
    )(*arrays)


def finish_kernel(experts, extra, *refs):
    sems = refs[-1]
    n = (len(refs) - 1 - 5) // 2
    sources, outs, small = refs[:n], refs[n : 2 * n], refs[2 * n : -1]
    copies = [pltpu.make_async_copy(sources[i], outs[i], sems.at[i]) for i in range(n)]
    for copy in copies:
        copy.start()
    rows = extra.shape[0]
    small[0][...] = extra[:, :experts]
    diagonal = lanes_of((rows, rows)) == lax.broadcasted_iota(jnp.int32, (rows, rows), 0)
    for i in range(4):
        column = extra[:, experts + i : experts + i + 1]
        small[1 + i][...] = jnp.sum(jnp.where(diagonal, column, 0.0), axis=0, keepdims=True)
    for copy in copies:
        copy.wait()


def finish(experts, extra, arrays):
    rows = extra.shape[0]
    f32 = jnp.float32
    somewhere, vmem = pl.BlockSpec(memory_space=pl.ANY), pl.BlockSpec(memory_space=pltpu.VMEM)
    return pl.pallas_call(
        functools.partial(finish_kernel, experts),
        out_shape=[jax.ShapeDtypeStruct(array.shape, array.dtype) for array in arrays]
        + [jax.ShapeDtypeStruct((rows, experts), f32)]
        + [jax.ShapeDtypeStruct((1, rows), f32)] * 4,
        in_specs=[vmem] + [somewhere] * len(arrays),
        out_specs=[somewhere] * len(arrays) + [vmem] * 5,
        scratch_shapes=[pltpu.SemaphoreType.DMA((len(arrays),))],
        name="finish",
    )(extra, *arrays)


def per_device(
    tokens,
    packed_weight,
    output_weight,
    router_weight,
    first_gain,
    first_bias,
    second_gain,
    second_bias,
    expert_up,
    expert_down,
    expert_choice,
    slot_index,
    cotangent,
):
    local_tokens = tokens.shape[0]
    model_width = tokens.shape[1]
    top_count = expert_choice.shape[1]
    experts = lax.axis_size("expert")
    capacity = max(15 * local_tokens * top_count // (16 * experts), 2)
    rows_owned = packed_weight.shape[0]
    padded = -(-capacity // 16) * 16
    dense = gather_dense(
        packed_weight,
        output_weight,
        router_weight,
        (first_gain, first_bias, second_gain, second_bias),
    )
    dense = dense.reshape(model_width, dense.shape[2])
    choice, slot = expert_choice.T, slot_index.T
    back_rows, back_grad, up_grad, down_grad, packed, mixed, hidden_first = run_forward(
        tokens, cotangent, choice, slot, dense, expert_up[0], expert_down[0], capacity
    )
    slots = experts * padded
    block_output, input_grad, main_grad, side_grad, extra_grad = run_backward(
        (experts, capacity, padded),
        (
            tokens,
            cotangent,
            choice,
            slot,
            packed,
            mixed,
            hidden_first,
            back_rows.reshape(slots, model_width),
            back_grad.reshape(slots, model_width),
            dense,
        ),
        rows_owned,
    )
    done = finish(
        experts, extra_grad, (block_output, input_grad, main_grad, side_grad, up_grad, down_grad)
    )
    return (
        *done[:4],
        done[6],
        *(vector.reshape(rows_owned) for vector in done[7:]),
        done[4][None],
        done[5][None],
    )


def solution(mesh):
    return jax.shard_map(
        per_device,
        mesh=mesh,
        in_specs=(
            P(("dp", "expert"), None),
            P(("dp", "expert"), None),
            P(("dp", "expert"), None),
            P(("dp", "expert"), None),
            P(("dp", "expert")),
            P(("dp", "expert")),
            P(("dp", "expert")),
            P(("dp", "expert")),
            P("expert", None, "dp"),
            P("expert", None, "dp"),
            P(("dp", "expert"), None),
            P(("dp", "expert"), None),
            P(("dp", "expert"), None),
        ),
        out_specs=(
            P(("dp", "expert"), None),
            P(("dp", "expert"), None),
            P(("dp", "expert"), None),
            P(("dp", "expert"), None),
            P(("dp", "expert"), None),
            P(("dp", "expert")),
            P(("dp", "expert")),
            P(("dp", "expert")),
            P(("dp", "expert")),
            P("expert", None, "dp"),
            P("expert", None, "dp"),
        ),
        check_vma=False,
    )
```

```python
import functools

import jax
import jax.numpy as jnp
from jax import lax
from jax.experimental import pallas as pl
from jax.experimental.pallas import tpu as pltpu
from jax.sharding import PartitionSpec as P

HEADS = 12
HEAD = 64
SEQ = 197


epsilon = 1e-06
inv_root_two = 0.7071067811865476
inv_root_two_pi = 0.3989422804014327


EXTRA = 128
MESH = pl.DeviceIdType.MESH
VMEM_LIMIT = 60 * 1024 * 1024


class Place:
    def __init__(self):
        self.nx = lax.axis_size("dp") // 2
        self.ny = self.nx
        self.nz = lax.axis_size("expert") // self.ny
        dp, expert = lax.axis_index("dp"), lax.axis_index("expert")
        self.x, self.c = dp // 2, dp % 2
        self.z, self.y = expert // self.ny, expert % self.ny

    def device(self, x, c, z, y):
        return (x * 2 + c, z * self.ny + y)

    def owner(self, x, c, z, y):
        return (x * 2 + c) * (self.nz * self.ny) + z * self.ny + y

    def sibling(self):
        return self.device(self.x, 1 - self.c, self.z, self.y)


def flip(value, k):
    bit = 1
    out = value
    while bit <= k:
        if k & bit:
            out = out + bit * (1 - 2 * ((value // bit) % 2))
        bit *= 2
    return out


def toggle(value, k, size):
    out, bit = 0, 1
    while bit < size:
        out = out + bit * ((value // bit + k // bit) % 2)
        bit *= 2
    return out


def spot(place, core, kz, kf, ks, x_first=()):
    x, y = place.x, place.y
    way = 0 if x_first and kz in x_first else core
    dx = (1 - way) * (flip(x, kf) - x) + way * (flip(x, ks) - x)
    dy = (1 - way) * (flip(y, ks) - y) + way * (flip(y, kf) - y)
    z = flip(place.z, kz) if isinstance(kz, int) else toggle(place.z, kz, place.nz)
    return (x + dx, core, z, y + dy)


def greet(devices):
    barrier = pltpu.get_barrier_semaphore()
    for device in devices:
        pl.semaphore_signal(barrier, inc=1, device_id=device, device_id_type=MESH)
    pl.semaphore_wait(barrier, len(devices))


def grid_partners(place):
    partners = [place.device(*spot(place, place.c, k, 0, 0)) for k in range(1, place.nz)]
    partners += [place.device(*spot(place, place.c, 0, k, 0)) for k in range(1, place.nx)]
    partners += [place.device(*spot(place, place.c, 0, 0, k)) for k in range(1, place.nx)]
    return partners + [place.sibling()]


def labels_of(nx, nz):
    return [(kz, kf, ks) for ks in range(nx) for kf in range(nx) for kz in range(nz)]


def row_stats(rows):
    centred = rows - jnp.mean(rows, axis=-1, keepdims=True)
    inverse = lax.rsqrt(jnp.mean(centred * centred, axis=-1, keepdims=True) + epsilon)
    return centred * inverse, inverse


def row_stats_back(grad, unit_rows, inverse, gain_row):
    grad_unit = grad * gain_row
    mean_grad = jnp.mean(grad_unit, axis=-1, keepdims=True)
    mean_dot = jnp.mean(grad_unit * unit_rows, axis=-1, keepdims=True)
    return inverse * (grad_unit - mean_grad - unit_rows * mean_dot)


def dot_nt(left, right):
    return lax.dot_general(left, right, (((1,), (1,)), ((), ())), preferred_element_type=jnp.float32)


def dot_tn(left, right):
    return lax.dot_general(left, right, (((0,), (0,)), ((), ())), preferred_element_type=jnp.float32)


def dot_nn(left, right):
    return jnp.dot(left, right, preferred_element_type=jnp.float32)


def lanes_of(shape):
    return lax.broadcasted_iota(jnp.int32, shape, len(shape) - 1)


def router_terms(normed, extra, choice, experts):
    logits = dot_nn(normed, extra)
    lane = lanes_of(logits.shape)
    terms = jnp.where(lane < experts, jnp.exp(logits), 0.0)
    probs = terms / jnp.sum(terms, axis=-1, keepdims=True)
    lane = lane.astype(jnp.float32)
    masks = [(lane == one).astype(jnp.float32) for one in choice]
    gates = [jnp.sum(mask * probs, axis=-1, keepdims=True) for mask in masks]
    return probs, masks, gates


def read_choices(choice_in, slot_in, turn, rows_up, capacity):
    top, count = choice_in.shape
    turn[...] = jnp.zeros_like(turn)
    turn[:top, :count] = choice_in[...].astype(jnp.float32)
    turn[top : 2 * top, :count] = slot_in[...].astype(jnp.float32)
    turned = turn[...].T[:rows_up]
    live = lax.broadcasted_iota(jnp.int32, (rows_up, 1), 0) < count
    choice = [turned[:, k : k + 1] for k in range(top)]
    slot = [
        jnp.where(live, turned[:, top + k : top + k + 1], float(capacity)) for k in range(top)
    ]
    return choice, slot


def place_terms(choice, slot, capacity, padded, experts):
    lane = lanes_of((choice[0].shape[0], experts * padded)).astype(jnp.float32)
    places = []
    for one, at in zip(choice, slot):
        where = jnp.where(at < capacity, one * padded + at, float(experts * padded))
        places.append((lane == where).astype(jnp.float32).astype(jnp.bfloat16))
    return places


def gather_kernel(
    nx,
    nz,
    taken,
    main,
    side,
    router,
    first,
    second,
    third,
    fourth,
    cotangent,
    choice_in,
    slot_in,
    out,
    cots_out,
    shard,
    rows_pad,
    turn,
    turn_router,
    cots,
    own_sem,
    send_sem,
    recv_sem,
    cots_sem,
    line_sem,
):
    place = Place()
    ny = nx
    x_first = (nz - 1,)
    rows, width = side.shape
    experts = router.shape[0]
    shard[:, : 3 * width] = main[...]
    shard[:, 3 * width : 4 * width] = side[...]
    lane = lanes_of((rows, EXTRA))
    diagonal = lanes_of((rows, rows)) == lax.broadcasted_iota(jnp.int32, (rows, rows), 0)
    extra = jnp.zeros((rows, EXTRA), jnp.float32)
    for i, vector in enumerate((first, second, third, fourth)):
        spread = jnp.where(diagonal, vector[...].astype(jnp.float32), 0.0)
        column = jnp.sum(spread, axis=1, keepdims=True)
        extra = jnp.where(lane == experts + i, column, extra)
    shard[:, 4 * width :] = extra.astype(shard.dtype)
    turn_router[...] = jnp.zeros_like(turn_router)
    turn_router[:experts, :rows] = router[...].astype(jnp.float32)
    turned = turn_router[...].T
    shard[:, 4 * width : 4 * width + experts] = turned[:rows, :experts].astype(shard.dtype)
    labels = labels_of(nx, nz)
    number = {}
    for label in labels:
        if label != (0, 0, 0):
            number["plane", label] = len(number)
    for label in labels:
        number["pair", label] = len(number)
    across = [
        place.device(place.x, place.c, flip(place.z, j), flip(place.y, k))
        for j in range(1, nz)
        for k in range(1, ny)
    ]
    greet(grid_partners(place) + across)
    sent = []

    def spot_at(kz, kf, ks):
        way = 0 if kz in x_first else place.c
        x, y = place.x, place.y
        dx = (1 - way) * (flip(x, kf) - x) + way * (flip(x, ks) - x)
        dy = (1 - way) * (flip(y, ks) - y) + way * (flip(y, kf) - y)
        return (x + dx, place.c, place.z, y + dy)

    def here(label):
        return place.owner(*spot(place, place.c, *label, x_first))

    def send(kind, label, origin, target):
        at = number[kind, label]
        source = shard if origin == (0, 0, 0) else out.at[here(origin)]
        copy = pltpu.make_async_remote_copy(
            src_ref=source,
            dst_ref=out.at[here(origin)],
            send_sem=send_sem.at[at],
            recv_sem=recv_sem.at[at],
            device_id=target,
            device_id_type=MESH,
        )
        copy.start()
        sent.append(copy)

    def arrived(kind, label, index):
        at = number[kind, label]
        pltpu.make_async_remote_copy(
            src_ref=out.at[index],
            dst_ref=out.at[index],
            send_sem=send_sem.at[at],
            recv_sem=recv_sem.at[at],
            device_id=place.sibling(),
            device_id_type=MESH,
        ).wait_recv()

    def spread_first(kz):
        for kf in range(1, nx):
            send("plane", (kz, kf, 0), (kz, 0, 0), place.device(*spot_at(kz, kf, 0)))

    def spread_second(kz, kf):
        for ks in range(1, nx):
            send("plane", (kz, kf, ks), (kz, kf, 0), place.device(*spot_at(kz, 0, ks)))

    def share(label):
        send("pair", label, label, place.sibling())

    spread_first(0)
    spread_second(0, 0)
    for kz in range(1, nz, 2):
        send("plane", (kz, 0, 0), (0, 0, 0), place.device(*spot(place, place.c, kz, 0, 0)))
    share((0, 0, 0))
    own = pltpu.make_async_copy(shard, out.at[here((0, 0, 0))], own_sem.at[0])
    own.start()
    me = place.z * ny + place.y
    count = cotangent.shape[0]
    rows_pad[...] = jnp.zeros_like(rows_pad)
    rows_pad[:count] = cotangent[...]
    choice, slot = read_choices(choice_in, slot_in, turn, rows_pad.shape[0], taken)
    places = place_terms(choice, slot, taken, cots.shape[1], cots.shape[0])
    value = dot_tn(sum(places[1:], places[0]), rows_pad[...])
    cots[...] = value.astype(cots.dtype).reshape(cots.shape)
    keep = pltpu.make_async_copy(cots.at[me], cots_out.at[place.x, me], own_sem.at[1])
    keep.start()

    def cots_copy(j, k):
        there = (flip(place.z, j), flip(place.y, k))
        return pltpu.make_async_remote_copy(
            src_ref=cots.at[there[0] * ny + there[1]],
            dst_ref=cots_out.at[place.x, me],
            send_sem=cots_sem.at[0, j, k],
            recv_sem=cots_sem.at[1, j, k],
            device_id=place.device(place.x, place.c, *there),
            device_id_type=MESH,
        )

    def line_copy(j, k, kx, source, ref):
        return pltpu.make_async_remote_copy(
            src_ref=source,
            dst_ref=ref,
            send_sem=line_sem.at[0, j, k, kx],
            recv_sem=line_sem.at[1, j, k, kx],
            device_id=place.device(flip(place.x, kx), place.c, place.z, place.y),
            device_id_type=MESH,
        )

    def cots_spread(j, k):
        origin = flip(place.z, j) * ny + flip(place.y, k)
        block = cots_out.at[place.x, origin]
        if (j, k) != (0, 0):
            pltpu.make_async_remote_copy(
                src_ref=block,
                dst_ref=block,
                send_sem=cots_sem.at[0, j, k],
                recv_sem=cots_sem.at[1, j, k],
                device_id=place.sibling(),
                device_id_type=MESH,
            ).wait_recv()
        for kx in range(1, nx):
            line_copy(j, k, kx, block if (j, k) != (0, 0) else cots.at[me], block).start()

    turns = [0, 1] + [kz for odd in range(nz - 1, 1, -2) for kz in (odd, odd - 1)]
    offsets = [(j, k) for j in turns for k in range(ny)]
    for i in range(1, nz + 1):
        if i < nz:
            kz = turns[i]
            arrived("plane", (kz, 0, 0), here((kz, 0, 0)))
            if kz % 2 and kz > 1:
                neighbour = place.device(*spot(place, place.c, 1, 0, 0))
                send("plane", (kz - 1, 0, 0), (kz, 0, 0), neighbour)
            spread_first(kz)
            spread_second(kz, 0)
            share((kz, 0, 0))
        for kf in range(1, nx):
            label = (turns[i - 1], kf, 0)
            arrived("plane", label, here(label))
            spread_second(turns[i - 1], kf)
            share(label)
        if i == 1:
            for j, k in offsets[1:]:
                cots_copy(j, k).start()
    for at, kz in enumerate(turns):
        for kf in range(nx):
            for ks in range(1, nx):
                arrived("plane", (kz, kf, ks), here((kz, kf, ks)))
                share((kz, kf, ks))
        if at == 1:
            for j, k in offsets[:ny]:
                cots_spread(j, k)
        if at >= 2:
            for k in range(ny):
                cots_spread(turns[at - 1], k)
    for k in range(ny):
        if nz > 1:
            cots_spread(turns[-1], k)
    for label in labels:
        arrived("pair", label, place.owner(*spot(place, 1 - place.c, *label, x_first)))
    own.wait()
    keep.wait()
    for j, k in offsets:
        origin = flip(place.z, j) * ny + flip(place.y, k)
        for kx in range(1, nx):
            block = cots_out.at[flip(place.x, kx), origin]
            line_copy(j, k, kx, block, block).wait_recv()
            line_copy(j, k, kx, block, block).wait_send()
        if (j, k) != (0, 0):
            cots_copy(j, k).wait_send()
    for copy in sent:
        copy.wait_send()


def gather_dense(main, side, router, vectors, cotangent, choice_in, slot_in, taken):
    nx = lax.axis_size("dp") // 2
    nz = lax.axis_size("expert") // nx
    devices = 2 * nx * nx * nz
    edges = devices - 1
    rows, width = side.shape
    shape = (rows, 4 * width + EXTRA)
    top, count = choice_in.shape
    rows_up = -(-count // 16) * 16
    block = (nz * nx, -(-taken // 16) * 16, width)
    vmem = pl.BlockSpec(memory_space=pltpu.VMEM)
    return pl.pallas_call(
        functools.partial(gather_kernel, nx, nz, taken),
        out_shape=(
            jax.ShapeDtypeStruct((devices,) + shape, side.dtype),
            jax.ShapeDtypeStruct((nx,) + block, side.dtype),
        ),
        in_specs=[vmem] * 10,
        out_specs=(pl.BlockSpec(memory_space=pl.ANY),) * 2,
        scratch_shapes=[
            pltpu.VMEM(shape, side.dtype),
            pltpu.VMEM((rows_up, width), side.dtype),
            pltpu.VMEM((max(8, 2 * top), -(-rows_up // 128) * 128), jnp.float32),
            pltpu.VMEM((-(-block[0] // 8) * 8, -(-rows // 128) * 128), jnp.float32),
            pltpu.VMEM(block, side.dtype),
            pltpu.SemaphoreType.DMA((2,)),
            pltpu.SemaphoreType.DMA((edges,)),
            pltpu.SemaphoreType.DMA((edges,)),
            pltpu.SemaphoreType.DMA((2, nz, nx)),
            pltpu.SemaphoreType.DMA((2, nz, nx, nx)),
        ],
        compiler_params=pltpu.CompilerParams(
            collective_id=0, has_side_effects=True, vmem_limit_bytes=VMEM_LIMIT
        ),
        name="gather_dense",
    )(main, side, router, *(vector.reshape(1, rows) for vector in vectors), cotangent, choice_in, slot_in)


def expert_kernel(
    nx,
    nz,
    experts,
    taken,
    tokens,
    cots_in,
    choice_in,
    slot_in,
    dense,
    up,
    down,
    back_out,
    back_grad,
    up_grad,
    down_grad,
    packed,
    mixed,
    hidden_out,
    rows_pad,
    turn,
    rows_in,
    gate_of,
    landed,
    slope,
    hidden,
    grad_pre,
    product,
    kept,
    pair_out,
    pair_in,
    line_out,
    line_in,
    total,
    plane_sem,
    line_sem,
    pair_sem,
    sum_sem,
    part_sem,
    home_sem,
):
    place = Place()
    ny = nx
    x, c, z, y = place.x, place.c, place.z, place.y
    me = z * ny + y
    capacity, width = rows_in.shape[1:]
    count = tokens.shape[0]
    rows_up = rows_pad.shape[0]
    parts = width // 256
    half = jnp.bfloat16
    chunk = ny * nx * 2 * capacity
    f32 = jnp.float32
    backs = (back_out, back_grad)
    steps = 2 * nz
    partners = [
        place.device(x, c, flip(z, j), flip(y, k))
        for j in range(nz)
        for k in range(ny)
        if (j, k) != (0, 0)
    ]
    partners += [place.device(flip(x, k), c, z, y) for k in range(1, nx)]
    greet(partners + [place.sibling()])

    def copy_of(sem, at, source, target_ref, target):
        return pltpu.make_async_remote_copy(
            src_ref=source,
            dst_ref=target_ref,
            send_sem=sem.at[(0,) + at],
            recv_sem=sem.at[(1,) + at],
            device_id=target,
            device_id_type=MESH,
        )

    def send(sem, at, source, target_ref, target):
        copy_of(sem, at, source, target_ref, target).start()

    def arrived(sem, at, ref):
        copy_of(sem, at, ref, ref, place.sibling()).wait_recv()

    def left(sem, at, ref):
        copy_of(sem, at, ref, ref, place.sibling()).wait_send()

    def seat(a, j, k, kx, core):
        return landed.at[a, toggle(z, j, nz), flip(y, k), flip(x, kx), core]

    def spread(a, j, k, source):
        for kx in range(1, nx):
            target = place.device(flip(x, kx), c, z, y)
            send(line_sem, (a, j, k, kx), source, seat(a, j, k, 0, c), target)
        send(pair_sem, (a, j, k, 0), source, seat(a, j, k, 0, c), place.sibling())

    def turn_of(s):
        far = jnp.where(s == 1, nz - 1, nz + 1 - s)
        return jnp.where(s == 0, 0, jnp.where(s == 2, 1, far))

    def dispatch_part(j, near):
        for k in range(ny):
            if near and k == 0:
                spread(0, 0, 0, rows_in.at[me])
            else:
                there = (toggle(z, j, nz), flip(y, k))
                send(
                    plane_sem,
                    (j, k),
                    rows_in.at[there[0] * ny + there[1]],
                    seat(0, 0, 0, 0, c),
                    place.device(x, c, *there),
                )

    def dispatch(value):
        rows_in[...] = value.astype(half).reshape(rows_in.shape)
        dispatch_part(nz - 1, False)
        dispatch_part(0, True)
        if nz > 2:
            dispatch_part(1, False)
        landed[0, z, y, x, c] = rows_in[me]

    def take_plane(s):
        j = turn_of(s)
        for k in range(ny):

            def take(k=k):
                arrived(plane_sem, (j, k), seat(0, j, k, 0, c))
                spread(0, j, k, seat(0, j, k, 0, c))

            if k == 0:
                pl.when(j > 0)(take)
            else:
                take()
        later = jnp.maximum(s + 1, 3)
        goes = (s != 0) & (s != 2) & (later < nz)
        pl.when(goes)(lambda: dispatch_part(turn_of(later), False))

    def take_line(a, s):
        j = turn_of(s)
        for k in range(ny):
            for kx in range(1, nx):
                block = seat(a, j, k, kx, c)
                arrived(line_sem, (a, j, k, kx), block)
                send(pair_sem, (a, j, k, kx), block, block, place.sibling())

    def take_pair(a, s):
        j = turn_of(s)
        for k in range(ny):
            for kx in range(nx):
                arrived(pair_sem, (a, j, k, kx), seat(a, j, k, kx, 1 - c))

    def pair_left(i):
        left(sum_sem, (i % 2, turn_of(i // 2)), pair_out.at[i % 3])

    def line_left(i):
        for kx in range(1, nx):
            left(part_sem, (i % 2, turn_of(i // 2), kx), line_out.at[i % 3, kx - 1])

    def give_pair(i, value):
        a, j = i % 2, turn_of(i // 2)
        product[...] = value.reshape(product.shape)
        kept[i % 3] = product[:, :, c]
        pl.when(i >= 3)(lambda: pair_left(i - 3))
        pair_out[i % 3] = product[:, :, 1 - c].astype(half)
        send(sum_sem, (a, j), pair_out.at[i % 3], pair_in.at[a, j], place.sibling())

    def give_line(i):
        a, j = i % 2, turn_of(i // 2)
        arrived(sum_sem, (a, j), pair_in.at[a, j])
        kept[i % 3] = kept[i % 3] + pair_in[a, j].astype(f32)
        pl.when(i >= 3)(lambda: line_left(i - 3))
        for kx in range(1, nx):
            line_out[i % 3, kx - 1] = kept[i % 3, :, flip(x, kx)].astype(half)
            send(
                part_sem,
                (a, j, kx),
                line_out.at[i % 3, kx - 1],
                line_in.at[a, j, kx - 1],
                place.device(flip(x, kx), c, z, y),
            )

    def give_plane(i):
        a, j = i % 2, turn_of(i // 2)
        value = kept[i % 3, :, x]
        for kx in range(1, nx):
            arrived(part_sem, (a, j, kx), line_in.at[a, j, kx - 1])
            value = value + line_in[a, j, kx - 1].astype(f32)
        total[a, j] = value.astype(total.dtype)
        for b in range(2):
            for k in range(ny):

                def go(b=b, k=k):
                    there = (toggle(z, j, nz), flip(y, k))
                    send(
                        home_sem,
                        (b, j, k),
                        total.at[b, j, there[1]],
                        backs[b].at[me],
                        place.device(x, c, *there),
                    )

                def stay(b=b):
                    backs[b][me] = total[b, 0, y]

                if k == 0:
                    pl.when((a == b) & (j > 0))(go)
                    pl.when((a == b) & (j == 0))(stay)
                else:
                    pl.when(a == b)(go)

    def forward(i, s):
        j = turn_of(s)
        block = landed[0, toggle(z, j, nz)].reshape(chunk, width)
        logits = dot_nn(block, dense[:, 4 * width :])
        lane = lanes_of(logits.shape)
        terms = jnp.where(lane < experts, jnp.exp(logits), 0.0)
        mine = jnp.sum(jnp.where(lane == me, terms, 0.0), axis=-1, keepdims=True)
        gate_of[...] = mine / jnp.sum(terms, axis=-1, keepdims=True)
        before = dot_nn(block, up[...])
        bell = jnp.exp(-0.5 * before * before) * inv_root_two_pi
        share = 0.5 * (1.0 + lax.erf(before * inv_root_two))
        act = (before * share).astype(half)
        slope[...] = share + before * bell
        hidden[j] = act
        give_pair(i, dot_nt(act, down[...]))

    def backward(i, s):
        j = turn_of(s)
        block = landed[1, toggle(z, j, nz)].reshape(chunk, width).astype(f32)
        block = (block * gate_of[...]).astype(half)
        landed[1, toggle(z, j, nz)] = block.reshape(landed.shape[2:])
        pre = (dot_nn(block, down[...]) * slope[...]).astype(half)
        grad_pre[j] = pre
        give_pair(i, dot_nt(pre, up[...]))

    def weights(j):
        up_grad[...] += dot_tn(landed[0, toggle(z, j, nz)].reshape(chunk, width), grad_pre[j])
        down_grad[...] += dot_tn(landed[1, toggle(z, j, nz)].reshape(chunk, width), hidden[j])

    for j in range(nz):
        for k in range(ny):
            for kx in range(nx):
                block = cots_in.at[flip(x, kx), flip(z, j) * ny + flip(y, k)]
                send(pair_sem, (1, j, k, kx), block, seat(1, j, k, kx, c), place.sibling())
                landed[1, j, k, kx, c] = cots_in[kx, j * ny + k]
    rows_pad[...] = jnp.zeros_like(rows_pad)
    choice, slot = read_choices(choice_in, slot_in, turn, rows_up, taken)
    places = place_terms(choice, slot, taken, capacity, experts)
    place_any = sum(places[1:], places[0])
    rows_pad[:count] = tokens[...]
    inputs = rows_pad[...].astype(f32)
    turned = dense[:, 4 * width :].astype(f32).T
    gain_first, bias_first, gain_second, bias_second = (
        turned[experts + i : experts + i + 1] for i in range(4)
    )
    normed_first = (row_stats(inputs)[0] * gain_first + bias_first).astype(half)
    packed[...] = dot_nn(normed_first, dense[:, : 3 * width]).astype(half)

    key_live = lanes_of((1, rows_up)) < count
    lane = lanes_of((1, 128))
    sides = [((lane // 64) == i).astype(f32).astype(half) for i in range(2)]
    scale = HEAD ** (-0.5)
    for g in range(parts):
        for at in range(g * 256, g * 256 + 256, 128):
            query = packed[:, at : at + 128]
            key = packed[:, width + at : width + at + 128]
            value = packed[:, 2 * width + at : 2 * width + at + 128]
            total_mixed = 0.0
            for side in sides:
                terms = jnp.where(key_live, jnp.exp(dot_nt(query * side, key) * scale), 0.0)
                weigh = (terms * (1.0 / jnp.sum(terms, axis=-1, keepdims=True))).astype(half)
                total_mixed = total_mixed + dot_nn(weigh, value * side)
            mixed[:, at : at + 128] = total_mixed.astype(half)
    hidden_first = inputs + dot_nn(mixed[...], dense[:, 3 * width : 4 * width])
    hidden_out[...] = hidden_first
    normed_second = (row_stats(hidden_first)[0] * gain_second + bias_second).astype(half)
    dispatch(dot_tn(place_any, normed_second))
    take_plane(0)

    @pl.loop(0, steps)
    def _(i):
        a, s = i % 2, i // 2
        pl.when(a == 0)(lambda: take_line(0, s))
        take_pair(a, s)

        @pl.when(i == 0)
        def _():
            for early in range(1, min(3, nz)):
                take_plane(early)

        pl.when((a == 1) & (s >= 1) & (s + 2 < nz))(lambda: take_plane(s + 2))
        pl.when(a == 0)(lambda: forward(i, s))
        pl.when(a == 1)(lambda: backward(i, s))
        pl.when(i >= 1)(lambda: give_line(i - 1))
        pl.when(i >= 2)(lambda: give_plane(i - 2))

    up_grad[...] = jnp.zeros_like(up_grad)
    down_grad[...] = jnp.zeros_like(down_grad)

    @pl.loop(0, nz)
    def _(j):
        weights(j)

        @pl.when(j == 0)
        def _():
            give_line(steps - 1)
            give_plane(steps - 2)

        pl.when(j == 1)(lambda: give_plane(steps - 1))

    for i in range(max(steps - 3, 0), steps):
        pair_left(i)
        line_left(i)
    for a in range(2):

        @pl.loop(0, nz)
        def _(j, a=a):
            for k in range(ny):
                for kx in range(nx):
                    left(pair_sem, (a, j, k, kx), seat(a, j, k, kx, c))
                    if kx and a == 0:
                        left(line_sem, (a, j, k, kx), seat(a, j, k, 0, c))

                def rest(k=k):
                    there = toggle(z, j, nz) * ny + flip(y, k)
                    arrived(home_sem, (a, j, k), backs[a].at[there])
                    left(home_sem, (a, j, k), total.at[a, j, flip(y, k)])
                    if a == 0:
                        left(plane_sem, (j, k), rows_in.at[there])

                if k == 0:
                    pl.when(j > 0)(rest)
                else:
                    rest()


def run_forward(tokens, cots_in, choice_in, slot_in, dense, up, down, taken):
    nx = lax.axis_size("dp") // 2
    ny = nx
    nz = lax.axis_size("expert") // ny
    experts = ny * nz
    capacity = -(-taken // 16) * 16
    count, width = tokens.shape
    rows_up = -(-count // 16) * 16
    top = choice_in.shape[0]
    inner = up.shape[1]
    chunk = ny * nx * 2 * capacity
    half, f32 = jnp.bfloat16, jnp.float32
    vmem = pl.BlockSpec(memory_space=pltpu.VMEM)
    sems = [(2, nz) + shape for shape in ((ny, nx), (ny, nx), (), (nx,), (ny,))]
    sems = [(nz, ny)] + sems
    block = (experts, capacity, width)
    return pl.pallas_call(
        functools.partial(expert_kernel, nx, nz, experts, taken),
        out_shape=(
            jax.ShapeDtypeStruct(block, half),
            jax.ShapeDtypeStruct(block, half),
            jax.ShapeDtypeStruct(up.shape, f32),
            jax.ShapeDtypeStruct(down.shape, f32),
            jax.ShapeDtypeStruct((rows_up, 3 * width), half),
            jax.ShapeDtypeStruct((rows_up, width), half),
            jax.ShapeDtypeStruct((rows_up, width), f32),
        ),
        in_specs=[vmem] * 7,
        out_specs=(vmem,) * 7,
        scratch_shapes=[
            pltpu.VMEM((rows_up, width), half),
            pltpu.VMEM((max(8, 2 * top), -(-rows_up // 128) * 128), f32),
            pltpu.VMEM(block, half),
            pltpu.VMEM((chunk, 1), f32),
            pltpu.VMEM((2, nz, ny, nx, 2, capacity, width), half),
            pltpu.VMEM((chunk, inner), f32),
            pltpu.VMEM((nz, chunk, inner), half),
            pltpu.VMEM((nz, chunk, inner), half),
            pltpu.VMEM((ny, nx, 2, capacity, width), f32),
            pltpu.VMEM((3, ny, nx, capacity, width), f32),
            pltpu.VMEM((3, ny, nx, capacity, width), half),
            pltpu.VMEM((2, nz, ny, nx, capacity, width), half),
            pltpu.VMEM((3, nx - 1, ny, capacity, width), half),
            pltpu.VMEM((2, nz, nx - 1, ny, capacity, width), half),
            pltpu.VMEM((2, nz, ny, capacity, width), half),
        ]
        + [pltpu.SemaphoreType.DMA((2,) + shape) for shape in sems],
        compiler_params=pltpu.CompilerParams(
            collective_id=2, has_side_effects=True, vmem_limit_bytes=VMEM_LIMIT
        ),
        name="forward",
    )(tokens, cots_in, choice_in, slot_in, dense, up, down)


def backward_kernel(
    nx,
    nz,
    experts,
    capacity,
    padded,
    tokens,
    cotangent,
    choice_in,
    slot_in,
    packed,
    mixed,
    hidden_in,
    returned_in,
    grad_back,
    dense,
    block_out,
    input_out,
    main_out,
    side_out,
    extra_out,
    tokens_pad,
    cots_pad,
    turn,
    grads,
    tails,
    *boxes,
):
    place = Place()
    plane = nx * nx * nz
    count, width = tokens.shape
    rows_up = tokens_pad.shape[0]
    parts = width // 256
    half, f32 = jnp.bfloat16, jnp.float32
    pair, second, first, last, pair_t, second_t, first_t, last_t, sems = boxes
    owners = 2 * plane

    def refs(g):
        if g == parts + 1:
            return tails, pair_t, second_t, first_t, last_t
        return grads.at[g], pair.at[g], second.at[g], first.at[g], last.at[g]

    def copy_of(g, seat, source, target_ref, target):
        return pltpu.make_async_remote_copy(
            src_ref=source,
            dst_ref=target_ref,
            send_sem=sems.at[0, g, seat],
            recv_sem=sems.at[1, g, seat],
            device_id=target,
            device_id_type=MESH,
        )

    def arrived(g, seat, ref):
        copy_of(g, seat, ref, ref, place.sibling()).wait_recv()

    pairs = sorted(
        ((kf, ks) for kf in range(nx) for ks in range(nx)), key=lambda k: (k[1] == 0, k[0] == 0, k)
    )

    def at_of(kz, kf, ks):
        return ks * nx * nz + kf * nz + kz

    def scatter_pair(g):
        own, theirs = refs(g)[:2]
        for kf, ks in pairs:

            @pl.loop(0, nz)
            def _(i, kf=kf, ks=ks):
                kz = (i + 1) % nz
                index = place.owner(*spot(place, 1 - place.c, kz, kf, ks))
                at = at_of(kz, kf, ks)
                copy_of(g, at, own.at[index], theirs.at[at], place.sibling()).start()

    def gathered(g, kz, kf, ks):
        own, theirs, from_second, from_first, from_last = refs(g)
        at = at_of(kz, kf, ks)
        arrived(g, at, theirs.at[at])
        total = own[place.owner(*spot(place, place.c, kz, kf, ks))].astype(f32)
        total = total + theirs[at].astype(f32)
        if ks == 0:
            for k in range(1, nx):
                seat = at_of(kz, kf, k)
                arrived(g, plane + seat, from_second.at[seat - nx * nz])
                total = total + from_second[seat - nx * nz].astype(f32)
        if ks == 0 and kf == 0:
            for k in range(1, nx):
                seat = at_of(kz, k, 0)
                arrived(g, plane + seat, from_first.at[seat - nz])
                total = total + from_first[seat - nz].astype(f32)
        return total

    def pass_on(g, kz, kf, ks):
        own, theirs, from_second, from_first, from_last = refs(g)
        at = at_of(kz, kf, ks)
        theirs[at] = gathered(g, kz, kf, ks).astype(half)
        if ks:
            target_ref = from_second.at[at - nx * nz]
            target = spot(place, place.c, 0, 0, ks)
        elif kf:
            target_ref = from_first.at[at - nz]
            target = spot(place, place.c, 0, kf, 0)
        else:
            target_ref = from_last.at[kz - 1]
            target = spot(place, place.c, kz, 0, 0)
        copy_of(g, plane + at, theirs.at[at], target_ref, place.device(*target)).start()

    def scatter_stage(g, stage):
        if stage < 2:
            for kf, ks in pairs:
                if (ks > 0, ks == 0 and kf > 0)[stage]:

                    @pl.loop(0, nz)
                    def _(i, kf=kf, ks=ks):
                        pass_on(g, (i + 1) % nz, kf, ks)

        elif stage == 2:

            @pl.loop(1, nz)
            def _(kz):
                pass_on(g, kz, 0, 0)

        else:
            total = gathered(g, 0, 0, 0)
            from_last = refs(g)[4]
            for k in range(1, nz):
                arrived(g, plane + k, from_last.at[k - 1])
                total = total + from_last[k - 1].astype(f32)
            total = total[: side_out.shape[0]]
            if g == 0:
                side_out[...] = total
            elif g == parts + 1:
                extra_out[...] = total
            else:
                for i in range(3):
                    start = i * width + (g - 1) * 256
                    main_out[:, start : start + 256] = total[:, i * 256 : (i + 1) * 256]

    def scatter_end(g):
        own, theirs = refs(g)[:2]

        @pl.loop(0, plane)
        def _(at):
            copy_of(g, at, theirs.at[at], theirs.at[at], place.sibling()).wait_send()

            @pl.when(at > 0)
            def _():
                copy_of(g, plane + at, theirs.at[at], theirs.at[at], place.sibling()).wait_send()

    def fill(g, value, start):
        owned = owned_rows(value)
        if g == parts + 1:
            tails[...] = owned.astype(half)
        else:
            grads[g, :, :, start : start + value.shape[1]] = owned.astype(half)

    def owned_rows(value):
        rows = grads.shape[2]
        if rows * owners != width:
            shape = (rows * owners, width)
            at = lax.broadcasted_iota(jnp.int32, shape, 0)
            real = width // owners
            meant = jnp.where(at % rows < real, at // rows * real + at % rows, width)
            pick = (meant == lanes_of(shape)).astype(f32).astype(half)
            value = dot_nn(pick, value.astype(half))
        return value.reshape(owners, rows, value.shape[1])

    greet(grid_partners(place))

    for ref, source in ((tokens_pad, tokens), (cots_pad, cotangent)):
        ref[...] = jnp.zeros_like(ref)
        ref[:count] = source[...]
    choice, slot = read_choices(choice_in, slot_in, turn, rows_up, capacity)
    extra = dense[:, 4 * width :]
    turned = extra.astype(f32).T
    gain_first, bias_first, gain_second, bias_second = (
        turned[experts + i : experts + i + 1] for i in range(4)
    )
    grad_top = cots_pad[...].astype(f32)
    hidden_first = hidden_in[...]
    unit_second, inverse_second = row_stats(hidden_first)
    normed_second = (unit_second * gain_second + bias_second).astype(half)
    probs, masks, gates = router_terms(normed_second, extra, choice, experts)
    places = place_terms(choice, slot, capacity, padded, experts)
    returned = [dot_nn(one, returned_in[...]) for one in places]
    combined = sum(gate * rows for gate, rows in zip(gates, returned))
    block_out[...] = (hidden_first + combined)[:count].astype(half)
    gate_grads = [jnp.sum(grad_top * rows, axis=-1, keepdims=True) for rows in returned]
    grad_normed = dot_nn(sum(places[1:], places[0]), grad_back[...])
    grad_probs = sum(mask * grad for mask, grad in zip(masks, gate_grads))
    grad_logits = probs * (grad_probs - jnp.sum(probs * grad_probs, axis=-1, keepdims=True))
    grad_logits = grad_logits.astype(half)
    router_grad = dot_tn(normed_second, grad_logits)
    grad_normed = grad_normed + dot_nt(grad_logits, extra)
    second_sums = [
        jnp.sum(grad_normed * unit_second, axis=0, keepdims=True),
        jnp.sum(grad_normed, axis=0, keepdims=True),
    ]
    grad_hidden = grad_top + row_stats_back(grad_normed, unit_second, inverse_second, gain_second)
    grad_half = grad_hidden.astype(half)
    fill(0, dot_tn(mixed[...], grad_half), 0)
    scatter_pair(0)
    grad_mixed = dot_nt(grad_half, dense[:, 3 * width : 4 * width]).astype(half)
    unit_first, inverse_first = row_stats(tokens_pad[...].astype(f32))
    normed_first = (unit_first * gain_first + bias_first).astype(half)
    key_live = lax.broadcasted_iota(jnp.int32, (rows_up, rows_up), 0) < count
    lane = lanes_of((1, 128))
    sides = [((lane // 64) == i).astype(f32).astype(half) for i in range(2)]
    scale = HEAD ** (-0.5)
    grad_rows = jnp.zeros((rows_up, width), f32)
    for g in range(1, parts + 1):
        pieces = [[], [], []]
        for at in range((g - 1) * 256, g * 256, 128):
            query = packed[:, at : at + 128]
            key = packed[:, width + at : width + at + 128]
            value = packed[:, 2 * width + at : 2 * width + at + 128]
            grad = grad_mixed[:, at : at + 128]
            sums = [0.0, 0.0, 0.0]
            for side in sides:
                query_one, key_one, grad_one = query * side, key * side, grad * side
                terms = jnp.where(key_live, jnp.exp(dot_nt(key, query_one) * scale), 0.0)
                weights = terms * (1.0 / jnp.sum(terms, axis=0, keepdims=True))
                grad_weights = dot_nt(value, grad_one)
                delta = jnp.sum(weights * grad_weights, axis=0, keepdims=True)
                grad_scores = (weights * (grad_weights - delta) * scale).astype(half)
                sums[0] = sums[0] + dot_tn(grad_scores, key_one)
                sums[1] = sums[1] + dot_nn(grad_scores, query_one)
                sums[2] = sums[2] + dot_nn(weights.astype(half), grad_one)
            for piece, total in zip(pieces, sums):
                piece.append(total.astype(half))
        for i in range(3):
            joined = jnp.concatenate(pieces[i], axis=1)
            start = i * width + (g - 1) * 256
            grad_rows = grad_rows + dot_nt(joined, dense[:, start : start + 256])
            fill(g, dot_tn(normed_first, joined), i * 256)
        scatter_pair(g)
        for back in range(3):
            if g - 1 - back >= 0:
                scatter_stage(g - 1 - back, back)
    first_sums = [
        jnp.sum(grad_rows * unit_first, axis=0, keepdims=True),
        jnp.sum(grad_rows, axis=0, keepdims=True),
    ]
    lines = first_sums + second_sums
    line_at = lax.broadcasted_iota(jnp.int32, turned.shape, 0)
    columns = sum(jnp.where(line_at == experts + i, lines[i], 0.0) for i in range(4))
    fill(parts + 1, router_grad + columns.T, 0)
    scatter_pair(parts + 1)
    scatter_stage(parts, 0)
    grad_inputs = row_stats_back(grad_rows, unit_first, inverse_first, gain_first)
    input_out[...] = (grad_inputs + grad_hidden)[:count].astype(half)
    for g in range(parts + 1, parts + 6):
        for back in range(4):
            if g - 1 - back <= parts + 1 and (g, back) != (parts + 1, 0):
                scatter_stage(g - 1 - back, back)
    for g in range(parts + 2):
        scatter_end(g)


def run_backward(sizes, arrays, rows_owned):
    nx = lax.axis_size("dp") // 2
    nz = lax.axis_size("expert") // nx
    plane = nx * nx * nz
    tile_rows = -(-rows_owned // 8) * 8
    tokens, packed, dense = arrays[0], arrays[4], arrays[-1]
    count, width = tokens.shape
    rows_up = packed.shape[0]
    top = arrays[2].shape[0]
    parts = width // 256
    rest = dense.shape[1] - 4 * width
    half, f32 = jnp.bfloat16, jnp.float32
    vmem = pl.BlockSpec(memory_space=pltpu.VMEM)

    def boxes(lead, columns):
        return [
            pltpu.VMEM(lead + (size, tile_rows, columns), half)
            for size in (plane, plane - nx * nz, (nx - 1) * nz, nz - 1)
        ]

    return pl.pallas_call(
        functools.partial(backward_kernel, nx, nz, *sizes),
        out_shape=(
            jax.ShapeDtypeStruct((count, width), half),
            jax.ShapeDtypeStruct((count, width), half),
            jax.ShapeDtypeStruct((rows_owned, 3 * width), f32),
            jax.ShapeDtypeStruct((rows_owned, width), f32),
            jax.ShapeDtypeStruct((rows_owned, rest), f32),
        ),
        in_specs=[vmem] * len(arrays),
        out_specs=(vmem,) * 5,
        scratch_shapes=[
            pltpu.VMEM((rows_up, width), half),
            pltpu.VMEM((rows_up, width), half),
            pltpu.VMEM((max(8, 2 * top), -(-rows_up // 128) * 128), f32),
            pltpu.VMEM((parts + 1, 2 * plane, tile_rows, width), half),
            pltpu.VMEM((2 * plane, tile_rows, rest), half),
        ]
        + boxes((parts + 1,), width)
        + boxes((), rest)
        + [pltpu.SemaphoreType.DMA((2, parts + 2, 2 * plane))],
        compiler_params=pltpu.CompilerParams(
            collective_id=1, has_side_effects=True, vmem_limit_bytes=VMEM_LIMIT
        ),
        name="backward",
    )(*arrays)


def finish_kernel(experts, count, extra, *refs):
    sources, outs, small = refs[:count], refs[count : 2 * count], refs[2 * count : 2 * count + 5]
    held, turn, sems = refs[2 * count + 5 : -2], refs[-2], refs[-1]
    reads = [pltpu.make_async_copy(sources[i], held[i], sems.at[0, i]) for i in range(count)]
    writes = [pltpu.make_async_copy(held[i], outs[i], sems.at[1, i]) for i in range(count)]
    for copy in reads:
        copy.start()
    rows = extra.shape[0]
    turn[...] = jnp.zeros_like(turn)
    turn[:rows] = extra[...]
    turned = turn[...].T
    small[0][...] = turned[:experts, :rows]
    for i in range(4):
        small[1 + i][...] = turned[experts + i : experts + i + 1, :rows]
    for read, write in zip(reads, writes):
        read.wait()
        write.start()
    for copy in writes:
        copy.wait()


def finish(experts, extra, arrays):
    rows = extra.shape[0]
    f32 = jnp.float32
    somewhere, vmem = pl.BlockSpec(memory_space=pl.ANY), pl.BlockSpec(memory_space=pltpu.VMEM)
    return pl.pallas_call(
        functools.partial(finish_kernel, experts, len(arrays)),
        out_shape=[jax.ShapeDtypeStruct(array.shape, array.dtype) for array in arrays]
        + [jax.ShapeDtypeStruct((experts, rows), f32)]
        + [jax.ShapeDtypeStruct((1, rows), f32)] * 4,
        in_specs=[vmem] + [somewhere] * len(arrays),
        out_specs=[somewhere] * len(arrays) + [vmem] * 5,
        scratch_shapes=[pltpu.VMEM(array.shape, array.dtype) for array in arrays]
        + [pltpu.VMEM((-(-rows // 128) * 128, extra.shape[1]), f32)]
        + [pltpu.SemaphoreType.DMA((2, len(arrays)))],
        compiler_params=pltpu.CompilerParams(vmem_limit_bytes=VMEM_LIMIT),
        name="finish",
    )(extra, *arrays)


def per_device(
    tokens,
    packed_weight,
    output_weight,
    router_weight,
    first_gain,
    first_bias,
    second_gain,
    second_bias,
    expert_up,
    expert_down,
    expert_choice,
    slot_index,
    cotangent,
):
    local_tokens = tokens.shape[0]
    model_width = tokens.shape[1]
    top_count = expert_choice.shape[1]
    experts = lax.axis_size("expert")
    capacity = max(15 * local_tokens * top_count // (16 * experts), 2)
    rows_owned = packed_weight.shape[0]
    padded = -(-capacity // 16) * 16
    choice, slot = expert_choice.T, slot_index.T
    dense, cots = gather_dense(
        packed_weight,
        output_weight,
        router_weight.T,
        (first_gain, first_bias, second_gain, second_bias),
        cotangent,
        choice,
        slot,
        capacity,
    )
    dense = dense.reshape(model_width, dense.shape[2])
    back_rows, back_grad, up_grad, down_grad, packed, mixed, hidden_first = run_forward(
        tokens, cots, choice, slot, dense, expert_up[0], expert_down[0], capacity
    )
    slots = experts * padded
    block_output, input_grad, main_grad, side_grad, extra_grad = run_backward(
        (experts, capacity, padded),
        (
            tokens,
            cotangent,
            choice,
            slot,
            packed,
            mixed,
            hidden_first,
            back_rows.reshape(slots, model_width),
            back_grad.reshape(slots, model_width),
            dense,
        ),
        rows_owned,
    )
    done = finish(
        experts, extra_grad, (block_output, input_grad, main_grad, side_grad, up_grad, down_grad)
    )
    return (
        *done[:4],
        done[6].T,
        *(vector.reshape(rows_owned) for vector in done[7:]),
        done[4][None],
        done[5][None],
    )


def solution(mesh):
    return jax.shard_map(
        per_device,
        mesh=mesh,
        in_specs=(
            P(("dp", "expert"), None),
            P(("dp", "expert"), None),
            P(("dp", "expert"), None),
            P(("dp", "expert"), None),
            P(("dp", "expert")),
            P(("dp", "expert")),
            P(("dp", "expert")),
            P(("dp", "expert")),
            P("expert", None, "dp"),
            P("expert", None, "dp"),
            P(("dp", "expert"), None),
            P(("dp", "expert"), None),
            P(("dp", "expert"), None),
        ),
        out_specs=(
            P(("dp", "expert"), None),
            P(("dp", "expert"), None),
            P(("dp", "expert"), None),
            P(("dp", "expert"), None),
            P(("dp", "expert"), None),
            P(("dp", "expert")),
            P(("dp", "expert")),
            P(("dp", "expert")),
            P(("dp", "expert")),
            P("expert", None, "dp"),
            P("expert", None, "dp"),
        ),
        check_vma=False,
    )
```

```python
import functools

import jax
import jax.numpy as jnp
from jax import lax
from jax.experimental import pallas as pl
from jax.experimental.pallas import tpu as pltpu
from jax.sharding import PartitionSpec as P

HEADS = 12
HEAD = 64
SEQ = 197


epsilon = 1e-06
inv_root_two = 0.7071067811865476
inv_root_two_pi = 0.3989422804014327


EXTRA = 128
MESH = pl.DeviceIdType.MESH
VMEM_LIMIT = 60 * 1024 * 1024


class Place:
    def __init__(self):
        self.nx = lax.axis_size("dp") // 2
        self.ny = self.nx
        self.nz = lax.axis_size("expert") // self.ny
        dp, expert = lax.axis_index("dp"), lax.axis_index("expert")
        self.x, self.c = dp // 2, dp % 2
        self.z, self.y = expert // self.ny, expert % self.ny

    def device(self, x, c, z, y):
        return (x * 2 + c, z * self.ny + y)

    def owner(self, x, c, z, y):
        return (x * 2 + c) * (self.nz * self.ny) + z * self.ny + y

    def sibling(self):
        return self.device(self.x, 1 - self.c, self.z, self.y)


def flip(value, k):
    bit = 1
    out = value
    while bit <= k:
        if k & bit:
            out = out + bit * (1 - 2 * ((value // bit) % 2))
        bit *= 2
    return out


def toggle(value, k, size):
    out, bit = 0, 1
    while bit < size:
        out = out + bit * ((value // bit + k // bit) % 2)
        bit *= 2
    return out


def spot(place, core, kz, kf, ks, x_first=()):
    x, y = place.x, place.y
    way = 0 if x_first and kz in x_first else core
    dx = (1 - way) * (flip(x, kf) - x) + way * (flip(x, ks) - x)
    dy = (1 - way) * (flip(y, ks) - y) + way * (flip(y, kf) - y)
    z = flip(place.z, kz) if isinstance(kz, int) else toggle(place.z, kz, place.nz)
    return (x + dx, core, z, y + dy)


def greet(devices):
    barrier = pltpu.get_barrier_semaphore()
    for device in devices:
        pl.semaphore_signal(barrier, inc=1, device_id=device, device_id_type=MESH)
    pl.semaphore_wait(barrier, len(devices))


def grid_partners(place):
    partners = [place.device(*spot(place, place.c, k, 0, 0)) for k in range(1, place.nz)]
    partners += [place.device(*spot(place, place.c, 0, k, 0)) for k in range(1, place.nx)]
    partners += [place.device(*spot(place, place.c, 0, 0, k)) for k in range(1, place.nx)]
    return partners + [place.sibling()]


def labels_of(nx, nz):
    return [(kz, kf, ks) for ks in range(nx) for kf in range(nx) for kz in range(nz)]


def row_stats(rows):
    centred = rows - jnp.mean(rows, axis=-1, keepdims=True)
    inverse = lax.rsqrt(jnp.mean(centred * centred, axis=-1, keepdims=True) + epsilon)
    return centred * inverse, inverse


def row_stats_back(grad, unit_rows, inverse, gain_row):
    grad_unit = grad * gain_row
    mean_grad = jnp.mean(grad_unit, axis=-1, keepdims=True)
    mean_dot = jnp.mean(grad_unit * unit_rows, axis=-1, keepdims=True)
    return inverse * (grad_unit - mean_grad - unit_rows * mean_dot)


def dot_nt(left, right):
    return lax.dot_general(left, right, (((1,), (1,)), ((), ())), preferred_element_type=jnp.float32)


def dot_tn(left, right):
    return lax.dot_general(left, right, (((0,), (0,)), ((), ())), preferred_element_type=jnp.float32)


def dot_nn(left, right):
    return jnp.dot(left, right, preferred_element_type=jnp.float32)


def lanes_of(shape):
    return lax.broadcasted_iota(jnp.int32, shape, len(shape) - 1)


def router_terms(normed, extra, choice, experts):
    logits = dot_nn(normed, extra)
    lane = lanes_of(logits.shape)
    terms = jnp.where(lane < experts, jnp.exp(logits), 0.0)
    probs = terms / jnp.sum(terms, axis=-1, keepdims=True)
    lane = lane.astype(jnp.float32)
    masks = [(lane == one).astype(jnp.float32) for one in choice]
    gates = [jnp.sum(mask * probs, axis=-1, keepdims=True) for mask in masks]
    return probs, masks, gates


def read_choices(choice_in, slot_in, turn, rows_up, capacity):
    top, count = choice_in.shape
    turn[...] = jnp.zeros_like(turn)
    turn[:top, :count] = choice_in[...].astype(jnp.float32)
    turn[top : 2 * top, :count] = slot_in[...].astype(jnp.float32)
    turned = turn[...].T[:rows_up]
    live = lax.broadcasted_iota(jnp.int32, (rows_up, 1), 0) < count
    choice = [turned[:, k : k + 1] for k in range(top)]
    slot = [
        jnp.where(live, turned[:, top + k : top + k + 1], float(capacity)) for k in range(top)
    ]
    return choice, slot


def place_terms(choice, slot, capacity, padded, experts):
    lane = lanes_of((choice[0].shape[0], experts * padded)).astype(jnp.float32)
    places = []
    for one, at in zip(choice, slot):
        where = jnp.where(at < capacity, one * padded + at, float(experts * padded))
        places.append((lane == where).astype(jnp.float32).astype(jnp.bfloat16))
    return places


def early_of(nz):
    return max(nz // 2, 1)


def gather_kernel(
    nx,
    nz,
    taken,
    main,
    side,
    router,
    first,
    second,
    third,
    fourth,
    cotangent,
    choice_in,
    slot_in,
    out,
    cots_out,
    shard,
    rows_pad,
    turn,
    turn_router,
    cots,
    own_sem,
    send_sem,
    recv_sem,
    cots_sem,
    line_sem,
):
    place = Place()
    ny = nx
    x_first = (nz - 1,)
    early = early_of(nz)
    rows, width = side.shape
    experts = router.shape[0]
    shard[:, : 3 * width] = main[...]
    shard[:, 3 * width : 4 * width] = side[...]
    lane = lanes_of((rows, EXTRA))
    diagonal = lanes_of((rows, rows)) == lax.broadcasted_iota(jnp.int32, (rows, rows), 0)
    extra = jnp.zeros((rows, EXTRA), jnp.float32)
    for i, vector in enumerate((first, second, third, fourth)):
        spread = jnp.where(diagonal, vector[...].astype(jnp.float32), 0.0)
        column = jnp.sum(spread, axis=1, keepdims=True)
        extra = jnp.where(lane == experts + i, column, extra)
    shard[:, 4 * width :] = extra.astype(shard.dtype)
    turn_router[...] = jnp.zeros_like(turn_router)
    turn_router[:experts, :rows] = router[...].astype(jnp.float32)
    turned = turn_router[...].T
    shard[:, 4 * width : 4 * width + experts] = turned[:rows, :experts].astype(shard.dtype)
    labels = labels_of(nx, nz)
    number = {}
    for label in labels:
        if label != (0, 0, 0):
            number["plane", label] = len(number)
    for label in labels:
        number["pair", label] = len(number)
    across = [
        place.device(place.x, place.c, flip(place.z, j), flip(place.y, k))
        for j in range(1, nz)
        for k in range(1, ny)
    ]
    greet(grid_partners(place) + across)
    sent = []

    def spot_at(kz, kf, ks):
        way = 0 if kz in x_first else place.c
        x, y = place.x, place.y
        dx = (1 - way) * (flip(x, kf) - x) + way * (flip(x, ks) - x)
        dy = (1 - way) * (flip(y, ks) - y) + way * (flip(y, kf) - y)
        return (x + dx, place.c, place.z, y + dy)

    def here(label):
        return place.owner(*spot(place, place.c, *label, x_first))

    def send(kind, label, origin, target):
        at = number[kind, label]
        source = shard if origin == (0, 0, 0) else out.at[here(origin)]
        copy = pltpu.make_async_remote_copy(
            src_ref=source,
            dst_ref=out.at[here(origin)],
            send_sem=send_sem.at[at],
            recv_sem=recv_sem.at[at],
            device_id=target,
            device_id_type=MESH,
        )
        copy.start()
        sent.append(copy)

    def arrived(kind, label, index):
        at = number[kind, label]
        pltpu.make_async_remote_copy(
            src_ref=out.at[index],
            dst_ref=out.at[index],
            send_sem=send_sem.at[at],
            recv_sem=recv_sem.at[at],
            device_id=place.sibling(),
            device_id_type=MESH,
        ).wait_recv()

    def spread_first(kz):
        for kf in range(1, nx):
            send("plane", (kz, kf, 0), (kz, 0, 0), place.device(*spot_at(kz, kf, 0)))

    def spread_second(kz, kf):
        for ks in range(1, nx):
            send("plane", (kz, kf, ks), (kz, kf, 0), place.device(*spot_at(kz, 0, ks)))

    def share(label):
        send("pair", label, label, place.sibling())

    spread_first(0)
    spread_second(0, 0)
    for kz in range(1, nz, 2):
        send("plane", (kz, 0, 0), (0, 0, 0), place.device(*spot(place, place.c, kz, 0, 0)))
    share((0, 0, 0))
    own = pltpu.make_async_copy(shard, out.at[here((0, 0, 0))], own_sem.at[0])
    own.start()
    me = place.z * ny + place.y
    count = cotangent.shape[0]
    rows_pad[...] = jnp.zeros_like(rows_pad)
    rows_pad[:count] = cotangent[...]
    choice, slot = read_choices(choice_in, slot_in, turn, rows_pad.shape[0], taken)
    places = place_terms(choice, slot, taken, cots.shape[1], cots.shape[0])
    value = dot_tn(sum(places[1:], places[0]), rows_pad[...])
    cots[...] = value.astype(cots.dtype).reshape(cots.shape)
    keep = pltpu.make_async_copy(cots.at[me], cots_out.at[place.x, me], own_sem.at[1])
    keep.start()

    def cots_copy(j, k):
        there = (flip(place.z, j), flip(place.y, k))
        return pltpu.make_async_remote_copy(
            src_ref=cots.at[there[0] * ny + there[1]],
            dst_ref=cots_out.at[place.x, me],
            send_sem=cots_sem.at[0, j, k],
            recv_sem=cots_sem.at[1, j, k],
            device_id=place.device(place.x, place.c, *there),
            device_id_type=MESH,
        )

    def line_copy(j, k, kx, source, ref):
        return pltpu.make_async_remote_copy(
            src_ref=source,
            dst_ref=ref,
            send_sem=line_sem.at[0, j, k, kx],
            recv_sem=line_sem.at[1, j, k, kx],
            device_id=place.device(flip(place.x, kx), place.c, place.z, place.y),
            device_id_type=MESH,
        )

    def cots_spread(j, k):
        origin = flip(place.z, j) * ny + flip(place.y, k)
        block = cots_out.at[place.x, origin]
        if (j, k) != (0, 0):
            pltpu.make_async_remote_copy(
                src_ref=block,
                dst_ref=block,
                send_sem=cots_sem.at[0, j, k],
                recv_sem=cots_sem.at[1, j, k],
                device_id=place.sibling(),
                device_id_type=MESH,
            ).wait_recv()
        if j < early:
            for kx in range(1, nx):
                line_copy(j, k, kx, block if (j, k) != (0, 0) else cots.at[me], block).start()

    turns = [0, 1] + [kz for odd in range(nz - 1, 1, -2) for kz in (odd, odd - 1)]
    offsets = [(j, k) for j in turns for k in range(ny)]
    for i in range(1, nz + 1):
        if i < nz:
            kz = turns[i]
            arrived("plane", (kz, 0, 0), here((kz, 0, 0)))
            if kz % 2 and kz > 1:
                neighbour = place.device(*spot(place, place.c, 1, 0, 0))
                send("plane", (kz - 1, 0, 0), (kz, 0, 0), neighbour)
            spread_first(kz)
            spread_second(kz, 0)
            share((kz, 0, 0))
        for kf in range(1, nx):
            label = (turns[i - 1], kf, 0)
            arrived("plane", label, here(label))
            spread_second(turns[i - 1], kf)
            share(label)
        if i == 1:
            for j, k in offsets[1:]:
                cots_copy(j, k).start()
    for at, kz in enumerate(turns):
        for kf in range(nx):
            for ks in range(1, nx):
                arrived("plane", (kz, kf, ks), here((kz, kf, ks)))
                share((kz, kf, ks))
        if at == 1:
            for j, k in offsets[:ny]:
                cots_spread(j, k)
        if at >= 2:
            for k in range(ny):
                cots_spread(turns[at - 1], k)
    for k in range(ny):
        if nz > 1:
            cots_spread(turns[-1], k)
    for label in labels:
        arrived("pair", label, place.owner(*spot(place, 1 - place.c, *label, x_first)))
    own.wait()
    keep.wait()
    for j, k in offsets:
        origin = flip(place.z, j) * ny + flip(place.y, k)
        for kx in range(1, nx if j < early else 1):
            block = cots_out.at[flip(place.x, kx), origin]
            line_copy(j, k, kx, block, block).wait_recv()
            line_copy(j, k, kx, block, block).wait_send()
        if (j, k) != (0, 0):
            cots_copy(j, k).wait_send()
    for copy in sent:
        copy.wait_send()


def gather_dense(main, side, router, vectors, cotangent, choice_in, slot_in, taken):
    nx = lax.axis_size("dp") // 2
    nz = lax.axis_size("expert") // nx
    devices = 2 * nx * nx * nz
    edges = devices - 1
    rows, width = side.shape
    shape = (rows, 4 * width + EXTRA)
    top, count = choice_in.shape
    rows_up = -(-count // 16) * 16
    block = (nz * nx, -(-taken // 16) * 16, width)
    vmem = pl.BlockSpec(memory_space=pltpu.VMEM)
    return pl.pallas_call(
        functools.partial(gather_kernel, nx, nz, taken),
        out_shape=(
            jax.ShapeDtypeStruct((devices,) + shape, side.dtype),
            jax.ShapeDtypeStruct((nx,) + block, side.dtype),
        ),
        in_specs=[vmem] * 10,
        out_specs=(pl.BlockSpec(memory_space=pl.ANY),) * 2,
        scratch_shapes=[
            pltpu.VMEM(shape, side.dtype),
            pltpu.VMEM((rows_up, width), side.dtype),
            pltpu.VMEM((max(8, 2 * top), -(-rows_up // 128) * 128), jnp.float32),
            pltpu.VMEM((-(-block[0] // 8) * 8, -(-rows // 128) * 128), jnp.float32),
            pltpu.VMEM(block, side.dtype),
            pltpu.SemaphoreType.DMA((2,)),
            pltpu.SemaphoreType.DMA((edges,)),
            pltpu.SemaphoreType.DMA((edges,)),
            pltpu.SemaphoreType.DMA((2, nz, nx)),
            pltpu.SemaphoreType.DMA((2, nz, nx, nx)),
        ],
        compiler_params=pltpu.CompilerParams(
            collective_id=0, has_side_effects=True, vmem_limit_bytes=VMEM_LIMIT
        ),
        name="gather_dense",
    )(main, side, router, *(vector.reshape(1, rows) for vector in vectors), cotangent, choice_in, slot_in)


def expert_kernel(
    nx,
    nz,
    experts,
    taken,
    tokens,
    cots_in,
    choice_in,
    slot_in,
    dense,
    up,
    down,
    back_out,
    back_grad,
    up_grad,
    down_grad,
    packed,
    mixed,
    hidden_out,
    rows_pad,
    turn,
    rows_in,
    gate_of,
    landed,
    slope,
    hidden,
    grad_pre,
    product,
    kept,
    pair_out,
    pair_in,
    line_out,
    line_in,
    total,
    plane_sem,
    line_sem,
    pair_sem,
    sum_sem,
    part_sem,
    home_sem,
):
    place = Place()
    ny = nx
    x, c, z, y = place.x, place.c, place.z, place.y
    me = z * ny + y
    capacity, width = rows_in.shape[1:]
    count = tokens.shape[0]
    rows_up = rows_pad.shape[0]
    parts = width // 256
    half = jnp.bfloat16
    chunk = ny * nx * 2 * capacity
    inner = up.shape[1]
    f32 = jnp.float32
    backs = (back_out, back_grad)
    steps = 2 * nz
    early = early_of(nz)
    partners = [
        place.device(x, c, flip(z, j), flip(y, k))
        for j in range(nz)
        for k in range(ny)
        if (j, k) != (0, 0)
    ]
    partners += [place.device(flip(x, k), c, z, y) for k in range(1, nx)]
    greet(partners + [place.sibling()])

    def copy_of(sem, at, source, target_ref, target):
        return pltpu.make_async_remote_copy(
            src_ref=source,
            dst_ref=target_ref,
            send_sem=sem.at[(0,) + at],
            recv_sem=sem.at[(1,) + at],
            device_id=target,
            device_id_type=MESH,
        )

    def send(sem, at, source, target_ref, target):
        copy_of(sem, at, source, target_ref, target).start()

    def arrived(sem, at, ref):
        copy_of(sem, at, ref, ref, place.sibling()).wait_recv()

    def left(sem, at, ref):
        copy_of(sem, at, ref, ref, place.sibling()).wait_send()

    def seat(a, j, k, kx, core):
        return landed.at[a, toggle(z, j, nz), flip(y, k), flip(x, kx), core]

    def spread(a, j, k, source):
        for kx in range(1, nx):
            target = place.device(flip(x, kx), c, z, y)
            send(line_sem, (a, j, k, kx), source, seat(a, j, k, 0, c), target)
        send(pair_sem, (a, j, k, 0), source, seat(a, j, k, 0, c), place.sibling())

    def turn_of(s):
        far = jnp.where(s == 1, nz - 1, nz + 1 - s)
        return jnp.where(s == 0, 0, jnp.where(s == 2, 1, far))

    def dispatch_part(j, near):
        for k in range(ny):
            if near and k == 0:
                spread(0, 0, 0, rows_in.at[me])
            else:
                there = (toggle(z, j, nz), flip(y, k))
                send(
                    plane_sem,
                    (j, k),
                    rows_in.at[there[0] * ny + there[1]],
                    seat(0, 0, 0, 0, c),
                    place.device(x, c, *there),
                )

    def dispatch(value):
        rows_in[...] = value.astype(half).reshape(rows_in.shape)
        dispatch_part(nz - 1, False)
        dispatch_part(0, True)
        if nz > 2:
            dispatch_part(1, False)
        landed[0, z, y, x, c] = rows_in[me]

    def take_plane(s):
        j = turn_of(s)
        for k in range(ny):

            def take(k=k):
                arrived(plane_sem, (j, k), seat(0, j, k, 0, c))
                spread(0, j, k, seat(0, j, k, 0, c))

            if k == 0:
                pl.when(j > 0)(take)
            else:
                take()
        later = jnp.maximum(s + 1, 3)
        goes = (s != 0) & (s != 2) & (later < nz)
        pl.when(goes)(lambda: dispatch_part(turn_of(later), False))

    def take_line(a, j):
        for k in range(ny):
            for kx in range(1, nx):
                block = seat(a, j, k, kx, c)
                arrived(line_sem, (a, j, k, kx), block)
                send(pair_sem, (a, j, k, kx), block, block, place.sibling())

    def pair_gone(j, k, kx):
        return lambda: left(pair_sem, (1, j, k, kx), seat(1, j, k, kx, c))

    def line_gone(j, k, kx):
        return lambda: left(line_sem, (1, j, k, kx), seat(1, j, k, 0, c))

    def take_pair(a, s):
        j = turn_of(s)
        for k in range(ny):
            for kx in range(nx):
                arrived(pair_sem, (a, j, k, kx), seat(a, j, k, kx, 1 - c))

    def pair_left(i):
        left(sum_sem, (i % 2, turn_of(i // 2)), pair_out.at[i % 3])

    def line_left(i):
        for kx in range(1, nx):
            left(part_sem, (i % 2, turn_of(i // 2), kx), line_out.at[i % 3, kx - 1])

    def give_pair(i, held, weight):
        a, j = i % 2, turn_of(i // 2)
        product[...] = dot_nt(held[j].reshape(chunk, inner), weight[...]).reshape(product.shape)
        pl.when(i >= 3)(lambda: pair_left(i - 3))
        pair_out[i % 3] = product[:, :, 1 - c].astype(half)
        send(sum_sem, (a, j), pair_out.at[i % 3], pair_in.at[a, j], place.sibling())
        kept[i % 3] = product[:, :, c]

    def give_line(i):
        a, j = i % 2, turn_of(i // 2)
        arrived(sum_sem, (a, j), pair_in.at[a, j])
        kept[i % 3] = kept[i % 3] + pair_in[a, j].astype(f32)
        pl.when(i >= 3)(lambda: line_left(i - 3))
        for kx in range(1, nx):
            line_out[i % 3, kx - 1] = kept[i % 3, :, flip(x, kx)].astype(half)
            send(
                part_sem,
                (a, j, kx),
                line_out.at[i % 3, kx - 1],
                line_in.at[a, j, kx - 1],
                place.device(flip(x, kx), c, z, y),
            )

    def give_plane(i):
        a, j = i % 2, turn_of(i // 2)
        value = kept[i % 3, :, x]
        for kx in range(1, nx):
            arrived(part_sem, (a, j, kx), line_in.at[a, j, kx - 1])
            value = value + line_in[a, j, kx - 1].astype(f32)
        total[a, j] = value.astype(total.dtype)
        for b in range(2):
            for k in range(ny):

                def go(b=b, k=k):
                    there = (toggle(z, j, nz), flip(y, k))
                    send(
                        home_sem,
                        (b, j, k),
                        total.at[b, j, there[1]],
                        backs[b].at[me],
                        place.device(x, c, *there),
                    )

                def stay(b=b):
                    backs[b][me] = total[b, 0, y]

                if k == 0:
                    pl.when((a == b) & (j > 0))(go)
                    pl.when((a == b) & (j == 0))(stay)
                else:
                    pl.when(a == b)(go)

    def forward(i, s):
        j = turn_of(s)
        block = landed[0, toggle(z, j, nz)].reshape(chunk, width)
        logits = dot_nn(block, dense[:, 4 * width :])
        lane = lanes_of(logits.shape)
        terms = jnp.where(lane < experts, jnp.exp(logits), 0.0)
        mine = jnp.sum(jnp.where(lane == me, terms, 0.0), axis=-1, keepdims=True)
        gate_of[...] = mine / jnp.sum(terms, axis=-1, keepdims=True)
        before = dot_nn(block, up[...])
        bell = jnp.exp(-0.5 * before * before) * inv_root_two_pi
        share = 0.5 * (1.0 + lax.erf(before * inv_root_two))
        act = (before * share).astype(half)
        slope[...] = share + before * bell
        hidden[j] = act.reshape(hidden.shape[1:])
        give_pair(i, hidden, down)

    def backward(i, s):
        j = turn_of(s)
        for k in range(ny):
            for kx in range(1, nx):
                pl.when(j >= early)(pair_gone(j, k, kx))
        block = landed[1, toggle(z, j, nz)].reshape(chunk, width).astype(f32)
        block = (block * gate_of[...]).astype(half)
        landed[1, toggle(z, j, nz)] = block.reshape(landed.shape[2:])
        pre = (dot_nn(block, down[...]) * slope[...]).astype(half)
        grad_pre[j] = pre.reshape(grad_pre.shape[1:])
        give_pair(i, grad_pre, up)

    def weights(j):
        up_grad[...] += dot_tn(landed[0, toggle(z, j, nz)].reshape(chunk, width), grad_pre[j].reshape(chunk, inner))
        down_grad[...] += dot_tn(landed[1, toggle(z, j, nz)].reshape(chunk, width), hidden[j].reshape(chunk, inner))

    for j in range(nz):
        for k in range(ny):
            for kx in range(nx if j < early else 1):
                spots = (flip(z, j), flip(y, k), flip(x, kx))
                at = (spots[2], spots[0] * ny + spots[1])
                if j < early:
                    to = seat(1, j, k, kx, c)
                    send(pair_sem, (1, j, k, kx), cots_in.at[at], to, place.sibling())
                else:
                    spread(1, j, k, cots_in.at[at])
                landed[(1,) + spots + (c,)] = cots_in[at]
    rows_pad[...] = jnp.zeros_like(rows_pad)
    choice, slot = read_choices(choice_in, slot_in, turn, rows_up, taken)
    places = place_terms(choice, slot, taken, capacity, experts)
    place_any = sum(places[1:], places[0])
    rows_pad[:count] = tokens[...]
    inputs = rows_pad[...].astype(f32)
    turned = dense[:, 4 * width :].astype(f32).T
    gain_first, bias_first, gain_second, bias_second = (
        turned[experts + i : experts + i + 1] for i in range(4)
    )
    normed_first = (row_stats(inputs)[0] * gain_first + bias_first).astype(half)
    packed[...] = dot_nn(normed_first, dense[:, : 3 * width]).astype(half)

    key_live = lanes_of((1, rows_up)) < count
    lane = lanes_of((1, 128))
    sides = [((lane // 64) == i).astype(f32).astype(half) for i in range(2)]
    scale = HEAD ** (-0.5)
    for g in range(parts):
        for at in range(g * 256, g * 256 + 256, 128):
            query = packed[:, at : at + 128]
            key = packed[:, width + at : width + at + 128]
            value = packed[:, 2 * width + at : 2 * width + at + 128]
            total_mixed = 0.0
            for side in sides:
                terms = jnp.where(key_live, jnp.exp(dot_nt(query * side, key) * scale), 0.0)
                weigh = (terms * (1.0 / jnp.sum(terms, axis=-1, keepdims=True))).astype(half)
                total_mixed = total_mixed + dot_nn(weigh, value * side)
            mixed[:, at : at + 128] = total_mixed.astype(half)
    hidden_first = inputs + dot_nn(mixed[...], dense[:, 3 * width : 4 * width])
    hidden_out[...] = hidden_first
    normed_second = (row_stats(hidden_first)[0] * gain_second + bias_second).astype(half)
    dispatch(dot_tn(place_any, normed_second))
    for j in range(early, nz):
        take_line(1, j)
    take_plane(0)

    @pl.loop(0, steps)
    def _(i):
        a, s = i % 2, i // 2
        pl.when(a == 0)(lambda: take_line(0, turn_of(s)))
        take_pair(a, s)

        @pl.when(i == 0)
        def _():
            for early in range(1, min(3, nz)):
                take_plane(early)

        pl.when((a == 1) & (s >= 1) & (s + 2 < nz))(lambda: take_plane(s + 2))
        pl.when(a == 0)(lambda: forward(i, s))
        pl.when(a == 1)(lambda: backward(i, s))
        pl.when(i >= 1)(lambda: give_line(i - 1))
        pl.when(i >= 2)(lambda: give_plane(i - 2))

    up_grad[...] = jnp.zeros_like(up_grad)
    down_grad[...] = jnp.zeros_like(down_grad)

    @pl.loop(0, nz)
    def _(j):
        weights(j)

        @pl.when(j == 0)
        def _():
            give_line(steps - 1)
            give_plane(steps - 2)

        pl.when(j == 1)(lambda: give_plane(steps - 1))

    for i in range(max(steps - 3, 0), steps):
        pair_left(i)
        line_left(i)
    for a in range(2):

        @pl.loop(0, nz)
        def _(j, a=a):
            for k in range(ny):
                for kx in range(nx):
                    if kx and a == 1:
                        pl.when(j < early)(pair_gone(j, k, kx))
                    else:
                        left(pair_sem, (a, j, k, kx), seat(a, j, k, kx, c))
                    if kx and a == 0:
                        left(line_sem, (a, j, k, kx), seat(a, j, k, 0, c))
                    if kx and a == 1:
                        pl.when(j >= early)(line_gone(j, k, kx))

                def rest(k=k):
                    there = toggle(z, j, nz) * ny + flip(y, k)
                    arrived(home_sem, (a, j, k), backs[a].at[there])
                    left(home_sem, (a, j, k), total.at[a, j, flip(y, k)])
                    if a == 0:
                        left(plane_sem, (j, k), rows_in.at[there])

                if k == 0:
                    pl.when(j > 0)(rest)
                else:
                    rest()


def run_forward(tokens, cots_in, choice_in, slot_in, dense, up, down, taken):
    nx = lax.axis_size("dp") // 2
    ny = nx
    nz = lax.axis_size("expert") // ny
    experts = ny * nz
    capacity = -(-taken // 16) * 16
    count, width = tokens.shape
    rows_up = -(-count // 16) * 16
    top = choice_in.shape[0]
    inner = up.shape[1]
    chunk = ny * nx * 2 * capacity
    half, f32 = jnp.bfloat16, jnp.float32
    vmem = pl.BlockSpec(memory_space=pltpu.VMEM)
    sems = [(2, nz) + shape for shape in ((ny, nx), (ny, nx), (), (nx,), (ny,))]
    sems = [(nz, ny)] + sems
    block = (experts, capacity, width)
    return pl.pallas_call(
        functools.partial(expert_kernel, nx, nz, experts, taken),
        out_shape=(
            jax.ShapeDtypeStruct(block, half),
            jax.ShapeDtypeStruct(block, half),
            jax.ShapeDtypeStruct(up.shape, f32),
            jax.ShapeDtypeStruct(down.shape, f32),
            jax.ShapeDtypeStruct((rows_up, 3 * width), half),
            jax.ShapeDtypeStruct((rows_up, width), half),
            jax.ShapeDtypeStruct((rows_up, width), f32),
        ),
        in_specs=[vmem] * 7,
        out_specs=(vmem,) * 7,
        scratch_shapes=[
            pltpu.VMEM((rows_up, width), half),
            pltpu.VMEM((max(8, 2 * top), -(-rows_up // 128) * 128), f32),
            pltpu.VMEM(block, half),
            pltpu.VMEM((chunk, 1), f32),
            pltpu.VMEM((2, nz, ny, nx, 2, capacity, width), half),
            pltpu.VMEM((chunk, inner), f32),
            pltpu.VMEM((nz, ny, nx, 2, capacity, inner), half),
            pltpu.VMEM((nz, ny, nx, 2, capacity, inner), half),
            pltpu.VMEM((ny, nx, 2, capacity, width), f32),
            pltpu.VMEM((3, ny, nx, capacity, width), f32),
            pltpu.VMEM((3, ny, nx, capacity, width), half),
            pltpu.VMEM((2, nz, ny, nx, capacity, width), half),
            pltpu.VMEM((3, nx - 1, ny, capacity, width), half),
            pltpu.VMEM((2, nz, nx - 1, ny, capacity, width), half),
            pltpu.VMEM((2, nz, ny, capacity, width), half),
        ]
        + [pltpu.SemaphoreType.DMA((2,) + shape) for shape in sems],
        compiler_params=pltpu.CompilerParams(
            collective_id=2, has_side_effects=True, vmem_limit_bytes=VMEM_LIMIT
        ),
        name="forward",
    )(tokens, cots_in, choice_in, slot_in, dense, up, down)


def backward_kernel(
    nx,
    nz,
    experts,
    capacity,
    padded,
    tokens,
    cotangent,
    choice_in,
    slot_in,
    packed,
    mixed,
    hidden_in,
    returned_in,
    grad_back,
    dense,
    block_out,
    input_out,
    main_out,
    side_out,
    extra_out,
    tokens_pad,
    cots_pad,
    turn,
    grads,
    tails,
    *boxes,
):
    place = Place()
    plane = nx * nx * nz
    count, width = tokens.shape
    rows_up = tokens_pad.shape[0]
    parts = width // 256
    half, f32 = jnp.bfloat16, jnp.float32
    pair, second, first, last, pair_t, second_t, first_t, last_t, sems = boxes
    owners = 2 * plane

    def refs(g):
        if g == parts + 1:
            return tails, pair_t, second_t, first_t, last_t
        return grads.at[g], pair.at[g], second.at[g], first.at[g], last.at[g]

    def copy_of(g, seat, source, target_ref, target):
        return pltpu.make_async_remote_copy(
            src_ref=source,
            dst_ref=target_ref,
            send_sem=sems.at[0, g, seat],
            recv_sem=sems.at[1, g, seat],
            device_id=target,
            device_id_type=MESH,
        )

    def arrived(g, seat, ref):
        copy_of(g, seat, ref, ref, place.sibling()).wait_recv()

    pairs = sorted(
        ((kf, ks) for kf in range(nx) for ks in range(nx)), key=lambda k: (k[1] == 0, k[0] == 0, k)
    )

    def at_of(kz, kf, ks):
        return ks * nx * nz + kf * nz + kz

    def scatter_pair(g):
        own, theirs = refs(g)[:2]
        for kf, ks in pairs:

            @pl.loop(0, nz)
            def _(i, kf=kf, ks=ks):
                kz = (i + 1) % nz
                index = place.owner(*spot(place, 1 - place.c, kz, kf, ks))
                at = at_of(kz, kf, ks)
                copy_of(g, at, own.at[index], theirs.at[at], place.sibling()).start()

    def gathered(g, kz, kf, ks):
        own, theirs, from_second, from_first, from_last = refs(g)
        at = at_of(kz, kf, ks)
        arrived(g, at, theirs.at[at])
        total = own[place.owner(*spot(place, place.c, kz, kf, ks))].astype(f32)
        total = total + theirs[at].astype(f32)
        if ks == 0:
            for k in range(1, nx):
                seat = at_of(kz, kf, k)
                arrived(g, plane + seat, from_second.at[seat - nx * nz])
                total = total + from_second[seat - nx * nz].astype(f32)
        if ks == 0 and kf == 0:
            for k in range(1, nx):
                seat = at_of(kz, k, 0)
                arrived(g, plane + seat, from_first.at[seat - nz])
                total = total + from_first[seat - nz].astype(f32)
        return total

    def pass_on(g, kz, kf, ks):
        own, theirs, from_second, from_first, from_last = refs(g)
        at = at_of(kz, kf, ks)
        theirs[at] = gathered(g, kz, kf, ks).astype(half)
        if ks:
            target_ref = from_second.at[at - nx * nz]
            target = spot(place, place.c, 0, 0, ks)
        elif kf:
            target_ref = from_first.at[at - nz]
            target = spot(place, place.c, 0, kf, 0)
        else:
            target_ref = from_last.at[kz - 1]
            target = spot(place, place.c, kz, 0, 0)
        copy_of(g, plane + at, theirs.at[at], target_ref, place.device(*target)).start()

    def scatter_stage(g, stage):
        if stage < 2:
            for kf, ks in pairs:
                if (ks > 0, ks == 0 and kf > 0)[stage]:

                    @pl.loop(0, nz)
                    def _(i, kf=kf, ks=ks):
                        pass_on(g, (i + 1) % nz, kf, ks)

        elif stage == 2:

            @pl.loop(1, nz)
            def _(kz):
                pass_on(g, kz, 0, 0)

        else:
            total = gathered(g, 0, 0, 0)
            from_last = refs(g)[4]
            for k in range(1, nz):
                arrived(g, plane + k, from_last.at[k - 1])
                total = total + from_last[k - 1].astype(f32)
            total = total[: side_out.shape[0]]
            if g == 0:
                side_out[...] = total
            elif g == parts + 1:
                extra_out[...] = total
            else:
                for i in range(3):
                    start = i * width + (g - 1) * 256
                    main_out[:, start : start + 256] = total[:, i * 256 : (i + 1) * 256]

    def scatter_end(g):
        own, theirs = refs(g)[:2]

        @pl.loop(0, plane)
        def _(at):
            copy_of(g, at, theirs.at[at], theirs.at[at], place.sibling()).wait_send()

            @pl.when(at > 0)
            def _():
                copy_of(g, plane + at, theirs.at[at], theirs.at[at], place.sibling()).wait_send()

    def fill(g, value, start):
        owned = owned_rows(value)
        if g == parts + 1:
            tails[...] = owned.astype(half)
        else:
            grads[g, :, :, start : start + value.shape[1]] = owned.astype(half)

    def owned_rows(value):
        rows = grads.shape[2]
        if rows * owners != width:
            shape = (rows * owners, width)
            at = lax.broadcasted_iota(jnp.int32, shape, 0)
            real = width // owners
            meant = jnp.where(at % rows < real, at // rows * real + at % rows, width)
            pick = (meant == lanes_of(shape)).astype(f32).astype(half)
            value = dot_nn(pick, value.astype(half))
        return value.reshape(owners, rows, value.shape[1])

    greet(grid_partners(place))

    for ref, source in ((tokens_pad, tokens), (cots_pad, cotangent)):
        ref[...] = jnp.zeros_like(ref)
        ref[:count] = source[...]
    choice, slot = read_choices(choice_in, slot_in, turn, rows_up, capacity)
    extra = dense[:, 4 * width :]
    turned = extra.astype(f32).T
    gain_first, bias_first, gain_second, bias_second = (
        turned[experts + i : experts + i + 1] for i in range(4)
    )
    grad_top = cots_pad[...].astype(f32)
    hidden_first = hidden_in[...]
    unit_second, inverse_second = row_stats(hidden_first)
    normed_second = (unit_second * gain_second + bias_second).astype(half)
    probs, masks, gates = router_terms(normed_second, extra, choice, experts)
    places = place_terms(choice, slot, capacity, padded, experts)
    returned = [dot_nn(one, returned_in[...]) for one in places]
    combined = sum(gate * rows for gate, rows in zip(gates, returned))
    block_out[...] = (hidden_first + combined)[:count].astype(half)
    gate_grads = [jnp.sum(grad_top * rows, axis=-1, keepdims=True) for rows in returned]
    grad_normed = dot_nn(sum(places[1:], places[0]), grad_back[...])
    grad_probs = sum(mask * grad for mask, grad in zip(masks, gate_grads))
    grad_logits = probs * (grad_probs - jnp.sum(probs * grad_probs, axis=-1, keepdims=True))
    grad_logits = grad_logits.astype(half)
    router_grad = dot_tn(normed_second, grad_logits)
    grad_normed = grad_normed + dot_nt(grad_logits, extra)
    second_sums = [
        jnp.sum(grad_normed * unit_second, axis=0, keepdims=True),
        jnp.sum(grad_normed, axis=0, keepdims=True),
    ]
    grad_hidden = grad_top + row_stats_back(grad_normed, unit_second, inverse_second, gain_second)
    grad_half = grad_hidden.astype(half)
    fill(0, dot_tn(mixed[...], grad_half), 0)
    scatter_pair(0)
    grad_mixed = dot_nt(grad_half, dense[:, 3 * width : 4 * width]).astype(half)
    unit_first, inverse_first = row_stats(tokens_pad[...].astype(f32))
    normed_first = (unit_first * gain_first + bias_first).astype(half)
    key_live = lax.broadcasted_iota(jnp.int32, (rows_up, rows_up), 0) < count
    lane = lanes_of((1, 128))
    sides = [((lane // 64) == i).astype(f32).astype(half) for i in range(2)]
    scale = HEAD ** (-0.5)
    grad_rows = jnp.zeros((rows_up, width), f32)
    for g in range(1, parts + 1):
        pieces = [[], [], []]
        for at in range((g - 1) * 256, g * 256, 128):
            query = packed[:, at : at + 128]
            key = packed[:, width + at : width + at + 128]
            value = packed[:, 2 * width + at : 2 * width + at + 128]
            grad = grad_mixed[:, at : at + 128]
            sums = [0.0, 0.0, 0.0]
            for side in sides:
                query_one, key_one, grad_one = query * side, key * side, grad * side
                terms = jnp.where(key_live, jnp.exp(dot_nt(key, query_one) * scale), 0.0)
                weights = terms * (1.0 / jnp.sum(terms, axis=0, keepdims=True))
                grad_weights = dot_nt(value, grad_one)
                delta = jnp.sum(weights * grad_weights, axis=0, keepdims=True)
                grad_scores = (weights * (grad_weights - delta) * scale).astype(half)
                sums[0] = sums[0] + dot_tn(grad_scores, key_one)
                sums[1] = sums[1] + dot_nn(grad_scores, query_one)
                sums[2] = sums[2] + dot_nn(weights.astype(half), grad_one)
            for piece, total in zip(pieces, sums):
                piece.append(total.astype(half))
        for i in range(3):
            joined = jnp.concatenate(pieces[i], axis=1)
            start = i * width + (g - 1) * 256
            grad_rows = grad_rows + dot_nt(joined, dense[:, start : start + 256])
            fill(g, dot_tn(normed_first, joined), i * 256)
        scatter_pair(g)
        for back in range(3):
            if g - 1 - back >= 0:
                scatter_stage(g - 1 - back, back)
    first_sums = [
        jnp.sum(grad_rows * unit_first, axis=0, keepdims=True),
        jnp.sum(grad_rows, axis=0, keepdims=True),
    ]
    lines = first_sums + second_sums
    line_at = lax.broadcasted_iota(jnp.int32, turned.shape, 0)
    columns = sum(jnp.where(line_at == experts + i, lines[i], 0.0) for i in range(4))
    fill(parts + 1, router_grad + columns.T, 0)
    scatter_pair(parts + 1)
    scatter_stage(parts, 0)
    grad_inputs = row_stats_back(grad_rows, unit_first, inverse_first, gain_first)
    input_out[...] = (grad_inputs + grad_hidden)[:count].astype(half)
    for g in range(parts + 1, parts + 6):
        for back in range(4):
            if g - 1 - back <= parts + 1 and (g, back) != (parts + 1, 0):
                scatter_stage(g - 1 - back, back)
    for g in range(parts + 2):
        scatter_end(g)


def run_backward(sizes, arrays, rows_owned):
    nx = lax.axis_size("dp") // 2
    nz = lax.axis_size("expert") // nx
    plane = nx * nx * nz
    tile_rows = -(-rows_owned // 8) * 8
    tokens, packed, dense = arrays[0], arrays[4], arrays[-1]
    count, width = tokens.shape
    rows_up = packed.shape[0]
    top = arrays[2].shape[0]
    parts = width // 256
    rest = dense.shape[1] - 4 * width
    half, f32 = jnp.bfloat16, jnp.float32
    vmem = pl.BlockSpec(memory_space=pltpu.VMEM)

    def boxes(lead, columns):
        return [
            pltpu.VMEM(lead + (size, tile_rows, columns), half)
            for size in (plane, plane - nx * nz, (nx - 1) * nz, nz - 1)
        ]

    return pl.pallas_call(
        functools.partial(backward_kernel, nx, nz, *sizes),
        out_shape=(
            jax.ShapeDtypeStruct((count, width), half),
            jax.ShapeDtypeStruct((count, width), half),
            jax.ShapeDtypeStruct((rows_owned, 3 * width), f32),
            jax.ShapeDtypeStruct((rows_owned, width), f32),
            jax.ShapeDtypeStruct((rows_owned, rest), f32),
        ),
        in_specs=[vmem] * len(arrays),
        out_specs=(vmem,) * 5,
        scratch_shapes=[
            pltpu.VMEM((rows_up, width), half),
            pltpu.VMEM((rows_up, width), half),
            pltpu.VMEM((max(8, 2 * top), -(-rows_up // 128) * 128), f32),
            pltpu.VMEM((parts + 1, 2 * plane, tile_rows, width), half),
            pltpu.VMEM((2 * plane, tile_rows, rest), half),
        ]
        + boxes((parts + 1,), width)
        + boxes((), rest)
        + [pltpu.SemaphoreType.DMA((2, parts + 2, 2 * plane))],
        compiler_params=pltpu.CompilerParams(
            collective_id=1, has_side_effects=True, vmem_limit_bytes=VMEM_LIMIT
        ),
        name="backward",
    )(*arrays)


def finish_kernel(experts, count, extra, *refs):
    sources, outs, small = refs[:count], refs[count : 2 * count], refs[2 * count : 2 * count + 5]
    held, turn, sems = refs[2 * count + 5 : -2], refs[-2], refs[-1]
    reads = [pltpu.make_async_copy(sources[i], held[i], sems.at[0, i]) for i in range(count)]
    writes = [pltpu.make_async_copy(held[i], outs[i], sems.at[1, i]) for i in range(count)]
    for copy in reads:
        copy.start()
    rows = extra.shape[0]
    turn[...] = jnp.zeros_like(turn)
    turn[:rows] = extra[...]
    turned = turn[...].T
    small[0][...] = turned[:experts, :rows]
    for i in range(4):
        small[1 + i][...] = turned[experts + i : experts + i + 1, :rows]
    for read, write in zip(reads, writes):
        read.wait()
        write.start()
    for copy in writes:
        copy.wait()


def finish(experts, extra, arrays):
    rows = extra.shape[0]
    f32 = jnp.float32
    somewhere, vmem = pl.BlockSpec(memory_space=pl.ANY), pl.BlockSpec(memory_space=pltpu.VMEM)
    return pl.pallas_call(
        functools.partial(finish_kernel, experts, len(arrays)),
        out_shape=[jax.ShapeDtypeStruct(array.shape, array.dtype) for array in arrays]
        + [jax.ShapeDtypeStruct((experts, rows), f32)]
        + [jax.ShapeDtypeStruct((1, rows), f32)] * 4,
        in_specs=[vmem] + [somewhere] * len(arrays),
        out_specs=[somewhere] * len(arrays) + [vmem] * 5,
        scratch_shapes=[pltpu.VMEM(array.shape, array.dtype) for array in arrays]
        + [pltpu.VMEM((-(-rows // 128) * 128, extra.shape[1]), f32)]
        + [pltpu.SemaphoreType.DMA((2, len(arrays)))],
        compiler_params=pltpu.CompilerParams(vmem_limit_bytes=VMEM_LIMIT),
        name="finish",
    )(extra, *arrays)


def per_device(
    tokens,
    packed_weight,
    output_weight,
    router_weight,
    first_gain,
    first_bias,
    second_gain,
    second_bias,
    expert_up,
    expert_down,
    expert_choice,
    slot_index,
    cotangent,
):
    local_tokens = tokens.shape[0]
    model_width = tokens.shape[1]
    top_count = expert_choice.shape[1]
    experts = lax.axis_size("expert")
    capacity = max(15 * local_tokens * top_count // (16 * experts), 2)
    rows_owned = packed_weight.shape[0]
    padded = -(-capacity // 16) * 16
    choice, slot = expert_choice.T, slot_index.T
    dense, cots = gather_dense(
        packed_weight,
        output_weight,
        router_weight.T,
        (first_gain, first_bias, second_gain, second_bias),
        cotangent,
        choice,
        slot,
        capacity,
    )
    dense = dense.reshape(model_width, dense.shape[2])
    back_rows, back_grad, up_grad, down_grad, packed, mixed, hidden_first = run_forward(
        tokens, cots, choice, slot, dense, expert_up[0], expert_down[0], capacity
    )
    slots = experts * padded
    block_output, input_grad, main_grad, side_grad, extra_grad = run_backward(
        (experts, capacity, padded),
        (
            tokens,
            cotangent,
            choice,
            slot,
            packed,
            mixed,
            hidden_first,
            back_rows.reshape(slots, model_width),
            back_grad.reshape(slots, model_width),
            dense,
        ),
        rows_owned,
    )
    done = finish(
        experts, extra_grad, (block_output, input_grad, main_grad, side_grad, up_grad, down_grad)
    )
    return (
        *done[:4],
        done[6].T,
        *(vector.reshape(rows_owned) for vector in done[7:]),
        done[4][None],
        done[5][None],
    )


def solution(mesh):
    return jax.shard_map(
        per_device,
        mesh=mesh,
        in_specs=(
            P(("dp", "expert"), None),
            P(("dp", "expert"), None),
            P(("dp", "expert"), None),
            P(("dp", "expert"), None),
            P(("dp", "expert")),
            P(("dp", "expert")),
            P(("dp", "expert")),
            P(("dp", "expert")),
            P("expert", None, "dp"),
            P("expert", None, "dp"),
            P(("dp", "expert"), None),
            P(("dp", "expert"), None),
            P(("dp", "expert"), None),
        ),
        out_specs=(
            P(("dp", "expert"), None),
            P(("dp", "expert"), None),
            P(("dp", "expert"), None),
            P(("dp", "expert"), None),
            P(("dp", "expert"), None),
            P(("dp", "expert")),
            P(("dp", "expert")),
            P(("dp", "expert")),
            P(("dp", "expert")),
            P("expert", None, "dp"),
            P("expert", None, "dp"),
        ),
        check_vma=False,
    )
```

```python
import functools

import jax
import jax.numpy as jnp
from jax import lax
from jax.experimental import pallas as pl
from jax.experimental.pallas import tpu as pltpu
from jax.sharding import PartitionSpec as P

HEADS = 12
HEAD = 64
SEQ = 197


epsilon = 1e-06
inv_root_two = 0.7071067811865476
inv_root_two_pi = 0.3989422804014327


EXTRA = 128
MESH = pl.DeviceIdType.MESH
VMEM_LIMIT = 60 * 1024 * 1024


class Place:
    def __init__(self):
        self.nx = lax.axis_size("dp") // 2
        self.ny = self.nx
        self.nz = lax.axis_size("expert") // self.ny
        dp, expert = lax.axis_index("dp"), lax.axis_index("expert")
        self.x, self.c = dp // 2, dp % 2
        self.z, self.y = expert // self.ny, expert % self.ny

    def device(self, x, c, z, y):
        return (x * 2 + c, z * self.ny + y)

    def owner(self, x, c, z, y):
        return (x * 2 + c) * (self.nz * self.ny) + z * self.ny + y

    def sibling(self):
        return self.device(self.x, 1 - self.c, self.z, self.y)


def flip(value, k):
    bit = 1
    out = value
    while bit <= k:
        if k & bit:
            out = out + bit * (1 - 2 * ((value // bit) % 2))
        bit *= 2
    return out


def toggle(value, k, size):
    out, bit = 0, 1
    while bit < size:
        out = out + bit * ((value // bit + k // bit) % 2)
        bit *= 2
    return out


def spot(place, core, kz, kf, ks, x_first=()):
    x, y = place.x, place.y
    way = 0 if x_first and kz in x_first else core
    dx = (1 - way) * (flip(x, kf) - x) + way * (flip(x, ks) - x)
    dy = (1 - way) * (flip(y, ks) - y) + way * (flip(y, kf) - y)
    z = flip(place.z, kz) if isinstance(kz, int) else toggle(place.z, kz, place.nz)
    return (x + dx, core, z, y + dy)


def greet(devices):
    barrier = pltpu.get_barrier_semaphore()
    for device in devices:
        pl.semaphore_signal(barrier, inc=1, device_id=device, device_id_type=MESH)
    pl.semaphore_wait(barrier, len(devices))


def grid_partners(place):
    partners = [place.device(*spot(place, place.c, k, 0, 0)) for k in range(1, place.nz)]
    partners += [place.device(*spot(place, place.c, 0, k, 0)) for k in range(1, place.nx)]
    partners += [place.device(*spot(place, place.c, 0, 0, k)) for k in range(1, place.nx)]
    return partners + [place.sibling()]


def labels_of(nx, nz):
    return [(kz, kf, ks) for ks in range(nx) for kf in range(nx) for kz in range(nz)]


def row_stats(rows):
    centred = rows - jnp.mean(rows, axis=-1, keepdims=True)
    inverse = lax.rsqrt(jnp.mean(centred * centred, axis=-1, keepdims=True) + epsilon)
    return centred * inverse, inverse


def row_stats_back(grad, unit_rows, inverse, gain_row):
    grad_unit = grad * gain_row
    mean_grad = jnp.mean(grad_unit, axis=-1, keepdims=True)
    mean_dot = jnp.mean(grad_unit * unit_rows, axis=-1, keepdims=True)
    return inverse * (grad_unit - mean_grad - unit_rows * mean_dot)


def dot_nt(left, right):
    return lax.dot_general(left, right, (((1,), (1,)), ((), ())), preferred_element_type=jnp.float32)


def dot_tn(left, right):
    return lax.dot_general(left, right, (((0,), (0,)), ((), ())), preferred_element_type=jnp.float32)


def dot_nn(left, right):
    return jnp.dot(left, right, preferred_element_type=jnp.float32)


def lanes_of(shape):
    return lax.broadcasted_iota(jnp.int32, shape, len(shape) - 1)


def router_terms(normed, extra, choice, experts):
    logits = dot_nn(normed, extra)
    lane = lanes_of(logits.shape)
    terms = jnp.where(lane < experts, jnp.exp(logits), 0.0)
    probs = terms / jnp.sum(terms, axis=-1, keepdims=True)
    lane = lane.astype(jnp.float32)
    masks = [(lane == one).astype(jnp.float32) for one in choice]
    gates = [jnp.sum(mask * probs, axis=-1, keepdims=True) for mask in masks]
    return probs, masks, gates


def read_choices(choice_in, slot_in, turn, rows_up, capacity):
    top, count = choice_in.shape
    turn[...] = jnp.zeros_like(turn)
    turn[:top, :count] = choice_in[...].astype(jnp.float32)
    turn[top : 2 * top, :count] = slot_in[...].astype(jnp.float32)
    turned = turn[...].T[:rows_up]
    live = lax.broadcasted_iota(jnp.int32, (rows_up, 1), 0) < count
    choice = [turned[:, k : k + 1] for k in range(top)]
    slot = [
        jnp.where(live, turned[:, top + k : top + k + 1], float(capacity)) for k in range(top)
    ]
    return choice, slot


def place_terms(choice, slot, capacity, padded, experts):
    lane = lanes_of((choice[0].shape[0], experts * padded)).astype(jnp.float32)
    places = []
    for one, at in zip(choice, slot):
        where = jnp.where(at < capacity, one * padded + at, float(experts * padded))
        places.append((lane == where).astype(jnp.float32).astype(jnp.bfloat16))
    return places


def early_of(nz):
    return max(nz // 2, 1)


def gather_kernel(
    nx,
    nz,
    taken,
    main,
    side,
    router,
    first,
    second,
    third,
    fourth,
    cotangent,
    choice_in,
    slot_in,
    out,
    cots_out,
    shard,
    rows_pad,
    turn,
    turn_router,
    cots,
    own_sem,
    send_sem,
    recv_sem,
    cots_sem,
    line_sem,
):
    place = Place()
    ny = nx
    x_first = (nz - 1,)
    early = early_of(nz)
    rows, width = side.shape
    experts = router.shape[0]
    shard[:, : 3 * width] = main[...]
    shard[:, 3 * width : 4 * width] = side[...]
    lane = lanes_of((rows, EXTRA))
    diagonal = lanes_of((rows, rows)) == lax.broadcasted_iota(jnp.int32, (rows, rows), 0)
    extra = jnp.zeros((rows, EXTRA), jnp.float32)
    for i, vector in enumerate((first, second, third, fourth)):
        spread = jnp.where(diagonal, vector[...].astype(jnp.float32), 0.0)
        column = jnp.sum(spread, axis=1, keepdims=True)
        extra = jnp.where(lane == experts + i, column, extra)
    shard[:, 4 * width :] = extra.astype(shard.dtype)
    turn_router[...] = jnp.zeros_like(turn_router)
    turn_router[:experts, :rows] = router[...].astype(jnp.float32)
    turned = turn_router[...].T
    shard[:, 4 * width : 4 * width + experts] = turned[:rows, :experts].astype(shard.dtype)
    labels = labels_of(nx, nz)
    number = {}
    for label in labels:
        if label != (0, 0, 0):
            number["plane", label] = len(number)
    for label in labels:
        number["pair", label] = len(number)
    across = [
        place.device(place.x, place.c, flip(place.z, j), flip(place.y, k))
        for j in range(1, nz)
        for k in range(1, ny)
    ]
    greet(grid_partners(place) + across)
    sent = []

    def spot_at(kz, kf, ks):
        way = 0 if kz in x_first else place.c
        x, y = place.x, place.y
        dx = (1 - way) * (flip(x, kf) - x) + way * (flip(x, ks) - x)
        dy = (1 - way) * (flip(y, ks) - y) + way * (flip(y, kf) - y)
        return (x + dx, place.c, place.z, y + dy)

    def here(label):
        return place.owner(*spot(place, place.c, *label, x_first))

    def send(kind, label, origin, target):
        at = number[kind, label]
        source = shard if origin == (0, 0, 0) else out.at[here(origin)]
        copy = pltpu.make_async_remote_copy(
            src_ref=source,
            dst_ref=out.at[here(origin)],
            send_sem=send_sem.at[at],
            recv_sem=recv_sem.at[at],
            device_id=target,
            device_id_type=MESH,
        )
        copy.start()
        sent.append(copy)

    def arrived(kind, label, index):
        at = number[kind, label]
        pltpu.make_async_remote_copy(
            src_ref=out.at[index],
            dst_ref=out.at[index],
            send_sem=send_sem.at[at],
            recv_sem=recv_sem.at[at],
            device_id=place.sibling(),
            device_id_type=MESH,
        ).wait_recv()

    def spread_first(kz):
        for kf in range(1, nx):
            send("plane", (kz, kf, 0), (kz, 0, 0), place.device(*spot_at(kz, kf, 0)))

    def spread_second(kz, kf):
        for ks in range(1, nx):
            send("plane", (kz, kf, ks), (kz, kf, 0), place.device(*spot_at(kz, 0, ks)))

    def share(label):
        send("pair", label, label, place.sibling())

    spread_first(0)
    spread_second(0, 0)
    for kz in range(1, nz, 2):
        send("plane", (kz, 0, 0), (0, 0, 0), place.device(*spot(place, place.c, kz, 0, 0)))
    share((0, 0, 0))
    own = pltpu.make_async_copy(shard, out.at[here((0, 0, 0))], own_sem.at[0])
    own.start()
    me = place.z * ny + place.y
    count = cotangent.shape[0]
    rows_pad[...] = jnp.zeros_like(rows_pad)
    rows_pad[:count] = cotangent[...]
    choice, slot = read_choices(choice_in, slot_in, turn, rows_pad.shape[0], taken)
    places = place_terms(choice, slot, taken, cots.shape[1], cots.shape[0])
    value = dot_tn(sum(places[1:], places[0]), rows_pad[...])
    cots[...] = value.astype(cots.dtype).reshape(cots.shape)
    keep = pltpu.make_async_copy(cots.at[me], cots_out.at[place.x, me], own_sem.at[1])
    keep.start()

    def cots_copy(j, k):
        there = (flip(place.z, j), flip(place.y, k))
        return pltpu.make_async_remote_copy(
            src_ref=cots.at[there[0] * ny + there[1]],
            dst_ref=cots_out.at[place.x, me],
            send_sem=cots_sem.at[0, j, k],
            recv_sem=cots_sem.at[1, j, k],
            device_id=place.device(place.x, place.c, *there),
            device_id_type=MESH,
        )

    def line_copy(j, k, kx, source, ref):
        return pltpu.make_async_remote_copy(
            src_ref=source,
            dst_ref=ref,
            send_sem=line_sem.at[0, j, k, kx],
            recv_sem=line_sem.at[1, j, k, kx],
            device_id=place.device(flip(place.x, kx), place.c, place.z, place.y),
            device_id_type=MESH,
        )

    def cots_spread(j, k):
        origin = flip(place.z, j) * ny + flip(place.y, k)
        block = cots_out.at[place.x, origin]
        if (j, k) != (0, 0):
            pltpu.make_async_remote_copy(
                src_ref=block,
                dst_ref=block,
                send_sem=cots_sem.at[0, j, k],
                recv_sem=cots_sem.at[1, j, k],
                device_id=place.sibling(),
                device_id_type=MESH,
            ).wait_recv()
        if j < early:
            for kx in range(1, nx):
                line_copy(j, k, kx, block if (j, k) != (0, 0) else cots.at[me], block).start()

    turns = [0, 1] + [kz for odd in range(nz - 1, 1, -2) for kz in (odd, odd - 1)]
    offsets = [(j, k) for j in turns for k in range(ny)]
    for i in range(1, nz + 1):
        if i < nz:
            kz = turns[i]
            arrived("plane", (kz, 0, 0), here((kz, 0, 0)))
            if kz % 2 and kz > 1:
                neighbour = place.device(*spot(place, place.c, 1, 0, 0))
                send("plane", (kz - 1, 0, 0), (kz, 0, 0), neighbour)
            spread_first(kz)
            spread_second(kz, 0)
            share((kz, 0, 0))
        for kf in range(1, nx):
            label = (turns[i - 1], kf, 0)
            arrived("plane", label, here(label))
            spread_second(turns[i - 1], kf)
            share(label)
        if i == 1:
            for j, k in offsets[1:]:
                cots_copy(j, k).start()
    for at, kz in enumerate(turns):
        for kf in range(nx):
            for ks in range(1, nx):
                arrived("plane", (kz, kf, ks), here((kz, kf, ks)))
                share((kz, kf, ks))
        if at == 1:
            for j, k in offsets[:ny]:
                cots_spread(j, k)
        if at >= 2:
            for k in range(ny):
                cots_spread(turns[at - 1], k)
    for k in range(ny):
        if nz > 1:
            cots_spread(turns[-1], k)
    for label in labels:
        arrived("pair", label, place.owner(*spot(place, 1 - place.c, *label, x_first)))
    own.wait()
    keep.wait()
    for j, k in offsets:
        origin = flip(place.z, j) * ny + flip(place.y, k)
        for kx in range(1, nx if j < early else 1):
            block = cots_out.at[flip(place.x, kx), origin]
            line_copy(j, k, kx, block, block).wait_recv()
            line_copy(j, k, kx, block, block).wait_send()
        if (j, k) != (0, 0):
            cots_copy(j, k).wait_send()
    for copy in sent:
        copy.wait_send()


def gather_dense(main, side, router, vectors, cotangent, choice_in, slot_in, taken):
    nx = lax.axis_size("dp") // 2
    nz = lax.axis_size("expert") // nx
    devices = 2 * nx * nx * nz
    edges = devices - 1
    rows, width = side.shape
    shape = (rows, 4 * width + EXTRA)
    top, count = choice_in.shape
    rows_up = -(-count // 16) * 16
    block = (nz * nx, -(-taken // 16) * 16, width)
    vmem = pl.BlockSpec(memory_space=pltpu.VMEM)
    return pl.pallas_call(
        functools.partial(gather_kernel, nx, nz, taken),
        out_shape=(
            jax.ShapeDtypeStruct((devices,) + shape, side.dtype),
            jax.ShapeDtypeStruct((nx,) + block, side.dtype),
        ),
        in_specs=[vmem] * 10,
        out_specs=(pl.BlockSpec(memory_space=pl.ANY),) * 2,
        scratch_shapes=[
            pltpu.VMEM(shape, side.dtype),
            pltpu.VMEM((rows_up, width), side.dtype),
            pltpu.VMEM((max(8, 2 * top), -(-rows_up // 128) * 128), jnp.float32),
            pltpu.VMEM((-(-block[0] // 8) * 8, -(-rows // 128) * 128), jnp.float32),
            pltpu.VMEM(block, side.dtype),
            pltpu.SemaphoreType.DMA((2,)),
            pltpu.SemaphoreType.DMA((edges,)),
            pltpu.SemaphoreType.DMA((edges,)),
            pltpu.SemaphoreType.DMA((2, nz, nx)),
            pltpu.SemaphoreType.DMA((2, nz, nx, nx)),
        ],
        compiler_params=pltpu.CompilerParams(
            collective_id=0, has_side_effects=True, vmem_limit_bytes=VMEM_LIMIT
        ),
        name="gather_dense",
    )(main, side, router, *(vector.reshape(1, rows) for vector in vectors), cotangent, choice_in, slot_in)


def expert_kernel(
    nx,
    nz,
    experts,
    taken,
    tokens,
    cots_in,
    choice_in,
    slot_in,
    dense,
    up,
    down,
    back_out,
    back_grad,
    up_grad,
    down_grad,
    packed,
    mixed,
    hidden_out,
    rows_pad,
    turn,
    rows_in,
    gate_of,
    landed,
    slope,
    hidden,
    grad_pre,
    product,
    kept,
    pair_out,
    pair_in,
    line_out,
    line_in,
    total,
    plane_sem,
    line_sem,
    pair_sem,
    sum_sem,
    part_sem,
    home_sem,
):
    place = Place()
    ny = nx
    x, c, z, y = place.x, place.c, place.z, place.y
    me = z * ny + y
    capacity, width = rows_in.shape[1:]
    count = tokens.shape[0]
    rows_up = rows_pad.shape[0]
    parts = width // 256
    half = jnp.bfloat16
    chunk = ny * nx * 2 * capacity
    inner = up.shape[1]
    f32 = jnp.float32
    backs = (back_out, back_grad)
    steps = 2 * nz
    early = early_of(nz)
    partners = [
        place.device(x, c, flip(z, j), flip(y, k))
        for j in range(nz)
        for k in range(ny)
        if (j, k) != (0, 0)
    ]
    partners += [place.device(flip(x, k), c, z, y) for k in range(1, nx)]
    greet(partners + [place.sibling()])

    def copy_of(sem, at, source, target_ref, target):
        return pltpu.make_async_remote_copy(
            src_ref=source,
            dst_ref=target_ref,
            send_sem=sem.at[(0,) + at],
            recv_sem=sem.at[(1,) + at],
            device_id=target,
            device_id_type=MESH,
        )

    def send(sem, at, source, target_ref, target):
        copy_of(sem, at, source, target_ref, target).start()

    def arrived(sem, at, ref):
        copy_of(sem, at, ref, ref, place.sibling()).wait_recv()

    def left(sem, at, ref):
        copy_of(sem, at, ref, ref, place.sibling()).wait_send()

    def seat(a, j, k, kx, core):
        return landed.at[a, toggle(z, j, nz), flip(y, k), flip(x, kx), core]

    def spread(a, j, k, source):
        for kx in range(1, nx):
            target = place.device(flip(x, kx), c, z, y)
            send(line_sem, (a, j, k, kx), source, seat(a, j, k, 0, c), target)
        send(pair_sem, (a, j, k, 0), source, seat(a, j, k, 0, c), place.sibling())

    def turn_of(s):
        far = jnp.where(s == 1, nz - 1, nz + 1 - s)
        return jnp.where(s == 0, 0, jnp.where(s == 2, 1, far))

    def dispatch_part(j, near):
        for k in range(ny):
            if near and k == 0:
                spread(0, 0, 0, rows_in.at[me])
            else:
                there = (toggle(z, j, nz), flip(y, k))
                send(
                    plane_sem,
                    (j, k),
                    rows_in.at[there[0] * ny + there[1]],
                    seat(0, 0, 0, 0, c),
                    place.device(x, c, *there),
                )

    def dispatch(value):
        rows_in[...] = value.astype(half).reshape(rows_in.shape)
        dispatch_part(nz - 1, False)
        dispatch_part(0, True)
        if nz > 2:
            dispatch_part(1, False)
        for j in range(nz - 2, 1, -1):
            dispatch_part(j, False)
        landed[0, z, y, x, c] = rows_in[me]

    def take_plane(s):
        j = turn_of(s)
        for k in range(ny):

            def take(k=k):
                arrived(plane_sem, (j, k), seat(0, j, k, 0, c))
                spread(0, j, k, seat(0, j, k, 0, c))

            if k == 0:
                pl.when(j > 0)(take)
            else:
                take()

    def take_line(a, j):
        for k in range(ny):
            for kx in range(1, nx):
                block = seat(a, j, k, kx, c)
                arrived(line_sem, (a, j, k, kx), block)
                send(pair_sem, (a, j, k, kx), block, block, place.sibling())

    def pair_gone(j, k, kx):
        return lambda: left(pair_sem, (1, j, k, kx), seat(1, j, k, kx, c))

    def line_gone(j, k, kx):
        return lambda: left(line_sem, (1, j, k, kx), seat(1, j, k, 0, c))

    def take_pair(a, s):
        j = turn_of(s)
        for k in range(ny):
            for kx in range(nx):
                arrived(pair_sem, (a, j, k, kx), seat(a, j, k, kx, 1 - c))

    def pair_left(i):
        left(sum_sem, (i % 2, turn_of(i // 2)), pair_out.at[i % 3])

    def line_left(i):
        for kx in range(1, nx):
            left(part_sem, (i % 2, turn_of(i // 2), kx), line_out.at[i % 3, kx - 1])

    def give_pair(i, held, weight):
        a, j = i % 2, turn_of(i // 2)
        product[...] = dot_nt(held[j].reshape(chunk, inner), weight[...]).reshape(product.shape)
        pl.when(i >= 3)(lambda: pair_left(i - 3))
        pair_out[i % 3] = product[:, :, 1 - c].astype(half)
        send(sum_sem, (a, j), pair_out.at[i % 3], pair_in.at[a, j], place.sibling())
        kept[i % 3] = product[:, :, c]

    def give_line(i):
        a, j = i % 2, turn_of(i // 2)
        arrived(sum_sem, (a, j), pair_in.at[a, j])
        kept[i % 3] = kept[i % 3] + pair_in[a, j].astype(f32)
        pl.when(i >= 3)(lambda: line_left(i - 3))
        for kx in range(1, nx):
            line_out[i % 3, kx - 1] = kept[i % 3, :, flip(x, kx)].astype(half)
            send(
                part_sem,
                (a, j, kx),
                line_out.at[i % 3, kx - 1],
                line_in.at[a, j, kx - 1],
                place.device(flip(x, kx), c, z, y),
            )

    def give_plane(i):
        a, j = i % 2, turn_of(i // 2)
        value = kept[i % 3, :, x]
        for kx in range(1, nx):
            arrived(part_sem, (a, j, kx), line_in.at[a, j, kx - 1])
            value = value + line_in[a, j, kx - 1].astype(f32)
        total[a, j] = value.astype(total.dtype)
        for b in range(2):
            for k in range(ny):

                def go(b=b, k=k):
                    there = (toggle(z, j, nz), flip(y, k))
                    send(
                        home_sem,
                        (b, j, k),
                        total.at[b, j, there[1]],
                        backs[b].at[me],
                        place.device(x, c, *there),
                    )

                def stay(b=b):
                    backs[b][me] = total[b, 0, y]

                if k == 0:
                    pl.when((a == b) & (j > 0))(go)
                    pl.when((a == b) & (j == 0))(stay)
                else:
                    pl.when(a == b)(go)

    def forward(i, s):
        j = turn_of(s)
        block = landed[0, toggle(z, j, nz)].reshape(chunk, width)
        logits = dot_nn(block, dense[:, 4 * width :])
        lane = lanes_of(logits.shape)
        terms = jnp.where(lane < experts, jnp.exp(logits), 0.0)
        mine = jnp.sum(jnp.where(lane == me, terms, 0.0), axis=-1, keepdims=True)
        gate_of[...] = mine / jnp.sum(terms, axis=-1, keepdims=True)
        before = dot_nn(block, up[...])
        bell = jnp.exp(-0.5 * before * before) * inv_root_two_pi
        share = 0.5 * (1.0 + lax.erf(before * inv_root_two))
        act = (before * share).astype(half)
        slope[...] = share + before * bell
        hidden[j] = act.reshape(hidden.shape[1:])
        give_pair(i, hidden, down)

    def backward(i, s):
        j = turn_of(s)
        for k in range(ny):
            for kx in range(1, nx):
                pl.when(j >= early)(pair_gone(j, k, kx))
        block = landed[1, toggle(z, j, nz)].reshape(chunk, width).astype(f32)
        block = (block * gate_of[...]).astype(half)
        landed[1, toggle(z, j, nz)] = block.reshape(landed.shape[2:])
        pre = (dot_nn(block, down[...]) * slope[...]).astype(half)
        grad_pre[j] = pre.reshape(grad_pre.shape[1:])
        give_pair(i, grad_pre, up)

    def weights(j):
        up_grad[...] += dot_tn(landed[0, toggle(z, j, nz)].reshape(chunk, width), grad_pre[j].reshape(chunk, inner))
        down_grad[...] += dot_tn(landed[1, toggle(z, j, nz)].reshape(chunk, width), hidden[j].reshape(chunk, inner))

    for j in range(nz):
        for k in range(ny):
            for kx in range(nx if j < early else 1):
                spots = (flip(z, j), flip(y, k), flip(x, kx))
                at = (spots[2], spots[0] * ny + spots[1])
                if j < early:
                    to = seat(1, j, k, kx, c)
                    send(pair_sem, (1, j, k, kx), cots_in.at[at], to, place.sibling())
                else:
                    spread(1, j, k, cots_in.at[at])
                landed[(1,) + spots + (c,)] = cots_in[at]
    rows_pad[...] = jnp.zeros_like(rows_pad)
    choice, slot = read_choices(choice_in, slot_in, turn, rows_up, taken)
    places = place_terms(choice, slot, taken, capacity, experts)
    place_any = sum(places[1:], places[0])
    rows_pad[:count] = tokens[...]
    inputs = rows_pad[...].astype(f32)
    turned = dense[:, 4 * width :].astype(f32).T
    gain_first, bias_first, gain_second, bias_second = (
        turned[experts + i : experts + i + 1] for i in range(4)
    )
    normed_first = (row_stats(inputs)[0] * gain_first + bias_first).astype(half)
    packed[...] = dot_nn(normed_first, dense[:, : 3 * width]).astype(half)

    key_live = lanes_of((1, rows_up)) < count
    lane = lanes_of((1, 128))
    sides = [((lane // 64) == i).astype(f32).astype(half) for i in range(2)]
    scale = HEAD ** (-0.5)
    for g in range(parts):
        for at in range(g * 256, g * 256 + 256, 128):
            query = packed[:, at : at + 128]
            key = packed[:, width + at : width + at + 128]
            value = packed[:, 2 * width + at : 2 * width + at + 128]
            total_mixed = 0.0
            for side in sides:
                terms = jnp.where(key_live, jnp.exp(dot_nt(query * side, key) * scale), 0.0)
                weigh = (terms * (1.0 / jnp.sum(terms, axis=-1, keepdims=True))).astype(half)
                total_mixed = total_mixed + dot_nn(weigh, value * side)
            mixed[:, at : at + 128] = total_mixed.astype(half)
    hidden_first = inputs + dot_nn(mixed[...], dense[:, 3 * width : 4 * width])
    hidden_out[...] = hidden_first
    normed_second = (row_stats(hidden_first)[0] * gain_second + bias_second).astype(half)
    dispatch(dot_tn(place_any, normed_second))
    for j in range(early, nz):
        take_line(1, j)
    take_plane(0)

    @pl.loop(0, steps)
    def _(i):
        a, s = i % 2, i // 2
        pl.when(a == 0)(lambda: take_line(0, turn_of(s)))
        take_pair(a, s)

        @pl.when(i == 0)
        def _():
            for early in range(1, min(3, nz)):
                take_plane(early)

        pl.when((a == 1) & (s >= 1) & (s + 2 < nz))(lambda: take_plane(s + 2))
        pl.when(a == 0)(lambda: forward(i, s))
        pl.when(a == 1)(lambda: backward(i, s))
        pl.when(i >= 1)(lambda: give_line(i - 1))
        pl.when(i >= 2)(lambda: give_plane(i - 2))

    up_grad[...] = jnp.zeros_like(up_grad)
    down_grad[...] = jnp.zeros_like(down_grad)

    @pl.loop(0, nz)
    def _(j):
        weights(j)

        @pl.when(j == 0)
        def _():
            give_line(steps - 1)
            give_plane(steps - 2)

        pl.when(j == 1)(lambda: give_plane(steps - 1))

    for i in range(max(steps - 3, 0), steps):
        pair_left(i)
        line_left(i)
    for a in range(2):

        @pl.loop(0, nz)
        def _(j, a=a):
            for k in range(ny):
                for kx in range(nx):
                    if kx and a == 1:
                        pl.when(j < early)(pair_gone(j, k, kx))
                    else:
                        left(pair_sem, (a, j, k, kx), seat(a, j, k, kx, c))
                    if kx and a == 0:
                        left(line_sem, (a, j, k, kx), seat(a, j, k, 0, c))
                    if kx and a == 1:
                        pl.when(j >= early)(line_gone(j, k, kx))

                def rest(k=k):
                    there = toggle(z, j, nz) * ny + flip(y, k)
                    arrived(home_sem, (a, j, k), backs[a].at[there])
                    left(home_sem, (a, j, k), total.at[a, j, flip(y, k)])
                    if a == 0:
                        left(plane_sem, (j, k), rows_in.at[there])

                if k == 0:
                    pl.when(j > 0)(rest)
                else:
                    rest()


def run_forward(tokens, cots_in, choice_in, slot_in, dense, up, down, taken):
    nx = lax.axis_size("dp") // 2
    ny = nx
    nz = lax.axis_size("expert") // ny
    experts = ny * nz
    capacity = -(-taken // 16) * 16
    count, width = tokens.shape
    rows_up = -(-count // 16) * 16
    top = choice_in.shape[0]
    inner = up.shape[1]
    chunk = ny * nx * 2 * capacity
    half, f32 = jnp.bfloat16, jnp.float32
    vmem = pl.BlockSpec(memory_space=pltpu.VMEM)
    sems = [(2, nz) + shape for shape in ((ny, nx), (ny, nx), (), (nx,), (ny,))]
    sems = [(nz, ny)] + sems
    block = (experts, capacity, width)
    return pl.pallas_call(
        functools.partial(expert_kernel, nx, nz, experts, taken),
        out_shape=(
            jax.ShapeDtypeStruct(block, half),
            jax.ShapeDtypeStruct(block, half),
            jax.ShapeDtypeStruct(up.shape, f32),
            jax.ShapeDtypeStruct(down.shape, f32),
            jax.ShapeDtypeStruct((rows_up, 3 * width), half),
            jax.ShapeDtypeStruct((rows_up, width), half),
            jax.ShapeDtypeStruct((rows_up, width), f32),
        ),
        in_specs=[vmem] * 7,
        out_specs=(vmem,) * 7,
        scratch_shapes=[
            pltpu.VMEM((rows_up, width), half),
            pltpu.VMEM((max(8, 2 * top), -(-rows_up // 128) * 128), f32),
            pltpu.VMEM(block, half),
            pltpu.VMEM((chunk, 1), f32),
            pltpu.VMEM((2, nz, ny, nx, 2, capacity, width), half),
            pltpu.VMEM((chunk, inner), f32),
            pltpu.VMEM((nz, ny, nx, 2, capacity, inner), half),
            pltpu.VMEM((nz, ny, nx, 2, capacity, inner), half),
            pltpu.VMEM((ny, nx, 2, capacity, width), f32),
            pltpu.VMEM((3, ny, nx, capacity, width), f32),
            pltpu.VMEM((3, ny, nx, capacity, width), half),
            pltpu.VMEM((2, nz, ny, nx, capacity, width), half),
            pltpu.VMEM((3, nx - 1, ny, capacity, width), half),
            pltpu.VMEM((2, nz, nx - 1, ny, capacity, width), half),
            pltpu.VMEM((2, nz, ny, capacity, width), half),
        ]
        + [pltpu.SemaphoreType.DMA((2,) + shape) for shape in sems],
        compiler_params=pltpu.CompilerParams(
            collective_id=2, has_side_effects=True, vmem_limit_bytes=VMEM_LIMIT
        ),
        name="forward",
    )(tokens, cots_in, choice_in, slot_in, dense, up, down)


def backward_kernel(
    nx,
    nz,
    experts,
    capacity,
    padded,
    tokens,
    cotangent,
    choice_in,
    slot_in,
    packed,
    mixed,
    hidden_in,
    returned_in,
    grad_back,
    dense,
    block_out,
    input_out,
    main_out,
    side_out,
    extra_out,
    tokens_pad,
    cots_pad,
    turn,
    grads,
    tails,
    *boxes,
):
    place = Place()
    plane = nx * nx * nz
    count, width = tokens.shape
    rows_up = tokens_pad.shape[0]
    parts = width // 256
    half, f32 = jnp.bfloat16, jnp.float32
    pair, second, first, last, pair_t, second_t, first_t, last_t, sems = boxes
    owners = 2 * plane

    def refs(g):
        if g == parts + 1:
            return tails, pair_t, second_t, first_t, last_t
        return grads.at[g], pair.at[g], second.at[g], first.at[g], last.at[g]

    def copy_of(g, seat, source, target_ref, target):
        return pltpu.make_async_remote_copy(
            src_ref=source,
            dst_ref=target_ref,
            send_sem=sems.at[0, g, seat],
            recv_sem=sems.at[1, g, seat],
            device_id=target,
            device_id_type=MESH,
        )

    def arrived(g, seat, ref):
        copy_of(g, seat, ref, ref, place.sibling()).wait_recv()

    pairs = sorted(
        ((kf, ks) for kf in range(nx) for ks in range(nx)), key=lambda k: (k[1] == 0, k[0] == 0, k)
    )

    def at_of(kz, kf, ks):
        return ks * nx * nz + kf * nz + kz

    def scatter_pair(g):
        own, theirs = refs(g)[:2]
        for kf, ks in pairs:

            @pl.loop(0, nz)
            def _(i, kf=kf, ks=ks):
                kz = (i + 1) % nz
                index = place.owner(*spot(place, 1 - place.c, kz, kf, ks))
                at = at_of(kz, kf, ks)
                copy_of(g, at, own.at[index], theirs.at[at], place.sibling()).start()

    def gathered(g, kz, kf, ks):
        own, theirs, from_second, from_first, from_last = refs(g)
        at = at_of(kz, kf, ks)
        arrived(g, at, theirs.at[at])
        total = own[place.owner(*spot(place, place.c, kz, kf, ks))].astype(f32)
        total = total + theirs[at].astype(f32)
        if ks == 0:
            for k in range(1, nx):
                seat = at_of(kz, kf, k)
                arrived(g, plane + seat, from_second.at[seat - nx * nz])
                total = total + from_second[seat - nx * nz].astype(f32)
        if ks == 0 and kf == 0:
            for k in range(1, nx):
                seat = at_of(kz, k, 0)
                arrived(g, plane + seat, from_first.at[seat - nz])
                total = total + from_first[seat - nz].astype(f32)
        return total

    def pass_on(g, kz, kf, ks):
        own, theirs, from_second, from_first, from_last = refs(g)
        at = at_of(kz, kf, ks)
        theirs[at] = gathered(g, kz, kf, ks).astype(half)
        if ks:
            target_ref = from_second.at[at - nx * nz]
            target = spot(place, place.c, 0, 0, ks)
        elif kf:
            target_ref = from_first.at[at - nz]
            target = spot(place, place.c, 0, kf, 0)
        else:
            target_ref = from_last.at[kz - 1]
            target = spot(place, place.c, kz, 0, 0)
        copy_of(g, plane + at, theirs.at[at], target_ref, place.device(*target)).start()

    def scatter_stage(g, stage):
        if stage < 2:
            for kf, ks in pairs:
                if (ks > 0, ks == 0 and kf > 0)[stage]:

                    @pl.loop(0, nz)
                    def _(i, kf=kf, ks=ks):
                        pass_on(g, (i + 1) % nz, kf, ks)

        elif stage == 2:

            @pl.loop(1, nz)
            def _(kz):
                pass_on(g, kz, 0, 0)

        else:
            total = gathered(g, 0, 0, 0)
            from_last = refs(g)[4]
            for k in range(1, nz):
                arrived(g, plane + k, from_last.at[k - 1])
                total = total + from_last[k - 1].astype(f32)
            total = total[: side_out.shape[0]]
            if g == 0:
                side_out[...] = total
            elif g == parts + 1:
                extra_out[...] = total
            else:
                for i in range(3):
                    start = i * width + (g - 1) * 256
                    main_out[:, start : start + 256] = total[:, i * 256 : (i + 1) * 256]

    def scatter_end(g):
        own, theirs = refs(g)[:2]

        @pl.loop(0, plane)
        def _(at):
            copy_of(g, at, theirs.at[at], theirs.at[at], place.sibling()).wait_send()

            @pl.when(at > 0)
            def _():
                copy_of(g, plane + at, theirs.at[at], theirs.at[at], place.sibling()).wait_send()

    def fill(g, value, start):
        owned = owned_rows(value)
        if g == parts + 1:
            tails[...] = owned.astype(half)
        else:
            grads[g, :, :, start : start + value.shape[1]] = owned.astype(half)

    def owned_rows(value):
        rows = grads.shape[2]
        if rows * owners != width:
            shape = (rows * owners, width)
            at = lax.broadcasted_iota(jnp.int32, shape, 0)
            real = width // owners
            meant = jnp.where(at % rows < real, at // rows * real + at % rows, width)
            pick = (meant == lanes_of(shape)).astype(f32).astype(half)
            value = dot_nn(pick, value.astype(half))
        return value.reshape(owners, rows, value.shape[1])

    greet(grid_partners(place))

    for ref, source in ((tokens_pad, tokens), (cots_pad, cotangent)):
        ref[...] = jnp.zeros_like(ref)
        ref[:count] = source[...]
    choice, slot = read_choices(choice_in, slot_in, turn, rows_up, capacity)
    extra = dense[:, 4 * width :]
    turned = extra.astype(f32).T
    gain_first, bias_first, gain_second, bias_second = (
        turned[experts + i : experts + i + 1] for i in range(4)
    )
    grad_top = cots_pad[...].astype(f32)
    hidden_first = hidden_in[...]
    unit_second, inverse_second = row_stats(hidden_first)
    normed_second = (unit_second * gain_second + bias_second).astype(half)
    probs, masks, gates = router_terms(normed_second, extra, choice, experts)
    places = place_terms(choice, slot, capacity, padded, experts)
    returned = [dot_nn(one, returned_in[...]) for one in places]
    combined = sum(gate * rows for gate, rows in zip(gates, returned))
    block_out[...] = (hidden_first + combined)[:count].astype(half)
    gate_grads = [jnp.sum(grad_top * rows, axis=-1, keepdims=True) for rows in returned]
    grad_normed = dot_nn(sum(places[1:], places[0]), grad_back[...])
    grad_probs = sum(mask * grad for mask, grad in zip(masks, gate_grads))
    grad_logits = probs * (grad_probs - jnp.sum(probs * grad_probs, axis=-1, keepdims=True))
    grad_logits = grad_logits.astype(half)
    router_grad = dot_tn(normed_second, grad_logits)
    grad_normed = grad_normed + dot_nt(grad_logits, extra)
    second_sums = [
        jnp.sum(grad_normed * unit_second, axis=0, keepdims=True),
        jnp.sum(grad_normed, axis=0, keepdims=True),
    ]
    grad_hidden = grad_top + row_stats_back(grad_normed, unit_second, inverse_second, gain_second)
    grad_half = grad_hidden.astype(half)
    fill(0, dot_tn(mixed[...], grad_half), 0)
    scatter_pair(0)
    grad_mixed = dot_nt(grad_half, dense[:, 3 * width : 4 * width]).astype(half)
    unit_first, inverse_first = row_stats(tokens_pad[...].astype(f32))
    normed_first = (unit_first * gain_first + bias_first).astype(half)
    key_live = lax.broadcasted_iota(jnp.int32, (rows_up, rows_up), 0) < count
    lane = lanes_of((1, 128))
    sides = [((lane // 64) == i).astype(f32).astype(half) for i in range(2)]
    scale = HEAD ** (-0.5)
    grad_rows = jnp.zeros((rows_up, width), f32)
    for g in range(1, parts + 1):
        pieces = [[], [], []]
        for at in range((g - 1) * 256, g * 256, 128):
            query = packed[:, at : at + 128]
            key = packed[:, width + at : width + at + 128]
            value = packed[:, 2 * width + at : 2 * width + at + 128]
            grad = grad_mixed[:, at : at + 128]
            sums = [0.0, 0.0, 0.0]
            for side in sides:
                query_one, key_one, grad_one = query * side, key * side, grad * side
                terms = jnp.where(key_live, jnp.exp(dot_nt(key, query_one) * scale), 0.0)
                weights = terms * (1.0 / jnp.sum(terms, axis=0, keepdims=True))
                grad_weights = dot_nt(value, grad_one)
                delta = jnp.sum(weights * grad_weights, axis=0, keepdims=True)
                grad_scores = (weights * (grad_weights - delta) * scale).astype(half)
                sums[0] = sums[0] + dot_tn(grad_scores, key_one)
                sums[1] = sums[1] + dot_nn(grad_scores, query_one)
                sums[2] = sums[2] + dot_nn(weights.astype(half), grad_one)
            for piece, total in zip(pieces, sums):
                piece.append(total.astype(half))
        for i in range(3):
            joined = jnp.concatenate(pieces[i], axis=1)
            start = i * width + (g - 1) * 256
            grad_rows = grad_rows + dot_nt(joined, dense[:, start : start + 256])
            fill(g, dot_tn(normed_first, joined), i * 256)
        scatter_pair(g)
        for back in range(3):
            if g - 1 - back >= 0:
                scatter_stage(g - 1 - back, back)
    first_sums = [
        jnp.sum(grad_rows * unit_first, axis=0, keepdims=True),
        jnp.sum(grad_rows, axis=0, keepdims=True),
    ]
    lines = first_sums + second_sums
    line_at = lax.broadcasted_iota(jnp.int32, turned.shape, 0)
    columns = sum(jnp.where(line_at == experts + i, lines[i], 0.0) for i in range(4))
    fill(parts + 1, router_grad + columns.T, 0)
    scatter_pair(parts + 1)
    scatter_stage(parts, 0)
    grad_inputs = row_stats_back(grad_rows, unit_first, inverse_first, gain_first)
    input_out[...] = (grad_inputs + grad_hidden)[:count].astype(half)
    for g in range(parts + 1, parts + 6):
        for back in range(4):
            if g - 1 - back <= parts + 1 and (g, back) != (parts + 1, 0):
                scatter_stage(g - 1 - back, back)
    for g in range(parts + 2):
        scatter_end(g)


def run_backward(sizes, arrays, rows_owned):
    nx = lax.axis_size("dp") // 2
    nz = lax.axis_size("expert") // nx
    plane = nx * nx * nz
    tile_rows = -(-rows_owned // 8) * 8
    tokens, packed, dense = arrays[0], arrays[4], arrays[-1]
    count, width = tokens.shape
    rows_up = packed.shape[0]
    top = arrays[2].shape[0]
    parts = width // 256
    rest = dense.shape[1] - 4 * width
    half, f32 = jnp.bfloat16, jnp.float32
    vmem = pl.BlockSpec(memory_space=pltpu.VMEM)

    def boxes(lead, columns):
        return [
            pltpu.VMEM(lead + (size, tile_rows, columns), half)
            for size in (plane, plane - nx * nz, (nx - 1) * nz, nz - 1)
        ]

    return pl.pallas_call(
        functools.partial(backward_kernel, nx, nz, *sizes),
        out_shape=(
            jax.ShapeDtypeStruct((count, width), half),
            jax.ShapeDtypeStruct((count, width), half),
            jax.ShapeDtypeStruct((rows_owned, 3 * width), f32),
            jax.ShapeDtypeStruct((rows_owned, width), f32),
            jax.ShapeDtypeStruct((rows_owned, rest), f32),
        ),
        in_specs=[vmem] * len(arrays),
        out_specs=(vmem,) * 5,
        scratch_shapes=[
            pltpu.VMEM((rows_up, width), half),
            pltpu.VMEM((rows_up, width), half),
            pltpu.VMEM((max(8, 2 * top), -(-rows_up // 128) * 128), f32),
            pltpu.VMEM((parts + 1, 2 * plane, tile_rows, width), half),
            pltpu.VMEM((2 * plane, tile_rows, rest), half),
        ]
        + boxes((parts + 1,), width)
        + boxes((), rest)
        + [pltpu.SemaphoreType.DMA((2, parts + 2, 2 * plane))],
        compiler_params=pltpu.CompilerParams(
            collective_id=1, has_side_effects=True, vmem_limit_bytes=VMEM_LIMIT
        ),
        name="backward",
    )(*arrays)


def finish_kernel(experts, count, extra, *refs):
    sources, outs, small = refs[:count], refs[count : 2 * count], refs[2 * count : 2 * count + 5]
    held, turn, sems = refs[2 * count + 5 : -2], refs[-2], refs[-1]
    reads = [pltpu.make_async_copy(sources[i], held[i], sems.at[0, i]) for i in range(count)]
    writes = [pltpu.make_async_copy(held[i], outs[i], sems.at[1, i]) for i in range(count)]
    for copy in reads:
        copy.start()
    rows = extra.shape[0]
    turn[...] = jnp.zeros_like(turn)
    turn[:rows] = extra[...]
    turned = turn[...].T
    small[0][...] = turned[:experts, :rows]
    for i in range(4):
        small[1 + i][...] = turned[experts + i : experts + i + 1, :rows]
    for read, write in zip(reads, writes):
        read.wait()
        write.start()
    for copy in writes:
        copy.wait()


def finish(experts, extra, arrays):
    rows = extra.shape[0]
    f32 = jnp.float32
    somewhere, vmem = pl.BlockSpec(memory_space=pl.ANY), pl.BlockSpec(memory_space=pltpu.VMEM)
    return pl.pallas_call(
        functools.partial(finish_kernel, experts, len(arrays)),
        out_shape=[jax.ShapeDtypeStruct(array.shape, array.dtype) for array in arrays]
        + [jax.ShapeDtypeStruct((experts, rows), f32)]
        + [jax.ShapeDtypeStruct((1, rows), f32)] * 4,
        in_specs=[vmem] + [somewhere] * len(arrays),
        out_specs=[somewhere] * len(arrays) + [vmem] * 5,
        scratch_shapes=[pltpu.VMEM(array.shape, array.dtype) for array in arrays]
        + [pltpu.VMEM((-(-rows // 128) * 128, extra.shape[1]), f32)]
        + [pltpu.SemaphoreType.DMA((2, len(arrays)))],
        compiler_params=pltpu.CompilerParams(vmem_limit_bytes=VMEM_LIMIT),
        name="finish",
    )(extra, *arrays)


def per_device(
    tokens,
    packed_weight,
    output_weight,
    router_weight,
    first_gain,
    first_bias,
    second_gain,
    second_bias,
    expert_up,
    expert_down,
    expert_choice,
    slot_index,
    cotangent,
):
    local_tokens = tokens.shape[0]
    model_width = tokens.shape[1]
    top_count = expert_choice.shape[1]
    experts = lax.axis_size("expert")
    capacity = max(15 * local_tokens * top_count // (16 * experts), 2)
    rows_owned = packed_weight.shape[0]
    padded = -(-capacity // 16) * 16
    choice, slot = expert_choice.T, slot_index.T
    dense, cots = gather_dense(
        packed_weight,
        output_weight,
        router_weight.T,
        (first_gain, first_bias, second_gain, second_bias),
        cotangent,
        choice,
        slot,
        capacity,
    )
    dense = dense.reshape(model_width, dense.shape[2])
    back_rows, back_grad, up_grad, down_grad, packed, mixed, hidden_first = run_forward(
        tokens, cots, choice, slot, dense, expert_up[0], expert_down[0], capacity
    )
    slots = experts * padded
    block_output, input_grad, main_grad, side_grad, extra_grad = run_backward(
        (experts, capacity, padded),
        (
            tokens,
            cotangent,
            choice,
            slot,
            packed,
            mixed,
            hidden_first,
            back_rows.reshape(slots, model_width),
            back_grad.reshape(slots, model_width),
            dense,
        ),
        rows_owned,
    )
    done = finish(
        experts, extra_grad, (block_output, input_grad, main_grad, side_grad, up_grad, down_grad)
    )
    return (
        *done[:4],
        done[6].T,
        *(vector.reshape(rows_owned) for vector in done[7:]),
        done[4][None],
        done[5][None],
    )


def solution(mesh):
    return jax.shard_map(
        per_device,
        mesh=mesh,
        in_specs=(
            P(("dp", "expert"), None),
            P(("dp", "expert"), None),
            P(("dp", "expert"), None),
            P(("dp", "expert"), None),
            P(("dp", "expert")),
            P(("dp", "expert")),
            P(("dp", "expert")),
            P(("dp", "expert")),
            P("expert", None, "dp"),
            P("expert", None, "dp"),
            P(("dp", "expert"), None),
            P(("dp", "expert"), None),
            P(("dp", "expert"), None),
        ),
        out_specs=(
            P(("dp", "expert"), None),
            P(("dp", "expert"), None),
            P(("dp", "expert"), None),
            P(("dp", "expert"), None),
            P(("dp", "expert"), None),
            P(("dp", "expert")),
            P(("dp", "expert")),
            P(("dp", "expert")),
            P(("dp", "expert")),
            P("expert", None, "dp"),
            P("expert", None, "dp"),
        ),
        check_vma=False,
    )
```
